32 devices in a mesh: dp: 4 (over y, x), seq: 8 (over z, core).
Axes of the slice: x: 2, y: 2, z: 4, core: 2. Of those that a mesh axis runs over, the one named last changes fastest.
Arguments:
- tokens: bfloat16 [4, 1280, 2048], P('dp', 'seq'), may hold values from -6 to 6
- w_query: bfloat16 [2048, 2048], P(('dp', 'seq')), may hold values from -0.125 to 0.125
- w_key: bfloat16 [2048, 2048], P(('dp', 'seq')), may hold values from -0.125 to 0.125
- w_value: bfloat16 [2048, 2048], P(('dp', 'seq')), may hold values from -0.125 to 0.125
- w_out: bfloat16 [2048, 2048], P(None, ('dp', 'seq')), may hold values from -0.125 to 0.125
- w_gate: bfloat16 [2048, 8192], P(('dp', 'seq')), may hold values from -0.125 to 0.125
- w_up: bfloat16 [2048, 8192], P(('dp', 'seq')), may hold values from -0.125 to 0.125
- w_down: bfloat16 [8192, 2048], P(None, ('dp', 'seq')), may hold values from -0.0625 to 0.0625
- gain_query: bfloat16 [2048], P(('dp', 'seq')), may hold values from 0.5 to 1.5
- gain_key: bfloat16 [2048], P(('dp', 'seq')), may hold values from 0.5 to 1.5
- gain_attn: bfloat16 [2048], P(('dp', 'seq')), may hold values from 0.5 to 1.5
- gain_mlp: bfloat16 [2048], P(('dp', 'seq')), may hold values from 0.5 to 1.5
- cotangent: bfloat16 [4, 1280, 2048], P('dp', 'seq'), may hold values from -6 to 6
- key_mask: int32 [4, 1280], P('dp', 'seq'), may hold values 0 or 1
- lengths: int32 [4], P('dp'), may hold values from 640 to 1280, as said below
- tract_order: int32 [4, 16], P('dp', 'seq'), may hold values from 0 to 15, as said below
Outputs:
- layer_out: bfloat16 [4, 1280, 2048], P('dp', 'seq')
- grad_tokens: bfloat16 [4, 1280, 2048], P('dp', 'seq')
- grad_w_query: float32 [2048, 2048], P(('dp', 'seq'))
- grad_w_key: float32 [2048, 2048], P(('dp', 'seq'))
- grad_w_value: float32 [2048, 2048], P(('dp', 'seq'))
- grad_w_out: float32 [2048, 2048], P(None, ('dp', 'seq'))
- grad_w_gate: float32 [2048, 8192], P(('dp', 'seq'))
- grad_w_up: float32 [2048, 8192], P(('dp', 'seq'))
- grad_w_down: float32 [8192, 2048], P(None, ('dp', 'seq'))
- grad_gain_query: float32 [2048], P(('dp', 'seq'))
- grad_gain_key: float32 [2048], P(('dp', 'seq'))
- grad_gain_attn: float32 [2048], P(('dp', 'seq'))
- grad_gain_mlp: float32 [2048], P(('dp', 'seq'))
The draws below stay inside these ranges and needn't reach their ends.
Inputs may be any that keep to these rules, and one draw needn't show every extreme that they name: `lengths`: some row has all 1280 tokens valid. `tract_order`: each row is a permutation of 0 to 15: entry j is the place, in units of 80 tokens, of the row's j-th stored block.
All inputs are finite; a program needn't handle non-finite values. No bound on the sum of `key_mask` on one device may be relied on, other than what follows from the above.
Results may differ from the reference program's by a relative error of at most 0.02.
Values may be sent and summed in bfloat16 or wider, within the bound.
A program may use at most 768 MiB of HBM per device.

```python
import jax
import jax.numpy as jnp
from jax import lax

D = 2048
FF = 8192
HEADS = 16
HEAD_DIM = 128
ROW_LEN = 1280
BATCH = 4
STRETCH = 80
STRETCHES = 16


def draw_lengths(key, part):
    spread = jax.random.randint(key, (BATCH,), ROW_LEN // 2, ROW_LEN + 1)
    place = jax.random.randint(jax.random.fold_in(key, 7), (), 0, BATCH)
    return spread.at[place].set(ROW_LEN).astype(jnp.int32)


def one_order(row_key):
    return jax.random.permutation(row_key, STRETCHES)


def draw_tract_order(key, part):
    row_keys = jax.random.split(jax.random.fold_in(key, 11), BATCH)
    return jax.vmap(one_order)(row_keys).astype(jnp.int32)


def place_ends(array, key, least, largest):
    longest = array.shape.index(max(array.shape))
    spots = []
    for shift in (0, 1):
        where = [jax.random.randint(jax.random.fold_in(key, axis), (), 0, length) for axis, length in enumerate(array.shape)]
        where[longest] = (where[longest] + shift) % array.shape[longest]
        spots.append(tuple(where))
    return array.at[spots[0]].set(least).at[spots[1]].set(largest)


def block_levels(key, extent, cuts, least, top_value):
    def one(position, shards_of):
        draws = jax.random.uniform(jax.random.fold_in(jax.random.fold_in(key, 6), position), (shards_of,), jnp.float32, least / len(cuts), top_value / len(cuts))
        return jnp.repeat(jnp.exp(draws), extent[position] // shards_of).reshape((-1,) + (1,) * (len(extent) - position - 1))

    loudness = one(*cuts[0])
    for cut in cuts[1:]:
        loudness = loudness * one(*cut)
    return loudness


def gaussian(own_key, dims, scale, most, shards=(), kind=jnp.bfloat16):
    level = block_levels(own_key, dims, shards, -0.22, 0.18) if shards else 1.0
    drawn = jax.random.normal(own_key, dims, jnp.float32) * scale * level
    return jnp.minimum(jnp.maximum(drawn, -most), most).astype(kind)


def setup_inputs(seed: int = 0) -> dict:
    key_list = jax.random.split(jax.random.key(seed), 17)
    return {
        "tokens": gaussian(key_list[0], (BATCH, ROW_LEN, D), 1.0, 6.0, ((0, 4), (1, 8))),
        "w_query": gaussian(key_list[1], (D, D), D ** -0.5, 0.125, ((0, 32),)),
        "w_key": gaussian(key_list[2], (D, D), D ** -0.5, 0.125, ((0, 32),)),
        "w_value": gaussian(key_list[3], (D, D), D ** -0.5, 0.125, ((0, 32),)),
        "w_out": gaussian(key_list[4], (D, D), D ** -0.5, 0.125, ((1, 32),)),
        "w_gate": gaussian(key_list[5], (D, FF), D ** -0.5, 0.125, ((0, 32),)),
        "w_up": gaussian(key_list[6], (D, FF), D ** -0.5, 0.125, ((0, 32),)),
        "w_down": gaussian(key_list[7], (FF, D), FF ** -0.5, 0.0625, ((1, 32),)),
        "gain_query": jnp.clip(1.0 + 0.1 * jax.random.normal(key_list[8], (D,), jnp.float32), 0.5, 1.5).astype(jnp.bfloat16),
        "gain_key": jnp.clip(1.0 + 0.1 * jax.random.normal(key_list[9], (D,), jnp.float32), 0.5, 1.5).astype(jnp.bfloat16),
        "gain_attn": jnp.clip(1.0 + 0.1 * jax.random.normal(key_list[10], (D,), jnp.float32), 0.5, 1.5).astype(jnp.bfloat16),
        "gain_mlp": jnp.clip(1.0 + 0.1 * jax.random.normal(key_list[11], (D,), jnp.float32), 0.5, 1.5).astype(jnp.bfloat16),
        "cotangent": gaussian(key_list[12], (BATCH, ROW_LEN, D), 1.0, 6.0, ((0, 4), (1, 8))),
        "key_mask": place_ends((jax.random.randint(key_list[13], (BATCH, ROW_LEN), 0, 4) < 3).astype(jnp.int32), jax.random.fold_in(key_list[13], 1), 0, 1),
        "lengths": draw_lengths(jax.random.fold_in(key_list[16], 71), 0),
        "tract_order": draw_tract_order(jax.random.fold_in(key_list[16], 71), 0),
    }


rope_base = 500000.0
norm_eps = 1e-06
highest = lax.Precision.HIGHEST

@jax.custom_vjp
def low(v):
    return lax.optimization_barrier(v.astype(jnp.bfloat16)).astype(jnp.float32)

@jax.custom_vjp
def low_back(v):
    return v

def low_keep(v):
    return (low(v), None)

def low_pass(kept, grad):
    return (grad,)

def back_keep(v):
    return (v, None)

def back_low(kept, grad):
    return (low(grad),)
low.defvjp(low_keep, low_pass)
low_back.defvjp(back_keep, back_low)

def matmul(left, right):
    return jnp.dot(left, right, precision=highest)

def rms_factor(values):
    return lax.rsqrt(lax.optimization_barrier(jnp.mean(values * values, axis=-1, keepdims=True)) + norm_eps)

def rope_tables(positions):
    half_dim = HEAD_DIM // 2
    steps_f = jnp.arange(half_dim).astype(jnp.float32) * (2.0 / HEAD_DIM)
    inv_freq = jnp.power(rope_base, -steps_f)
    angle = positions.astype(jnp.float32)[:, None] * inv_freq[None, :]
    angle = jnp.concatenate([angle, angle], axis=-1)[:, None, :]
    return (jnp.cos(angle), jnp.sin(angle))

def rotate(values, cosine, sine):
    half_dim = values.shape[-1] // 2
    turned = jnp.concatenate([-values[..., half_dim:], values[..., :half_dim]], axis=-1)
    return values * cosine + turned * sine

def attend_block(block, key_low, value_low, key_pos, key_usable):
    query_low, query_pos = block
    scores = jnp.einsum('qhd,khd->hqk', query_low, key_low, precision=highest) * HEAD_DIM ** (-0.5)
    scores = low_back(scores)
    causal = key_pos[None, :] <= query_pos[:, None]
    allowed = causal & (key_usable[None, :] | (key_pos[None, :] == query_pos[:, None]))
    expo = jnp.where(allowed[None], jnp.exp(scores), 0.0)
    weight_sum = lax.optimization_barrier(jnp.sum(expo, axis=-1))
    summed = low_back(jnp.einsum('hqk,khd->qhd', low(expo), value_low, precision=highest))
    return summed / jnp.transpose(weight_sum)[:, :, None]

def layer(x_row, w_query, w_key, w_value, w_out, w_gate, w_up, w_down, gain_query, gain_key, gain_attn, gain_mlp, positions, key_usable):
    row_len = x_row.shape[0]
    q_raw = low_back(matmul(x_row, w_query))
    k_raw = low_back(matmul(x_row, w_key))
    v_raw = low_back(matmul(x_row, w_value))
    q_norm = q_raw * rms_factor(q_raw) * gain_query
    k_norm = k_raw * rms_factor(k_raw) * gain_key
    cosine, sine = rope_tables(positions)
    head_shape = (row_len, HEADS, HEAD_DIM)
    query_low = low(rotate(q_norm.reshape(head_shape), cosine, sine))
    key_low = low(rotate(k_norm.reshape(head_shape), cosine, sine))
    value_low = low(v_raw).reshape(head_shape)
    block_rows = 512 if row_len % 512 == 0 else row_len
    blocks = row_len // block_rows

    def attend(block):
        return attend_block(block, key_low, value_low, positions, key_usable)
    attn = lax.map(jax.checkpoint(attend), (query_low.reshape((blocks, block_rows, HEADS, HEAD_DIM)), positions.reshape((blocks, block_rows))))
    attn_low = low(attn.reshape((row_len, D)))
    branch = low_back(matmul(attn_low, w_out))
    hidden_in = x_row + branch * rms_factor(branch) * gain_attn
    hidden_low = low(hidden_in)
    gate_val = low_back(matmul(hidden_low, w_gate))
    up_val = low_back(matmul(hidden_low, w_up))
    mixed_low = low(jax.nn.silu(gate_val) * up_val)
    mlp_val = low_back(matmul(mixed_low, w_down))
    return hidden_in + mlp_val * rms_factor(mlp_val) * gain_mlp

def reference(tokens, w_query, w_key, w_value, w_out, w_gate, w_up, w_down, gain_query, gain_key, gain_attn, gain_mlp, cotangent, key_mask, lengths, tract_order):
    params = tuple((p.astype(jnp.float32) for p in (w_query, w_key, w_value, w_out, w_gate, w_up, w_down, gain_query, gain_key, gain_attn, gain_mlp)))
    slot_index = jnp.arange(ROW_LEN, dtype=jnp.int32)

    def one_row(grad_sums, row_data):
        x_row, cot_row, mask_row, row_length, order_row = row_data
        positions = (order_row[slot_index // STRETCH] * STRETCH + slot_index % STRETCH).astype(jnp.int32)
        key_usable = (mask_row == 1) & (positions < row_length)

        def forward(x_in, *weights):
            return layer(x_in, *weights, positions, key_usable)
        layer_out, pull_back = jax.vjp(forward, x_row.astype(jnp.float32), *params)
        grads = pull_back(cot_row.astype(jnp.float32))
        grad_sums = tuple((total_grad + new_grad for total_grad, new_grad in zip(grad_sums, grads[1:])))
        return (grad_sums, (layer_out.astype(jnp.bfloat16), grads[0].astype(jnp.bfloat16)))
    zero_grads = tuple((jnp.zeros(p.shape, jnp.float32) for p in params))
    grad_sums, (outputs, grad_inputs) = lax.scan(one_row, zero_grads, (tokens, cotangent, key_mask, lengths, tract_order))
    return (outputs, grad_inputs, grad_sums[0], grad_sums[1], grad_sums[2], grad_sums[3], grad_sums[4], grad_sums[5], grad_sums[6], grad_sums[7], grad_sums[8], grad_sums[9], grad_sums[10])
```

```python
import jax
import jax.numpy as jnp
from jax import lax
from jax.sharding import PartitionSpec as P

HEAD_DIM = 128

rope_base = 500000.0
norm_eps = 1e-06
f32 = jnp.float32
bf16 = jnp.bfloat16


def rms_factor(values):
    return lax.rsqrt(jnp.mean(values * values, axis=-1, keepdims=True) + norm_eps)


def norm_back(grad_normed, raw_values, factor):
    unit_values = raw_values * factor
    return factor * (
        grad_normed - unit_values * jnp.mean(grad_normed * unit_values, axis=-1, keepdims=True)
    )


def rope_tables(positions, head_dim):
    half_dim = head_dim // 2
    steps_f = jnp.arange(half_dim).astype(f32) * (2.0 / head_dim)
    inv_freq = jnp.power(rope_base, -steps_f)
    angle = positions.astype(f32)[:, None] * inv_freq[None, :]
    angle = jnp.concatenate([angle, angle], axis=-1)[:, None, :]
    return (jnp.cos(angle), jnp.sin(angle))


def rotate(values, cosine, sine):
    half_dim = values.shape[-1] // 2
    turned = jnp.concatenate([-values[..., half_dim:], values[..., :half_dim]], axis=-1)
    return values * cosine + turned * sine


def unrotate(grads, cosine, sine):
    half_dim = grads.shape[-1] // 2
    moved = grads * sine
    back_part = jnp.concatenate([moved[..., half_dim:], -moved[..., :half_dim]], axis=-1)
    return grads * cosine + back_part


def allowed_mask(query_pos, key_code):
    key_pos = key_code // 2
    usable = key_code % 2 == 1
    causal = key_pos[None, :] <= query_pos[:, None]
    return causal & (usable[None, :] | (key_pos[None, :] == query_pos[:, None]))


def dot_nn(left, right):
    return jnp.dot(left, right, preferred_element_type=f32)


def dot_nt(left, right):
    return lax.dot_general(left, right, (((1,), (1,)), ((), ())), preferred_element_type=f32)


def dot_tn(left, right):
    return lax.dot_general(left, right, (((0,), (0,)), ((), ())), preferred_element_type=f32)


def spread_columns(parts, ways):
    rows = parts[0].shape[0]
    split = [p.reshape(rows, ways, p.shape[1] // ways) for p in parts]
    joined = jnp.concatenate(split, axis=2)
    return joined.reshape(rows, ways * joined.shape[2])


def collect(matrix):
    moved = lax.all_to_all(matrix, "seq", split_axis=1, concat_axis=0, tiled=True)
    return lax.all_gather(moved, "dp", axis=0, tiled=True)


def gather_rows(rows):
    return lax.all_gather(rows, "seq", axis=0, tiled=True)


def scatter_rows(partial_rows):
    return lax.psum_scatter(
        partial_rows.astype(bf16), "seq", scatter_dimension=0, tiled=True
    ).astype(f32)


def return_grads(grad, widths, ways):
    summed = lax.psum_scatter(grad.astype(bf16), "dp", scatter_dimension=0, tiled=True)
    rows = summed.shape[0] // ways
    moved = lax.all_to_all(summed, "seq", split_axis=0, concat_axis=1, tiled=True)
    moved = moved.reshape(rows, ways, sum(widths))
    outs, begin = [], 0
    for width in widths:
        outs.append(moved[:, :, begin : begin + width].reshape(rows, ways * width).astype(f32))
        begin += width
    return outs


def body(
    tokens,
    w_query,
    w_key,
    w_value,
    w_out,
    w_gate,
    w_up,
    w_down,
    gain_query,
    gain_key,
    gain_attn,
    gain_mlp,
    cotangent,
    key_mask,
    lengths,
    tract_order,
):
    ways = lax.axis_size("seq")
    me = lax.axis_index("seq")
    token_rows = tokens[0]
    tok_count, feat_width = token_rows.shape
    ff_width = w_gate.shape[1]
    own_feat = feat_width // ways
    own_heads = own_feat // HEAD_DIM
    own_ff = ff_width // ways
    row_len = tok_count * ways
    score_scale = HEAD_DIM ** (-0.5)
    half_len = tok_count // 2
    order_pair = tract_order[0]
    slot_index = jnp.arange(tok_count, dtype=jnp.int32)
    local_pos = (
        jnp.where(slot_index < half_len, order_pair[0], order_pair[1]) * half_len
        + slot_index % half_len
    )
    key_ok = ((key_mask[0] == 1) & (local_pos < lengths[0])).astype(jnp.int32)
    grad_out = cotangent[0].astype(f32)

    gain_local = jnp.stack([gain_query, gain_key, gain_attn, gain_mlp], axis=1)
    gain_pad = jnp.pad(gain_local, ((0, 0), (0, HEAD_DIM - 4)))
    gain_all = jnp.tile(gain_pad, (1, ways))
    m_qkv = collect(spread_columns([w_query, w_key, w_value], ways))
    m_out = collect(spread_columns([jnp.transpose(w_out), gain_all], ways))
    m_gu = collect(spread_columns([w_gate, w_up], ways))
    m_down = collect(spread_columns([jnp.transpose(w_down)], ways))
    gains = jnp.transpose(m_out[:, own_feat:])[:8].astype(f32)
    m_out = m_out[:, :own_feat]
    gain_q = lax.dynamic_slice_in_dim(gains[0], me * own_feat, own_feat, 0)
    gain_k = lax.dynamic_slice_in_dim(gains[1], me * own_feat, own_feat, 0)

    x_row = gather_rows(token_rows)
    key_code = gather_rows(local_pos * 2 + key_ok)
    pos = key_code // 2
    qkv = dot_nn(x_row, m_qkv)
    q_raw, k_raw, v_raw = (qkv[:, i * own_feat : (i + 1) * own_feat] for i in range(3))
    squares = lax.psum(
        jnp.stack([jnp.sum(q_raw * q_raw, axis=-1), jnp.sum(k_raw * k_raw, axis=-1)]), "seq"
    )
    factors = lax.rsqrt(squares / feat_width + norm_eps)
    q_factor, k_factor = factors[0][:, None], factors[1][:, None]
    cosine, sine = rope_tables(pos, HEAD_DIM)
    head_shape = (row_len, own_heads, HEAD_DIM)
    query_low = rotate((q_raw * q_factor * gain_q).reshape(head_shape), cosine, sine).astype(bf16)
    key_low = rotate((k_raw * k_factor * gain_k).reshape(head_shape), cosine, sine).astype(bf16)
    value_low = v_raw.astype(bf16).reshape(head_shape)

    mask = allowed_mask(pos, key_code)[None]
    scores = jnp.einsum("qhd,khd->hqk", query_low, key_low, preferred_element_type=f32) * score_scale
    expo = jnp.where(mask, jnp.exp(scores), 0.0)
    weight_sum = jnp.transpose(jnp.sum(expo, axis=-1))[:, :, None]
    expo_low = expo.astype(bf16)
    attn = jnp.einsum("hqk,khd->qhd", expo_low, value_low, preferred_element_type=f32) / weight_sum
    attn_low = attn.astype(bf16).reshape(row_len, own_feat)

    branch = scatter_rows(dot_nt(attn_low, m_out))
    branch_factor = rms_factor(branch)
    branch_unit = branch * branch_factor
    hidden_in = token_rows.astype(f32) + branch_unit * gains[2]
    hidden_low = gather_rows(hidden_in.astype(bf16))
    gate_up = dot_nn(hidden_low, m_gu)
    gate_val, up_val = gate_up[:, :own_ff], gate_up[:, own_ff:]
    sigma = jax.nn.sigmoid(gate_val)
    mixed_low = (gate_val * sigma * up_val).astype(bf16)
    mlp_val = scatter_rows(dot_nt(mixed_low, m_down))
    mlp_factor = rms_factor(mlp_val)
    mlp_unit = mlp_val * mlp_factor
    layer_out = hidden_in + mlp_unit * gains[3]
    grad_gain_mlp = jnp.sum(grad_out * mlp_unit, axis=0)
    grad_mlp = gather_rows(norm_back(grad_out * gains[3], mlp_val, mlp_factor).astype(bf16))

    grad_mixed = dot_nn(grad_mlp, m_down)
    grad_gate = grad_mixed * up_val * sigma * (1.0 + gate_val * (1.0 - sigma))
    grad_up = grad_mixed * gate_val * sigma
    grad_gu = jnp.concatenate([grad_gate, grad_up], axis=1).astype(bf16)
    grad_hidden = grad_out + scatter_rows(dot_nt(grad_gu, m_gu))
    dw_gu = return_grads(dot_tn(hidden_low, grad_gu), [own_ff, own_ff], ways)
    dw_down = return_grads(dot_tn(grad_mlp, mixed_low), [own_ff], ways)
    grad_gain_attn = jnp.sum(grad_hidden * branch_unit, axis=0)
    grad_branch = gather_rows(
        norm_back(grad_hidden * gains[2], branch, branch_factor).astype(bf16)
    )
    grad_attn = dot_nn(grad_branch, m_out).reshape(head_shape)
    dw_out = return_grads(dot_tn(grad_branch, attn_low), [own_feat], ways)
    grad_num = (grad_attn / weight_sum).astype(bf16)
    drop = jnp.transpose(jnp.sum(grad_attn * attn, axis=-1) / weight_sum[:, :, 0])
    grad_expo = jnp.einsum("qhd,khd->hqk", grad_num, value_low, preferred_element_type=f32)
    grad_scores = (expo * (grad_expo - drop[:, :, None])).astype(bf16)
    grad_q = (
        jnp.einsum("hqk,khd->qhd", grad_scores, key_low, preferred_element_type=f32) * score_scale
    )
    grad_k = (
        jnp.einsum("hqk,qhd->khd", grad_scores, query_low, preferred_element_type=f32) * score_scale
    )
    grad_v = jnp.einsum("hqk,qhd->khd", expo_low, grad_num, preferred_element_type=f32)
    grad_q_norm = unrotate(grad_q, cosine, sine).reshape(row_len, own_feat)
    grad_k_norm = unrotate(grad_k, cosine, sine).reshape(row_len, own_feat)
    q_unit, k_unit = q_raw * q_factor, k_raw * k_factor
    grad_gain_query = jnp.sum(grad_q_norm * q_unit, axis=0)
    grad_gain_key = jnp.sum(grad_k_norm * k_unit, axis=0)
    c_q, c_k = grad_q_norm * gain_q, grad_k_norm * gain_k
    means = (
        lax.psum(jnp.stack([jnp.sum(c_q * q_unit, axis=-1), jnp.sum(c_k * k_unit, axis=-1)]), "seq")
        / feat_width
    )
    grad_q_raw = q_factor * (c_q - q_unit * means[0][:, None])
    grad_k_raw = k_factor * (c_k - k_unit * means[1][:, None])
    grad_qkv = jnp.concatenate(
        [grad_q_raw, grad_k_raw, grad_v.reshape(row_len, own_feat)], axis=1
    ).astype(bf16)
    grad_tokens = grad_hidden + scatter_rows(dot_nt(grad_qkv, m_qkv))

    own_slot = jnp.zeros((2, feat_width), f32)
    own_slot = lax.dynamic_update_slice(
        own_slot, jnp.stack([grad_gain_query, grad_gain_key]), (0, me * own_feat)
    )
    gain_terms = jnp.concatenate([own_slot, jnp.stack([grad_gain_attn, grad_gain_mlp])])
    gain_columns = jnp.pad(jnp.transpose(gain_terms), ((0, 0), (0, HEAD_DIM - 4)))
    dw_qkv = return_grads(
        jnp.concatenate([dot_tn(x_row, grad_qkv), gain_columns], axis=1),
        [own_feat] * 3 + [HEAD_DIM],
        ways,
    )
    gain_grads = jnp.sum(dw_qkv[3].reshape(-1, ways, HEAD_DIM), axis=1)
    gain_grads = jnp.transpose(gain_grads[:, :8])
    return (
        layer_out.astype(bf16)[None],
        grad_tokens.astype(bf16)[None],
        dw_qkv[0],
        dw_qkv[1],
        dw_qkv[2],
        jnp.transpose(dw_out[0]),
        dw_gu[0],
        dw_gu[1],
        jnp.transpose(dw_down[0]),
        gain_grads[0],
        gain_grads[1],
        gain_grads[2],
        gain_grads[3],
    )


def solution(mesh):
    both = ("dp", "seq")
    in_specs = (
        P("dp", "seq", None),
        P(both, None),
        P(both, None),
        P(both, None),
        P(None, both),
        P(both, None),
        P(both, None),
        P(None, both),
        P(both),
        P(both),
        P(both),
        P(both),
        P("dp", "seq", None),
        P("dp", "seq"),
        P("dp"),
        P("dp", "seq"),
    )
    out_specs = (
        P("dp", "seq", None),
        P("dp", "seq", None),
        P(both, None),
        P(both, None),
        P(both, None),
        P(None, both),
        P(both, None),
        P(both, None),
        P(None, both),
        P(both),
        P(both),
        P(both),
        P(both),
    )
    return jax.shard_map(body, mesh=mesh, in_specs=in_specs, out_specs=out_specs, check_vma=False)
```

```python
import functools

import jax
import jax.numpy as jnp
from jax import lax
from jax.experimental import pallas as pl
from jax.experimental.pallas import tpu as pltpu
from jax.sharding import PartitionSpec as P

MESH = pl.DeviceIdType.MESH

HEAD_DIM = 128

rope_base = 500000.0
norm_eps = 1e-06
f32 = jnp.float32
bf16 = jnp.bfloat16


def rms_factor(values):
    return lax.rsqrt(jnp.mean(values * values, axis=-1, keepdims=True) + norm_eps)


def norm_back(grad_normed, raw_values, factor):
    unit_values = raw_values * factor
    return factor * (
        grad_normed - unit_values * jnp.mean(grad_normed * unit_values, axis=-1, keepdims=True)
    )


def rope_tables(positions, head_dim):
    half_dim = head_dim // 2
    steps_f = jnp.arange(half_dim).astype(f32) * (2.0 / head_dim)
    inv_freq = jnp.power(rope_base, -steps_f)
    angle = positions.astype(f32)[:, None] * inv_freq[None, :]
    angle = jnp.concatenate([angle, angle], axis=-1)[:, None, :]
    return (jnp.cos(angle), jnp.sin(angle))


def rotate(values, cosine, sine):
    half_dim = values.shape[-1] // 2
    turned = jnp.concatenate([-values[..., half_dim:], values[..., :half_dim]], axis=-1)
    return values * cosine + turned * sine


def unrotate(grads, cosine, sine):
    half_dim = grads.shape[-1] // 2
    moved = grads * sine
    back_part = jnp.concatenate([moved[..., half_dim:], -moved[..., :half_dim]], axis=-1)
    return grads * cosine + back_part


def allowed_mask(query_pos, key_code):
    key_pos = key_code // 2
    usable = key_code % 2 == 1
    causal = key_pos[None, :] <= query_pos[:, None]
    return causal & (usable[None, :] | (key_pos[None, :] == query_pos[:, None]))


def dot_nn(left, right):
    return jnp.dot(left, right, preferred_element_type=f32)


def dot_nt(left, right):
    return lax.dot_general(left, right, (((1,), (1,)), ((), ())), preferred_element_type=f32)


def dot_tn(left, right):
    return lax.dot_general(left, right, (((0,), (0,)), ((), ())), preferred_element_type=f32)


def across(piece):
    return lax.all_gather(piece, "dp", axis=0, tiled=True)


def dp_sum(grad):
    return lax.psum_scatter(grad, "dp", scatter_dimension=0, tiled=True)


def send_home(summed, ways):
    return lax.all_to_all(summed, "seq", split_axis=0, concat_axis=1, tiled=True)


def split_grads(moved, widths, ways):
    rows = moved.shape[0]
    moved = moved.reshape(rows, ways, sum(widths))
    outs, begin = [], 0
    for width in widths:
        outs.append(moved[:, :, begin : begin + width].reshape(rows, ways * width).astype(f32))
        begin += width
    return outs


class Line:
    def __init__(self, ways):
        self.chips = ways // 2
        self.last = self.chips - 1
        self.me = lax.axis_index("seq")
        self.chip = self.me // 2
        self.core = self.me % 2
        self.sibling = self.me + 1 - 2 * self.core

    def greet(self):
        barrier = pltpu.get_barrier_semaphore()
        has_low = jnp.minimum(self.chip, 1)
        has_high = jnp.minimum(self.last - self.chip, 1)
        pl.semaphore_signal(barrier, inc=1, device_id={"seq": self.sibling}, device_id_type=MESH)

        @pl.when(self.chip > 0)
        def _():
            pl.semaphore_signal(barrier, inc=1, device_id={"seq": self.me - 2}, device_id_type=MESH)

        @pl.when(self.chip < self.last)
        def _():
            pl.semaphore_signal(barrier, inc=1, device_id={"seq": self.me + 2}, device_id_type=MESH)

        pl.semaphore_wait(barrier, 1 + has_low + has_high)


def remote(src, dst, send_sem, recv_sem, device):
    return pltpu.make_async_remote_copy(
        src_ref=src,
        dst_ref=dst,
        send_sem=send_sem,
        recv_sem=recv_sem,
        device_id={"seq": device},
        device_id_type=MESH,
    )


def rows_at(index, count):
    return pl.ds(pl.multiple_of(index * count, count), count)


def each_strip(tok_count, strip, fn):
    def one(i, carry):
        fn(rows_at(i, strip))
        return carry

    lax.fori_loop(0, tok_count // strip, one, 0)


class RowGather:
    def __init__(self, line, tok, row_buf, sems):
        self.line, self.tok, self.buf = line, tok, row_buf
        self.up_send, self.down_send, self.col_recv, self.sib_send, self.sib_recv = sems

    @staticmethod
    def scratch(chips):
        return [pltpu.SemaphoreType.DMA((chips,))] * 5

    def piece(self, src, core):
        return self.buf.at[rows_at(2 * src + core, self.tok)]

    def hop(self, src, device, send):
        piece = self.piece(src, self.line.core)
        return remote(piece, piece, send.at[src], self.col_recv.at[src], device)

    def swap(self, src, core):
        piece = self.piece(src, core)
        return remote(
            piece, piece, self.sib_send.at[src], self.sib_recv.at[src], self.line.sibling
        )

    def start(self):
        line = self.line
        self.forward_up(line.chip)
        self.forward_down(line.chip)
        self.swap(line.chip, line.core).start()

    def forward_up(self, src):
        @pl.when(self.line.chip < self.line.last)
        def _():
            self.hop(src, self.line.me + 2, self.up_send).start()

    def forward_down(self, src):
        @pl.when(self.line.chip > 0)
        def _():
            self.hop(src, self.line.me - 2, self.down_send).start()

    def receive(self, src, up):
        self.hop(src, self.line.sibling, self.up_send).wait_recv()
        if up:
            self.forward_up(src)
        else:
            self.forward_down(src)
        self.swap(src, self.line.core).start()

    def visit(self, use_block):
        line = self.line
        self.swap(line.chip, 1 - line.core).wait_recv()
        use_block(line.chip)
        for away in range(1, line.chips):
            low, high = line.chip - away, line.chip + away

            @pl.when(low >= 0)
            def _():
                self.receive(low, True)

            @pl.when(high <= line.last)
            def _():
                self.receive(high, False)

            for src, there in ((low, low >= 0), (high, high <= line.last)):

                @pl.when(there)
                def _(src=src):
                    self.swap(src, 1 - line.core).wait_recv()
                    use_block(src)

    def finish(self):
        line = self.line
        for src in range(line.chips):
            self.swap(src, line.core).wait_send()

            @pl.when((src <= line.chip) & (line.chip < line.last))
            def _():
                self.hop(src, line.sibling, self.up_send).wait_send()

            @pl.when((src >= line.chip) & (line.chip > 0))
            def _():
                self.hop(src, line.sibling, self.down_send).wait_send()


class RowScatter:
    def __init__(self, line, tok, bufs, sems):
        self.line, self.tok = line, tok
        self.pair, self.sib_in, self.acc = bufs
        self.sib_send, self.sib_recv, self.send, self.recv = sems

    @staticmethod
    def scratch(chips, tok, width):
        return [
            pltpu.VMEM((2 * chips * tok, width), bf16),
            pltpu.VMEM((chips * tok, width), bf16),
            pltpu.VMEM(((chips + 1) * tok, width), bf16),
            pltpu.SemaphoreType.DMA((chips,)),
            pltpu.SemaphoreType.DMA((chips,)),
            pltpu.SemaphoreType.DMA((chips,)),
            pltpu.SemaphoreType.DMA((chips + 1,)),
        ]

    def swap(self, dest):
        tok, line = self.tok, self.line
        return remote(
            self.pair.at[rows_at(2 * dest + 1 - line.core, tok)],
            self.sib_in.at[rows_at(dest, tok)],
            self.sib_send.at[dest],
            self.sib_recv.at[dest],
            line.sibling,
        )

    def hop(self, dest, slot, device):
        tok = self.tok
        return remote(
            self.acc.at[rows_at(dest, tok)],
            self.acc.at[rows_at(slot, tok)],
            self.send.at[dest],
            self.recv.at[slot],
            device,
        )

    def produce(self, dest, left, right, tile):
        rows = rows_at(dest, 2 * self.tok)

        def one(n, carry):
            cols = rows_at(n, tile)
            self.pair[rows, cols] = dot_nt(left[rows, :], right[cols, :]).astype(bf16)
            return carry

        lax.fori_loop(0, right.shape[0] // tile, one, 0)
        self.swap(dest).start()

    def chip_sum(self, dest, strip):
        mine = self.pair[pl.ds((2 * dest + self.line.core) * self.tok + strip.start, strip.size), :]
        other = self.sib_in[pl.ds(dest * self.tok + strip.start, strip.size), :]
        return mine.astype(f32) + other.astype(f32)

    def acc_strip(self, slot, strip):
        return pl.ds(slot * self.tok + strip.start, strip.size)

    def run(self, left, right, tile):
        line, tok = self.line, self.tok
        chips = line.chips
        near_low = 1 - line.chip // (chips // 2)

        def leg(j, first):
            up = near_low if first else 1 - near_low
            dest = up * (chips - j) + (1 - up) * (j - 1)
            step = 2 * up - 1
            return up, dest, step, (dest - line.chip) * step > 0

        def make(j):
            for first in (True, False):
                up, dest, step, there = leg(j, first)

                @pl.when(there)
                def _(dest=dest):
                    self.produce(dest, left, right, tile)

        def pass_on(j):
            for first in (True, False):
                up, dest, step, there = leg(j, first)
                behind = up * line.chip + (1 - up) * (line.last - line.chip)
                target = line.chip + step
                ends = 1 - jnp.minimum((dest - target) * step, 1)
                slot = dest + (1 - up) * ends * (chips - dest)

                @pl.when(there)
                def _(dest=dest, behind=behind, slot=slot, step=step):
                    self.swap(dest).wait_recv()

                    @pl.when(behind > 0)
                    def _():
                        self.hop(dest, dest, line.sibling).wait_recv()

                        def add(strip):
                            at = self.acc_strip(dest, strip)
                            total = self.chip_sum(dest, strip) + self.acc[at, :].astype(f32)
                            self.acc[at, :] = total.astype(bf16)

                        each_strip(tok, 16, add)

                    @pl.when(behind == 0)
                    def _():
                        def put(strip):
                            at = self.acc_strip(dest, strip)
                            self.acc[at, :] = self.chip_sum(dest, strip).astype(bf16)

                        each_strip(tok, 16, put)

                    self.hop(dest, slot, line.me + 2 * step).start()

        make(1)
        for j in range(1, chips):
            if j + 1 < chips:
                make(j + 1)
            else:
                self.produce(line.chip, left, right, tile)
            pass_on(j)
        self.swap(line.chip).wait_recv()

        @pl.when(line.chip > 0)
        def _():
            self.hop(line.chip, line.chip, line.sibling).wait_recv()

        @pl.when(line.chip == 0)
        def _():
            self.acc[rows_at(line.chip, tok), :] = jnp.zeros((tok, self.acc.shape[1]), bf16)

        @pl.when(line.chip < line.last)
        def _():
            self.hop(line.chip, chips, line.sibling).wait_recv()

        @pl.when(line.chip == line.last)
        def _():
            self.acc[rows_at(chips, tok), :] = jnp.zeros((tok, self.acc.shape[1]), bf16)

    def total(self, strip):
        low = self.acc[self.acc_strip(self.line.chip, strip), :].astype(f32)
        high = self.acc[self.acc_strip(self.line.chips, strip), :].astype(f32)
        return self.chip_sum(self.line.chip, strip) + (low + high)

    def finish(self):
        line = self.line
        for dest in range(line.chips):
            self.swap(dest).wait_send()

            @pl.when(line.chip != dest)
            def _():
                self.hop(dest, dest, line.sibling).wait_send()


def mean_rows(values):
    return jnp.sum(values, axis=-1, keepdims=True) * (1.0 / values.shape[-1])


def call(kernel, outs, scratch, args, ident, cost=1):
    return pl.pallas_call(
        kernel,
        out_shape=outs,
        in_specs=[pl.BlockSpec(memory_space=pltpu.VMEM)] * len(args),
        out_specs=[pl.BlockSpec(memory_space=pltpu.VMEM)] * len(outs),
        scratch_shapes=scratch,
        cost_estimate=pl.CostEstimate(
            flops=cost * 10**9, transcendentals=0, bytes_accessed=cost * 3 * 10**6
        ),
        compiler_params=pltpu.CompilerParams(
            collective_id=ident, has_side_effects=True, vmem_limit_bytes=60 * 2**20
        ),
    )(*args)


def shape(dims, kind):
    return jax.ShapeDtypeStruct(dims, kind)


def gather_project(rows, codes, weights, ways, ident):
    tok, width = rows.shape
    cols = weights.shape[1]

    def kernel(rows_ref, code_ref, w_ref, all_ref, codes_ref, prod_ref, code_send, code_recv, *sems):
        line = Line(ways)
        me = line.me
        barrier = pltpu.get_barrier_semaphore()
        for off in range(1, ways):
            pl.semaphore_signal(
                barrier, inc=1, device_id={"seq": (me + off) % ways}, device_id_type=MESH
            )
        pl.semaphore_wait(barrier, ways - 1)
        gather = RowGather(line, tok, all_ref, sems)
        all_ref[rows_at(me, tok), :] = rows_ref[...]
        gather.start()
        codes_ref[me] = code_ref[...]

        def tell(off):
            return remote(
                code_ref, codes_ref.at[me], code_send.at[off], code_recv.at[off], (me + off) % ways
            )

        for off in range(1, ways):
            tell(off).start()

        def use(chip):
            at = rows_at(chip, 2 * tok)

            def one(n, carry):
                here = rows_at(n, 256)
                prod_ref[at, here] = dot_nn(all_ref[at, :], w_ref[:, here])
                return carry

            lax.fori_loop(0, cols // 256, one, 0)

        gather.visit(use)
        gather.finish()
        for off in range(1, ways):
            tell(off).wait()

    return call(
        kernel,
        [
            shape((ways * tok, width), bf16),
            shape((ways,) + codes.shape, jnp.int32),
            shape((ways * tok, cols), f32),
        ],
        [pltpu.SemaphoreType.DMA((ways,))] * 2 + RowGather.scratch(ways // 2),
        [rows, codes, weights],
        ident,
        55,
    )


def attn_out_to_ff(attn_low, m_out, m_gu, token_rows, gain_row, ways, ident):
    tok, width = token_rows.shape
    own_ff = m_gu.shape[1] // 2
    row = ways * tok

    def kernel(left, right, w_ref, x_ref, gain_ref, branch_ref, in_ref, all_ref, gu_ref, mix_ref, *rest):
        line = Line(ways)
        line.greet()
        scatter = RowScatter(line, tok, rest[:3], rest[3:7])
        gather = RowGather(line, tok, all_ref, rest[7:])
        scatter.run(left, right, 256)

        def settle(strip):
            branch = scatter.total(strip)
            factor = lax.rsqrt(mean_rows(branch * branch) + norm_eps)
            hidden = x_ref[strip, :].astype(f32) + branch * factor * gain_ref[...]
            branch_ref[strip, :] = branch
            in_ref[strip, :] = hidden
            all_ref[pl.ds(line.me * tok + strip.start, strip.size), :] = hidden.astype(bf16)

        each_strip(tok, 16, settle)
        gather.start()

        def use(chip):
            at = rows_at(chip, 2 * tok)

            def one(n, carry):
                here, there = rows_at(n, 256), pl.ds(pl.multiple_of(own_ff + n * 256, 256), 256)
                block = all_ref[at, :]
                gate = dot_nn(block, w_ref[:, here])
                up = dot_nn(block, w_ref[:, there])
                gu_ref[at, here] = gate.astype(bf16)
                gu_ref[at, there] = up.astype(bf16)
                mix_ref[at, here] = (gate * jax.nn.sigmoid(gate) * up).astype(bf16)
                return carry

            lax.fori_loop(0, own_ff // 256, one, 0)

        gather.visit(use)
        gather.finish()
        scatter.finish()

    return call(
        kernel,
        [
            shape((tok, width), f32),
            shape((tok, width), f32),
            shape((row, width), bf16),
            shape((row, 2 * own_ff), bf16),
            shape((row, own_ff), bf16),
        ],
        RowScatter.scratch(ways // 2, tok, width) + RowGather.scratch(ways // 2),
        [attn_low, m_out, m_gu, token_rows, gain_row],
        ident,
        105,
    )


def ff_turn(mixed_low, m_down, gate_up, hidden_in, grad_out, gain_row, ways, ident):
    tok, width = hidden_in.shape
    own_ff = m_down.shape[1]
    row = ways * tok

    def kernel(left, w_ref, gu_ref, in_ref, go_ref, gain_ref, out_ref, gg_ref, all_ref, dgu_ref, *rest):
        line = Line(ways)
        line.greet()
        scatter = RowScatter(line, tok, rest[:3], rest[3:7])
        gather = RowGather(line, tok, all_ref, rest[7:])
        scatter.run(left, w_ref, 256)
        gg_ref[...] = jnp.zeros_like(gg_ref)

        def settle(strip):
            mlp = scatter.total(strip)
            factor = lax.rsqrt(mean_rows(mlp * mlp) + norm_eps)
            unit = mlp * factor
            grad = go_ref[strip, :].astype(f32)
            out_ref[strip, :] = (in_ref[strip, :] + unit * gain_ref[...]).astype(bf16)
            terms = grad * unit
            gg_ref[...] += terms[:8] + terms[8:]
            lifted = grad * gain_ref[...]
            back = factor * (lifted - unit * mean_rows(lifted * unit))
            all_ref[pl.ds(line.me * tok + strip.start, strip.size), :] = back.astype(bf16)

        each_strip(tok, 16, settle)
        gather.start()

        def use(chip):
            at = rows_at(chip, 2 * tok)

            def one(n, carry):
                here, there = rows_at(n, 256), pl.ds(pl.multiple_of(own_ff + n * 256, 256), 256)
                grad = dot_nn(all_ref[at, :], w_ref[:, here])
                gate, up = gu_ref[at, here].astype(f32), gu_ref[at, there].astype(f32)
                sigma = jax.nn.sigmoid(gate)
                dgu_ref[at, here] = (grad * up * sigma * (1.0 + gate * (1.0 - sigma))).astype(bf16)
                dgu_ref[at, there] = (grad * gate * sigma).astype(bf16)
                return carry

            lax.fori_loop(0, own_ff // 256, one, 0)

        gather.visit(use)
        gather.finish()
        scatter.finish()

    return call(
        kernel,
        [
            shape((tok, width), bf16),
            shape((8, width), f32),
            shape((row, width), bf16),
            shape((row, 2 * own_ff), bf16),
        ],
        RowScatter.scratch(ways // 2, tok, width) + RowGather.scratch(ways // 2),
        [mixed_low, m_down, gate_up, hidden_in, grad_out, gain_row],
        ident,
        105,
    )


def ff_to_attn_back(grad_gu, m_gu, m_out, branch, grad_out, gain_row, ways, ident):
    tok, width = branch.shape
    own_feat = m_out.shape[1]
    row = ways * tok

    def kernel(left, right, w_ref, br_ref, go_ref, gain_ref, gh_ref, gg_ref, all_ref, ga_ref, *rest):
        line = Line(ways)
        line.greet()
        scatter = RowScatter(line, tok, rest[:3], rest[3:7])
        gather = RowGather(line, tok, all_ref, rest[7:])
        scatter.run(left, right, 256)
        gg_ref[...] = jnp.zeros_like(gg_ref)

        def settle(strip):
            grad = scatter.total(strip) + go_ref[strip, :].astype(f32)
            branch = br_ref[strip, :]
            factor = lax.rsqrt(mean_rows(branch * branch) + norm_eps)
            unit = branch * factor
            gh_ref[strip, :] = grad
            terms = grad * unit
            gg_ref[...] += terms[:8] + terms[8:]
            lifted = grad * gain_ref[...]
            back = factor * (lifted - unit * mean_rows(lifted * unit))
            all_ref[pl.ds(line.me * tok + strip.start, strip.size), :] = back.astype(bf16)

        each_strip(tok, 16, settle)
        gather.start()

        def use(chip):
            at = rows_at(chip, 2 * tok)
            ga_ref[at, :] = dot_nn(all_ref[at, :], w_ref[...])

        gather.visit(use)
        gather.finish()
        scatter.finish()

    return call(
        kernel,
        [
            shape((tok, width), f32),
            shape((8, width), f32),
            shape((row, width), bf16),
            shape((row, own_feat), f32),
        ],
        RowScatter.scratch(ways // 2, tok, width) + RowGather.scratch(ways // 2),
        [grad_gu, m_gu, m_out, branch, grad_out, gain_row],
        ident,
        105,
    )


def project_back(grad_qkv, m_qkv, grad_hidden, ways, ident):
    tok, width = grad_hidden.shape

    def kernel(left, right, gh_ref, out_ref, *rest):
        line = Line(ways)
        line.greet()
        scatter = RowScatter(line, tok, rest[:3], rest[3:7])
        scatter.run(left, right, 256)

        def settle(strip):
            out_ref[strip, :] = (gh_ref[strip, :] + scatter.total(strip)).astype(bf16)

        each_strip(tok, 16, settle)
        scatter.finish()

    return call(
        kernel,
        [shape((tok, width), bf16)],
        RowScatter.scratch(ways // 2, tok, width),
        [grad_qkv, m_qkv, grad_hidden],
        ident,
        55,
    )[0]


def exchange(sources, ways, ident, cost):
    rows = sources[0].shape[0]
    widths = [a.shape[1] // ways for a in sources]
    begins = [sum(widths[:i]) for i in range(len(widths))]
    count = len(sources)

    def kernel(*refs):
        ins, out_ref, send, recv, local = refs[:count], *refs[count:]
        me = lax.axis_index("seq")
        barrier = pltpu.get_barrier_semaphore()

        def greet(off, carry):
            pl.semaphore_signal(
                barrier, inc=1, device_id={"seq": (me + off) % ways}, device_id_type=MESH
            )
            return carry

        def move(off, i):
            dest = (me + off) % ways
            return remote(
                ins[i].at[:, rows_at(dest, widths[i])],
                out_ref.at[rows_at(me, rows), pl.ds(begins[i], widths[i])],
                send.at[off * count + i],
                recv.at[off * count + i],
                dest,
            )

        def keep(i):
            return pltpu.make_async_copy(
                ins[i].at[:, rows_at(me, widths[i])],
                out_ref.at[rows_at(me, rows), pl.ds(begins[i], widths[i])],
                local.at[i],
            )

        def each(what):
            def one(off, carry):
                for i in range(count):
                    what(move(off, i))
                return carry

            lax.fori_loop(1, ways, one, 0)

        for i in range(count):
            keep(i).start()
        lax.fori_loop(1, ways, greet, 0)
        pl.semaphore_wait(barrier, ways - 1)
        each(lambda copy: copy.start())
        for i in range(count):
            keep(i).wait()
        each(lambda copy: copy.wait())

    return pl.pallas_call(
        kernel,
        out_shape=shape((ways * rows, sum(widths)), bf16),
        in_specs=[pl.BlockSpec(memory_space=pl.ANY)] * count,
        out_specs=pl.BlockSpec(memory_space=pl.ANY),
        scratch_shapes=[
            pltpu.SemaphoreType.DMA((ways * count,)),
            pltpu.SemaphoreType.DMA((ways * count,)),
            pltpu.SemaphoreType.DMA((count,)),
        ],
        cost_estimate=pl.CostEstimate(
            flops=cost * 10**9, transcendentals=0, bytes_accessed=cost * 3 * 10**6
        ),
        compiler_params=pltpu.CompilerParams(collective_id=ident, has_side_effects=True),
    )(*sources)


def line_sum(terms, ways, ident):
    def kernel(terms_ref, out_ref, slots, send, recv):
        me = lax.axis_index("seq")
        barrier = pltpu.get_barrier_semaphore()
        for off in range(1, ways):
            pl.semaphore_signal(
                barrier, inc=1, device_id={"seq": (me + off) % ways}, device_id_type=MESH
            )
        pl.semaphore_wait(barrier, ways - 1)
        for off in range(1, ways):
            remote(
                terms_ref, slots.at[off], send.at[off], recv.at[off], (me + off) % ways
            ).start()
        total = terms_ref[...]
        for off in range(1, ways):
            remote(terms_ref, slots.at[off], send.at[off], recv.at[off], (me + off) % ways).wait_recv()
            total = total + slots[off]
        out_ref[...] = total
        for off in range(1, ways):
            remote(terms_ref, slots.at[off], send.at[off], recv.at[off], (me + off) % ways).wait_send()

    return call(
        kernel,
        [shape(terms.shape, f32)],
        [
            pltpu.VMEM((ways,) + terms.shape, f32),
            pltpu.SemaphoreType.DMA((ways,)),
            pltpu.SemaphoreType.DMA((ways,)),
        ],
        [terms],
        ident,
        8,
    )[0]


def body(
    tokens,
    w_query,
    w_key,
    w_value,
    w_out,
    w_gate,
    w_up,
    w_down,
    gain_query,
    gain_key,
    gain_attn,
    gain_mlp,
    cotangent,
    key_mask,
    lengths,
    tract_order,
):
    ways = lax.axis_size("seq")
    me = lax.axis_index("seq")
    token_rows = tokens[0]
    tok_count, feat_width = token_rows.shape
    ff_width = w_gate.shape[1]
    own_feat = feat_width // ways
    own_heads = own_feat // HEAD_DIM
    own_ff = ff_width // ways
    row_len = tok_count * ways
    score_scale = HEAD_DIM ** (-0.5)
    half_len = tok_count // 2
    order_pair = tract_order[0]
    slot_index = jnp.arange(tok_count, dtype=jnp.int32)
    local_pos = (
        jnp.where(slot_index < half_len, order_pair[0], order_pair[1]) * half_len
        + slot_index % half_len
    )
    key_ok = ((key_mask[0] == 1) & (local_pos < lengths[0])).astype(jnp.int32)

    gain_local = jnp.stack([gain_query, gain_key, gain_attn, gain_mlp], axis=1)
    gain_pad = jnp.pad(gain_local, ((0, 0), (0, HEAD_DIM - 4)))
    gain_all = jnp.tile(gain_pad, (1, ways))
    p_qkv = exchange([w_query, w_key, w_value], ways, 8, 20)
    m_qkv = across(p_qkv)
    p_qkv, w_gate, w_up, w_out_t, w_down_t, gain_all = lax.optimization_barrier(
        (p_qkv, w_gate, w_up, jnp.transpose(w_out), jnp.transpose(w_down), gain_all)
    )
    p_out = exchange([w_out_t, gain_all], ways, 9, 8)
    p_gu = exchange([w_gate, w_up], ways, 10, 40)
    p_down = exchange([w_down_t], ways, 11, 20)
    m_out, m_gu, m_down = across(p_out), across(p_gu), across(p_down)
    gains = jnp.transpose(m_out[:, own_feat:])[:8].astype(f32)
    m_out = m_out[:, :own_feat]
    gain_q = lax.dynamic_slice_in_dim(gains[0], me * own_feat, own_feat, 0)
    gain_k = lax.dynamic_slice_in_dim(gains[1], me * own_feat, own_feat, 0)

    code_pad = -tok_count % HEAD_DIM
    local_code = jnp.pad(local_pos * 2 + key_ok, (0, code_pad))[None]
    x_row, codes, qkv = gather_project(token_rows, local_code, m_qkv, ways, 1)
    key_code = codes[:, 0, :tok_count].reshape(row_len)
    pos = key_code // 2
    q_raw, k_raw, v_raw = (qkv[:, i * own_feat : (i + 1) * own_feat] for i in range(3))
    squares = line_sum(
        jnp.stack([jnp.sum(q_raw * q_raw, axis=-1), jnp.sum(k_raw * k_raw, axis=-1)]), ways, 2
    )
    factors = lax.rsqrt(squares / feat_width + norm_eps)
    q_factor, k_factor = factors[0][:, None], factors[1][:, None]
    cosine, sine = rope_tables(pos, HEAD_DIM)
    head_shape = (row_len, own_heads, HEAD_DIM)
    query_low = rotate((q_raw * q_factor * gain_q).reshape(head_shape), cosine, sine).astype(bf16)
    key_low = rotate((k_raw * k_factor * gain_k).reshape(head_shape), cosine, sine).astype(bf16)
    value_low = v_raw.astype(bf16).reshape(head_shape)

    mask = allowed_mask(pos, key_code)[None]
    scores = jnp.einsum("qhd,khd->hqk", query_low, key_low, preferred_element_type=f32) * score_scale
    expo = jnp.where(mask, jnp.exp(scores), 0.0)
    weight_sum = jnp.transpose(jnp.sum(expo, axis=-1))[:, :, None]
    expo_low = expo.astype(bf16)
    attn = jnp.einsum("hqk,khd->qhd", expo_low, value_low, preferred_element_type=f32) / weight_sum
    attn_low = attn.astype(bf16).reshape(row_len, own_feat)

    branch, hidden_in, hidden_low, gate_up, mixed_low = attn_out_to_ff(
        attn_low, m_out, m_gu, token_rows, gains[2:3], ways, 3
    )
    layer_out, grad_gain_mlp, grad_mlp, grad_gu = ff_turn(
        mixed_low, m_down, gate_up, hidden_in, cotangent[0], gains[3:4], ways, 4
    )
    d_down = dot_tn(grad_mlp, mixed_low).astype(bf16)
    d_gu = dot_tn(hidden_low, grad_gu).astype(bf16)
    grad_gu, d_down, d_gu = lax.optimization_barrier((grad_gu, d_down, d_gu))
    d_down = dp_sum(d_down)
    d_gu = dp_sum(d_gu)
    grad_hidden, grad_gain_attn, grad_branch, grad_attn = ff_to_attn_back(
        grad_gu, m_gu, m_out, branch, cotangent[0], gains[2:3], ways, 5
    )
    grad_attn, d_down = lax.optimization_barrier((grad_attn, d_down))
    d_down = send_home(d_down, ways)
    grad_attn = grad_attn.reshape(head_shape)
    grad_num = (grad_attn / weight_sum).astype(bf16)
    drop = jnp.transpose(jnp.sum(grad_attn * attn, axis=-1) / weight_sum[:, :, 0])
    grad_expo = jnp.einsum("qhd,khd->hqk", grad_num, value_low, preferred_element_type=f32)
    grad_scores = (expo * (grad_expo - drop[:, :, None])).astype(bf16)
    grad_q = (
        jnp.einsum("hqk,khd->qhd", grad_scores, key_low, preferred_element_type=f32) * score_scale
    )
    grad_k = (
        jnp.einsum("hqk,qhd->khd", grad_scores, query_low, preferred_element_type=f32) * score_scale
    )
    grad_v = jnp.einsum("hqk,qhd->khd", expo_low, grad_num, preferred_element_type=f32)
    grad_q_norm = unrotate(grad_q, cosine, sine).reshape(row_len, own_feat)
    grad_k_norm = unrotate(grad_k, cosine, sine).reshape(row_len, own_feat)
    q_unit, k_unit = q_raw * q_factor, k_raw * k_factor
    grad_gain_query = jnp.sum(grad_q_norm * q_unit, axis=0)
    grad_gain_key = jnp.sum(grad_k_norm * k_unit, axis=0)
    c_q, c_k = grad_q_norm * gain_q, grad_k_norm * gain_k
    terms = jnp.stack([jnp.sum(c_q * q_unit, axis=-1), jnp.sum(c_k * k_unit, axis=-1)])
    terms, d_down, d_gu = lax.optimization_barrier((terms, d_down, d_gu))
    means = line_sum(terms, ways, 6) / feat_width
    dw_down = split_grads(d_down, [own_ff], ways)
    dw_gu = split_grads(send_home(d_gu, ways), [own_ff, own_ff], ways)
    grad_q_raw = q_factor * (c_q - q_unit * means[0][:, None])
    grad_k_raw = k_factor * (c_k - k_unit * means[1][:, None])
    grad_qkv = jnp.concatenate(
        [grad_q_raw, grad_k_raw, grad_v.reshape(row_len, own_feat)], axis=1
    ).astype(bf16)

    own_slot = jnp.zeros((2, feat_width), f32)
    own_slot = lax.dynamic_update_slice(
        own_slot, jnp.stack([grad_gain_query, grad_gain_key]), (0, me * own_feat)
    )
    gain_terms = jnp.concatenate(
        [
            own_slot,
            jnp.sum(grad_gain_attn, axis=0, keepdims=True),
            jnp.sum(grad_gain_mlp, axis=0, keepdims=True),
        ]
    )
    gain_columns = jnp.pad(jnp.transpose(gain_terms), ((0, 0), (0, HEAD_DIM - 4)))
    d_attn = jnp.concatenate(
        [dot_tn(x_row, grad_qkv), dot_tn(grad_branch, attn_low), gain_columns], axis=1
    ).astype(bf16)
    grad_qkv, d_attn = lax.optimization_barrier((grad_qkv, d_attn))
    dw_qkv = split_grads(
        send_home(dp_sum(d_attn), ways), [own_feat] * 4 + [HEAD_DIM], ways
    )
    grad_tokens = project_back(grad_qkv, m_qkv, grad_hidden, ways, 7)
    gain_grads = jnp.sum(dw_qkv[4].reshape(-1, ways, HEAD_DIM), axis=1)
    gain_grads = jnp.transpose(gain_grads[:, :8])
    return (
        layer_out[None],
        grad_tokens[None],
        dw_qkv[0],
        dw_qkv[1],
        dw_qkv[2],
        jnp.transpose(dw_qkv[3]),
        dw_gu[0],
        dw_gu[1],
        jnp.transpose(dw_down[0]),
        gain_grads[0],
        gain_grads[1],
        gain_grads[2],
        gain_grads[3],
    )


def solution(mesh):
    both = ("dp", "seq")
    in_specs = (
        P("dp", "seq", None),
        P(both, None),
        P(both, None),
        P(both, None),
        P(None, both),
        P(both, None),
        P(both, None),
        P(None, both),
        P(both),
        P(both),
        P(both),
        P(both),
        P("dp", "seq", None),
        P("dp", "seq"),
        P("dp"),
        P("dp", "seq"),
    )
    out_specs = (
        P("dp", "seq", None),
        P("dp", "seq", None),
        P(both, None),
        P(both, None),
        P(both, None),
        P(None, both),
        P(both, None),
        P(both, None),
        P(None, both),
        P(both),
        P(both),
        P(both),
        P(both),
    )
    return jax.shard_map(body, mesh=mesh, in_specs=in_specs, out_specs=out_specs, check_vma=False)
```

```python
import functools

import jax
import jax.numpy as jnp
from jax import lax
from jax.experimental import pallas as pl
from jax.experimental.pallas import tpu as pltpu
from jax.sharding import PartitionSpec as P

MESH = pl.DeviceIdType.MESH

HEAD_DIM = 128

rope_base = 500000.0
norm_eps = 1e-06
f32 = jnp.float32
bf16 = jnp.bfloat16


def rms_factor(values):
    return lax.rsqrt(jnp.mean(values * values, axis=-1, keepdims=True) + norm_eps)


def norm_back(grad_normed, raw_values, factor):
    unit_values = raw_values * factor
    return factor * (
        grad_normed - unit_values * jnp.mean(grad_normed * unit_values, axis=-1, keepdims=True)
    )


def rope_tables(positions, head_dim):
    half_dim = head_dim // 2
    steps_f = jnp.arange(half_dim).astype(f32) * (2.0 / head_dim)
    inv_freq = jnp.power(rope_base, -steps_f)
    angle = positions.astype(f32)[:, None] * inv_freq[None, :]
    angle = jnp.concatenate([angle, angle], axis=-1)[:, None, :]
    return (jnp.cos(angle), jnp.sin(angle))


def rotate(values, cosine, sine):
    half_dim = values.shape[-1] // 2
    turned = jnp.concatenate([-values[..., half_dim:], values[..., :half_dim]], axis=-1)
    return values * cosine + turned * sine


def unrotate(grads, cosine, sine):
    half_dim = grads.shape[-1] // 2
    moved = grads * sine
    back_part = jnp.concatenate([moved[..., half_dim:], -moved[..., :half_dim]], axis=-1)
    return grads * cosine + back_part


def allowed_mask(query_pos, key_code):
    key_pos = key_code // 2
    usable = key_code % 2 == 1
    causal = key_pos[None, :] <= query_pos[:, None]
    return causal & (usable[None, :] | (key_pos[None, :] == query_pos[:, None]))


def dot_nn(left, right):
    return jnp.dot(left, right, preferred_element_type=f32)


def dot_nt(left, right):
    return lax.dot_general(left, right, (((1,), (1,)), ((), ())), preferred_element_type=f32)


def dot_tn(left, right):
    return lax.dot_general(left, right, (((0,), (0,)), ((), ())), preferred_element_type=f32)


def across(piece):
    return lax.all_gather(piece, "dp", axis=0, tiled=True)


def dp_sum(grad):
    return lax.psum_scatter(grad, "dp", scatter_dimension=0, tiled=True)


def send_home(summed, ways):
    return lax.all_to_all(summed, "seq", split_axis=0, concat_axis=1, tiled=True)


def split_grads(moved, widths, ways):
    rows = moved.shape[0]
    moved = moved.reshape(rows, ways, sum(widths))
    outs, begin = [], 0
    for width in widths:
        outs.append(moved[:, :, begin : begin + width].reshape(rows, ways * width).astype(f32))
        begin += width
    return outs


class Line:
    def __init__(self, ways):
        self.chips = ways // 2
        self.last = self.chips - 1
        self.me = lax.axis_index("seq")
        self.chip = self.me // 2
        self.core = self.me % 2
        self.sibling = self.me + 1 - 2 * self.core

    def greet(self, groups=1):
        barrier = pltpu.get_barrier_semaphore()
        group = lax.axis_index("dp")
        for off in range(1, groups):
            pl.semaphore_signal(
                barrier, inc=1, device_id={"dp": (group + off) % groups}, device_id_type=MESH
            )
        has_low = jnp.minimum(self.chip, 1)
        has_high = jnp.minimum(self.last - self.chip, 1)
        pl.semaphore_signal(barrier, inc=1, device_id={"seq": self.sibling}, device_id_type=MESH)

        @pl.when(self.chip > 0)
        def _():
            pl.semaphore_signal(barrier, inc=1, device_id={"seq": self.me - 2}, device_id_type=MESH)

        @pl.when(self.chip < self.last)
        def _():
            pl.semaphore_signal(barrier, inc=1, device_id={"seq": self.me + 2}, device_id_type=MESH)

        pl.semaphore_wait(barrier, groups + has_low + has_high)


def remote(src, dst, send_sem, recv_sem, device):
    return pltpu.make_async_remote_copy(
        src_ref=src,
        dst_ref=dst,
        send_sem=send_sem,
        recv_sem=recv_sem,
        device_id={"seq": device},
        device_id_type=MESH,
    )


def rows_at(index, count):
    return pl.ds(pl.multiple_of(index * count, count), count)


def each_strip(tok_count, strip, fn):
    def one(i, carry):
        fn(rows_at(i, strip))
        return carry

    lax.fori_loop(0, tok_count // strip, one, 0)


class RowGather:
    def __init__(self, line, half, buf, sems):
        self.line, self.half, self.buf = line, half, buf
        self.up_send, self.down_send, self.col_recv, self.sib_send, self.sib_recv = sems

    @staticmethod
    def scratch(chips):
        return [pltpu.SemaphoreType.DMA((2 * chips,))] * 5

    def piece(self, src, core, h):
        return self.buf.at[rows_at(h * 2 * self.line.chips + 2 * src + core, self.half)]

    def hop(self, src, h, device, send):
        piece, at = self.piece(src, self.line.core, h), h * self.line.chips + src
        return remote(piece, piece, send.at[at], self.col_recv.at[at], device)

    def swap(self, src, core, h):
        piece, at = self.piece(src, core, h), h * self.line.chips + src
        return remote(piece, piece, self.sib_send.at[at], self.sib_recv.at[at], self.line.sibling)

    def start(self, h):
        line = self.line
        self.forward_up(line.chip, h)
        self.forward_down(line.chip, h)
        self.swap(line.chip, line.core, h).start()

    def forward_up(self, src, h):
        @pl.when(self.line.chip < self.line.last)
        def _():
            self.hop(src, h, self.line.me + 2, self.up_send).start()

    def forward_down(self, src, h):
        @pl.when(self.line.chip > 0)
        def _():
            self.hop(src, h, self.line.me - 2, self.down_send).start()

    def receive(self, away, h):
        line = self.line
        low, high = line.chip - away, line.chip + away

        @pl.when(low >= 0)
        def _():
            self.hop(low, h, line.sibling, self.up_send).wait_recv()
            self.forward_up(low, h)
            self.swap(low, line.core, h).start()

        @pl.when(high <= line.last)
        def _():
            self.hop(high, h, line.sibling, self.down_send).wait_recv()
            self.forward_down(high, h)
            self.swap(high, line.core, h).start()

    def use_at(self, away, h, use):
        line = self.line
        low, high = line.chip - away, line.chip + away

        @pl.when(low >= 0)
        def _():
            self.swap(low, 1 - line.core, h).wait_recv()
            use(low, h)

        @pl.when((high <= line.last) & (away > 0))
        def _():
            self.swap(high, 1 - line.core, h).wait_recv()
            use(high, h)

    def finish(self):
        line = self.line
        for h in (0, 1):

            def one(src, carry, h=h):
                self.swap(src, line.core, h).wait_send()

                @pl.when((src <= line.chip) & (line.chip < line.last))
                def _():
                    self.hop(src, h, line.sibling, self.up_send).wait_send()

                @pl.when((src >= line.chip) & (line.chip > 0))
                def _():
                    self.hop(src, h, line.sibling, self.down_send).wait_send()

                return carry

            lax.fori_loop(0, line.chips, one, 0)


class RowScatter:
    def __init__(self, line, half, bufs, sems):
        self.line, self.half = line, half
        self.pair, self.sib_in, self.acc = bufs
        self.sib_send, self.sib_recv, self.send, self.recv = sems

    @staticmethod
    def scratch(chips, tok, width):
        return [
            pltpu.VMEM((2 * chips * tok, width), bf16),
            pltpu.VMEM((chips * tok, width), bf16),
            pltpu.VMEM(((chips + 1) * tok, width), bf16),
            pltpu.SemaphoreType.DMA((2 * chips,)),
            pltpu.SemaphoreType.DMA((2 * chips,)),
            pltpu.SemaphoreType.DMA((2 * chips,)),
            pltpu.SemaphoreType.DMA((2 * (chips + 1),)),
        ]

    def of(self, left, right, tile, joined):
        self.left, self.right, self.tile, self.joined = left, right, tile, joined
        return self

    def swap(self, dest, h):
        half, line = self.half, self.line
        at = h * line.chips + dest
        return remote(
            self.pair.at[rows_at(2 * at + 1 - line.core, half)],
            self.sib_in.at[rows_at(at, half)],
            self.sib_send.at[at],
            self.sib_recv.at[at],
            line.sibling,
        )

    def hop(self, dest, slot, h, device):
        half, slots = self.half, self.line.chips + 1
        return remote(
            self.acc.at[rows_at(h * slots + dest, half)],
            self.acc.at[rows_at(h * slots + slot, half)],
            self.send.at[h * self.line.chips + dest],
            self.recv.at[h * slots + slot],
            device,
        )

    def produce(self, dest, h):
        if self.joined and h:
            return
        spans = [rows_at(h * self.line.chips + dest, 2 * self.half)]
        if self.joined:
            spans.append(rows_at(self.line.chips + dest, 2 * self.half))

        def one(n, carry):
            cols = rows_at(n, self.tile)
            left = [self.left[span, :] for span in spans]
            left = jnp.concatenate(left, axis=0) if self.joined else left[0]
            part = dot_nt(left, self.right[cols, :]).astype(bf16)
            for i, span in enumerate(spans):
                self.pair[span, cols] = part[i * 2 * self.half : (i + 1) * 2 * self.half]
            return carry

        lax.fori_loop(0, self.right.shape[0] // self.tile, one, 0)
        for i in range(len(spans)):
            self.swap(dest, h + i).start()

    def strip_of(self, index, strip):
        return pl.ds(pl.multiple_of(index * self.half + strip.start, 16), strip.size)

    def chip_sum(self, dest, h, strip):
        at = h * self.line.chips + dest
        mine = self.pair[self.strip_of(2 * at + self.line.core, strip), :]
        other = self.sib_in[self.strip_of(at, strip), :]
        return mine.astype(f32) + other.astype(f32)

    def legs(self, s):
        line = self.line
        below, above = line.chip, line.last - line.chip
        return (
            (line.last - s + below, 1, below, (s >= below) & (s < line.last)),
            (s - above, -1, above, (s >= above) & (s < line.last)),
        )

    def make(self, s, h):
        for dest, _, _, there in self.legs(s):

            @pl.when(there)
            def _(dest=dest):
                self.produce(dest, h)

    def pass_on(self, s, h):
        line = self.line
        chips, slots = line.chips, line.chips + 1
        for dest, step, behind, there in self.legs(s):
            if step > 0:
                slot = dest
            else:
                ends = 1 - jnp.minimum(line.chip - 1 - dest, 1)
                slot = dest + ends * (chips - dest)

            @pl.when(there)
            def _(dest=dest, behind=behind, slot=slot, step=step):
                self.swap(dest, h).wait_recv()

                @pl.when(behind > 0)
                def _():
                    self.hop(dest, dest, h, line.sibling).wait_recv()

                    def add(strip):
                        at = self.strip_of(h * slots + dest, strip)
                        total = self.chip_sum(dest, h, strip) + self.acc[at, :].astype(f32)
                        self.acc[at, :] = total.astype(bf16)

                    each_strip(self.half, 16, add)

                @pl.when(behind == 0)
                def _():
                    def put(strip):
                        at = self.strip_of(h * slots + dest, strip)
                        self.acc[at, :] = self.chip_sum(dest, h, strip).astype(bf16)

                    each_strip(self.half, 16, put)

                self.hop(dest, slot, h, line.me + 2 * step).start()

    def close(self, h):
        line = self.line
        chips, slots = line.chips, line.chips + 1
        empty = jnp.zeros((self.half, self.acc.shape[1]), bf16)
        self.swap(line.chip, h).wait_recv()

        @pl.when(line.chip > 0)
        def _():
            self.hop(line.chip, line.chip, h, line.sibling).wait_recv()

        @pl.when(line.chip == 0)
        def _():
            self.acc[rows_at(h * slots + line.chip, self.half), :] = empty

        @pl.when(line.chip < line.last)
        def _():
            self.hop(line.chip, chips, h, line.sibling).wait_recv()

        @pl.when(line.chip == line.last)
        def _():
            self.acc[rows_at(h * slots + chips, self.half), :] = empty

    def total(self, h, strip):
        line = self.line
        slots = line.chips + 1
        low = self.acc[self.strip_of(h * slots + line.chip, strip), :].astype(f32)
        high = self.acc[self.strip_of(h * slots + line.chips, strip), :].astype(f32)
        return self.chip_sum(line.chip, h, strip) + (low + high)

    def finish(self, h):
        line = self.line

        def one(dest, carry):
            self.swap(dest, h).wait_send()

            @pl.when(line.chip != dest)
            def _():
                self.hop(dest, dest, h, line.sibling).wait_send()

            return carry

        lax.fori_loop(0, line.chips, one, 0)


def advance(scatter=None, sh=0, gather=None, gh=0, use=None):
    line = (scatter or gather).line
    if scatter:
        scatter.make(0, sh)

    def slot(s, carry):
        if gather:

            @pl.when(s > 0)
            def _():
                gather.receive(s, gh)

        if scatter:
            scatter.pass_on(s, sh)
            scatter.make(s + 1, sh)

            @pl.when(s == line.last - 1)
            def _():
                scatter.produce(line.chip, sh)

        if gather:

            @pl.when(s > 0)
            def _():
                gather.use_at(s - 1, gh, use)

        return carry

    lax.fori_loop(0, line.chips, slot, 0)


def mean_rows(values):
    return jnp.sum(values, axis=-1, keepdims=True) * (1.0 / values.shape[-1])


class Blocks:
    def __init__(self, line, count, pairs, sems):
        self.line, self.count, self.pairs, self.sems = line, count, pairs, sems

    def copy(self, i, index):
        src, dst = self.pairs[i]
        at = rows_at(index, self.count)
        return pltpu.make_async_copy(src.at[at], dst.at[at], self.sems.at[i, index])

    def send(self, i, chip, h):
        self.copy(i, h * self.line.chips + chip).start()

    def finish(self):
        def one(index, carry):
            for i in range(len(self.pairs)):
                self.copy(i, index).wait()
            return carry

        lax.fori_loop(0, 2 * self.line.chips, one, 0)


def call(kernel, outs, scratch, args, ident, cost=1, far_in=(), far_out=()):
    def space(i, far):
        return pl.BlockSpec(memory_space=pl.ANY if i in far else pltpu.VMEM)

    return pl.pallas_call(
        kernel,
        out_shape=outs,
        in_specs=[space(i, far_in) for i in range(len(args))],
        out_specs=[space(i, far_out) for i in range(len(outs))],
        scratch_shapes=scratch,
        cost_estimate=pl.CostEstimate(
            flops=cost * 10**9, transcendentals=0, bytes_accessed=cost * 3 * 10**6
        ),
        compiler_params=pltpu.CompilerParams(
            collective_id=ident, has_side_effects=True, vmem_limit_bytes=63 * 2**20
        ),
    )(*args)


def shape(dims, kind):
    return jax.ShapeDtypeStruct(dims, kind)


def gather_project(rows, codes, weights, ways, ident):
    tok, width = rows.shape
    cols = weights.shape[1] - HEAD_DIM
    half = tok // 2

    def kernel(
        rows_ref, code_ref, w_far, all_far, codes_ref, prod_far,
        w_ref, all_ref, prod_ref, w_sem, out_sem, code_send, code_recv, *sems
    ):
        line = Line(ways)
        w_copy = pltpu.make_async_copy(w_far.at[:, pl.ds(0, cols)], w_ref, w_sem)
        w_copy.start()
        outs = Blocks(line, 2 * half, [(all_ref, all_far), (prod_ref, prod_far)], out_sem)
        me = line.me
        barrier = pltpu.get_barrier_semaphore()
        for off in range(1, ways):
            pl.semaphore_signal(
                barrier, inc=1, device_id={"seq": (me + off) % ways}, device_id_type=MESH
            )
        pl.semaphore_wait(barrier, ways - 1)
        gather = RowGather(line, half, all_ref, sems)
        for h in (0, 1):
            all_ref[rows_at(h * ways + me, half), :] = rows_ref[pl.ds(h * half, half), :]
            gather.start(h)
        codes_ref[me] = code_ref[...]

        def tell(off):
            return remote(
                code_ref, codes_ref.at[me], code_send.at[off], code_recv.at[off], (me + off) % ways
            )

        for off in range(1, ways):
            tell(off).start()

        def use(chip, h):
            at = rows_at(h * line.chips + chip, 2 * half)

            prod_ref[at, :] = dot_nn(all_ref[at, :], w_ref[...])
            outs.send(0, chip, h)
            outs.send(1, chip, h)

        def step(j, carry):
            for h in (0, 1):
                gather.receive(j, h)
                gather.use_at(j - 1, h, use)
            return carry

        w_copy.wait()
        lax.fori_loop(1, line.chips, step, 0)
        for h in (0, 1):
            gather.use_at(line.last, h, use)
        gather.finish()
        outs.finish()
        for off in range(1, ways):
            tell(off).wait()

    return call(
        kernel,
        [
            shape((ways * tok, width), bf16),
            shape((ways,) + codes.shape, jnp.int32),
            shape((ways * tok, cols), f32),
        ],
        [
            pltpu.VMEM((width, cols), bf16),
            pltpu.VMEM((ways * tok, width), bf16),
            pltpu.VMEM((ways * tok, cols), f32),
            pltpu.SemaphoreType.DMA,
            pltpu.SemaphoreType.DMA((2, ways)),
            pltpu.SemaphoreType.DMA((ways,)),
            pltpu.SemaphoreType.DMA((ways,)),
        ]
        + RowGather.scratch(ways // 2),
        [rows, codes, weights],
        ident,
        55,
        (2,),
        (0, 2),
    )


def attn_out_and_ff(attn_low, m_mid, p_down, token_rows, grad_out, gains, groups, ways, ident):
    tok, width = token_rows.shape
    half = tok // 2
    own_feat, own_ff = attn_low.shape[1], p_down.shape[1]
    part = p_down.shape[0]
    row = ways * tok
    tile = min(own_ff, 1024)

    def kernel(
        left_far, mid_far, down_far, x_far, go_far, gains_ref,
        branch_far, out_ref, gg_ref, hid_far, mix_far, gm_far, dgu_far,
        left, mid_ref, down_ref, x_ref, go_ref, branch_ref, hid_ref, mix_ref, gm_ref, dgu_ref,
        in_sem, out_sem, branch_sem, down_send, down_recv, *rest
    ):
        line = Line(ways)
        group = lax.axis_index("dp")
        gu_cols, out_cols = pl.ds(0, 2 * own_ff), pl.ds(2 * own_ff, own_feat)
        fetch = [
            pltpu.make_async_copy(src, dst, in_sem.at[i])
            for i, (src, dst) in enumerate(
                [
                    (left_far, left),
                    (mid_far.at[:, out_cols], mid_ref.at[:, out_cols]),
                    (x_far, x_ref),
                    (mid_far.at[:, gu_cols], mid_ref.at[:, gu_cols]),
                    (down_far, down_ref.at[rows_at(group, part)]),
                    (go_far, go_ref),
                ]
            )
        ]
        for copy in fetch:
            copy.start()
        outs = Blocks(
            line,
            2 * half,
            [(hid_ref, hid_far), (mix_ref, mix_far), (gm_ref, gm_far), (dgu_ref, dgu_far)],
            out_sem,
        )
        keep_branch = pltpu.make_async_copy(branch_ref, branch_far, branch_sem)
        line.greet(groups)

        def spread(off):
            return pltpu.make_async_remote_copy(
                src_ref=down_far,
                dst_ref=down_ref.at[rows_at(group, part)],
                send_sem=down_send.at[off],
                recv_sem=down_recv.at[off],
                device_id={"dp": (group + off) % groups},
                device_id_type=MESH,
            )

        for off in range(1, groups):
            spread(off).start()
        scatter = RowScatter(line, half, rest[:3], rest[3:7])
        hidden = RowGather(line, half, hid_ref, rest[7:12])
        back = RowGather(line, half, gm_ref, rest[12:17])
        gg_ref[...] = jnp.zeros_like(gg_ref)
        gain_attn, gain_mlp = gains_ref[2:3, :], gains_ref[3:4, :]

        def own(h, strip):
            return pl.ds(pl.multiple_of((h * ways + line.me) * half + strip.start, 16), strip.size)

        def residual(at):
            branch = branch_ref[at, :]
            factor = lax.rsqrt(mean_rows(branch * branch) + norm_eps)
            return x_ref[at, :].astype(f32) + branch * factor * gain_attn

        def settle_attn(h):
            def one(strip):
                at = pl.ds(pl.multiple_of(h * half + strip.start, 16), strip.size)
                branch_ref[at, :] = scatter.total(h, strip)
                hid_ref[own(h, strip), :] = residual(at).astype(bf16)

            scatter.close(h)
            each_strip(half, 16, one)
            hidden.start(h)
            scatter.finish(h)

        def settle_mlp(h):
            def one(strip):
                at = pl.ds(pl.multiple_of(h * half + strip.start, 16), strip.size)
                mlp = scatter.total(h, strip)
                factor = lax.rsqrt(mean_rows(mlp * mlp) + norm_eps)
                unit = mlp * factor
                grad = go_ref[at, :].astype(f32)
                out_ref[at, :] = (residual(at) + unit * gain_mlp).astype(bf16)
                terms = grad * unit
                gg_ref[...] += terms[:8] + terms[8:]
                lifted = grad * gain_mlp
                turned = factor * (lifted - unit * mean_rows(lifted * unit))
                gm_ref[own(h, strip), :] = turned.astype(bf16)

            scatter.close(h)
            each_strip(half, 16, one)
            back.start(h)
            scatter.finish(h)

        def gate_up(chip, h):
            at = rows_at(h * line.chips + chip, 2 * half)

            outs.send(0, chip, h)

            def one(n, carry):
                here, there = rows_at(n, tile), pl.ds(pl.multiple_of(own_ff + n * tile, tile), tile)
                block = hid_ref[at, :]
                gate = dot_nn(block, mid_ref[:, here])
                up = dot_nn(block, mid_ref[:, there])
                dgu_ref[at, here] = gate.astype(bf16)
                dgu_ref[at, there] = up.astype(bf16)
                mix_ref[at, here] = (gate * jax.nn.sigmoid(gate) * up).astype(bf16)
                return carry

            lax.fori_loop(0, own_ff // tile, one, 0)
            outs.send(1, chip, h)

        def gate_up_back(chip, h):
            at = rows_at(h * line.chips + chip, 2 * half)

            outs.send(2, chip, h)

            def one(n, carry):
                here, there = rows_at(n, tile), pl.ds(pl.multiple_of(own_ff + n * tile, tile), tile)
                grad = dot_nn(gm_ref[at, :], down_ref[:, here])
                gate, up = dgu_ref[at, here].astype(f32), dgu_ref[at, there].astype(f32)
                sigma = jax.nn.sigmoid(gate)
                dgu_ref[at, here] = (grad * up * sigma * (1.0 + gate * (1.0 - sigma))).astype(bf16)
                dgu_ref[at, there] = (grad * gate * sigma).astype(bf16)
                return carry

            lax.fori_loop(0, own_ff // tile, one, 0)
            outs.send(3, chip, h)

        for copy in fetch[:3]:
            copy.wait()
        scatter.of(left, mid_ref.at[:, out_cols], 1024, True)
        advance(scatter, 0)
        fetch[3].wait()
        settle_attn(0)
        advance(scatter, 1, hidden, 0, gate_up)
        settle_attn(1)
        hidden.use_at(line.last, 0, gate_up)
        keep_branch.start()
        for copy in fetch[4:]:
            copy.wait()
        for off in range(1, groups):
            spread(off).wait()
        scatter.of(mix_ref, down_ref, 1024, False)
        advance(scatter, 0, hidden, 1, gate_up)
        settle_mlp(0)
        hidden.use_at(line.last, 1, gate_up)
        advance(scatter, 1, back, 0, gate_up_back)
        settle_mlp(1)
        back.use_at(line.last, 0, gate_up_back)
        advance(None, 0, back, 1, gate_up_back)
        back.use_at(line.last, 1, gate_up_back)
        hidden.finish()
        back.finish()
        keep_branch.wait()
        outs.finish()

    return call(
        kernel,
        [
            shape((tok, width), f32),
            shape((tok, width), bf16),
            shape((8, width), f32),
            shape((row, width), bf16),
            shape((row, own_ff), bf16),
            shape((row, width), bf16),
            shape((row, 2 * own_ff), bf16),
        ],
        [
            pltpu.VMEM((row, own_feat), bf16),
            pltpu.VMEM(m_mid.shape, bf16),
            pltpu.VMEM((groups * part, own_ff), bf16),
            pltpu.VMEM((tok, width), bf16),
            pltpu.VMEM((tok, width), bf16),
            pltpu.VMEM((tok, width), f32),
            pltpu.VMEM((row, width), bf16),
            pltpu.VMEM((row, own_ff), bf16),
            pltpu.VMEM((row, width), bf16),
            pltpu.VMEM((row, 2 * own_ff), bf16),
            pltpu.SemaphoreType.DMA((6,)),
            pltpu.SemaphoreType.DMA((4, ways)),
            pltpu.SemaphoreType.DMA,
            pltpu.SemaphoreType.DMA((groups,)),
            pltpu.SemaphoreType.DMA((groups,)),
        ]
        + RowScatter.scratch(ways // 2, tok, width)
        + RowGather.scratch(ways // 2)
        + RowGather.scratch(ways // 2),
        [attn_low, m_mid, p_down, token_rows, grad_out, gains],
        ident,
        150,
        range(5),
        (0, 3, 4, 5, 6),
    )


def ff_to_attn_back(grad_gu, m_mid, branch, grad_out, gain_row, ways, ident):
    tok, width = branch.shape
    half = tok // 2
    own_ff = grad_gu.shape[1] // 2
    own_feat = m_mid.shape[1] - 2 * own_ff
    row = ways * tok

    def kernel(
        left, w_ref, br_ref, go_ref, gain_ref, gh_ref, gg_ref, all_far, ga_ref,
        all_ref, out_sem, *rest
    ):
        line = Line(ways)
        outs = Blocks(line, 2 * half, [(all_ref, all_far)], out_sem)
        line.greet()
        scatter = RowScatter(line, half, rest[:3], rest[3:7])
        gather = RowGather(line, half, all_ref, rest[7:])
        gg_ref[...] = jnp.zeros_like(gg_ref)

        def settle(h):
            def one(strip):
                at = pl.ds(pl.multiple_of(h * half + strip.start, 16), strip.size)
                mine = pl.ds(
                    pl.multiple_of((h * ways + line.me) * half + strip.start, 16), strip.size
                )
                grad = scatter.total(h, strip) + go_ref[at, :].astype(f32)
                branch = br_ref[at, :]
                factor = lax.rsqrt(mean_rows(branch * branch) + norm_eps)
                unit = branch * factor
                gh_ref[at, :] = grad
                terms = grad * unit
                gg_ref[...] += terms[:8] + terms[8:]
                lifted = grad * gain_ref[...]
                turned = factor * (lifted - unit * mean_rows(lifted * unit))
                all_ref[mine, :] = turned.astype(bf16)

            scatter.close(h)
            each_strip(half, 16, one)
            gather.start(h)

        def use(chip, h):
            at = rows_at(h * line.chips + chip, 2 * half)
            outs.send(0, chip, h)
            ga_ref[at, :] = dot_nn(all_ref[at, :], w_ref[:, pl.ds(2 * own_ff, own_feat)])

        scatter.of(left, w_ref.at[:, pl.ds(0, 2 * own_ff)], 512, True)
        advance(scatter, 0)
        settle(0)
        advance(scatter, 1, gather, 0, use)
        settle(1)
        gather.use_at(line.last, 0, use)
        advance(None, 0, gather, 1, use)
        gather.use_at(line.last, 1, use)
        gather.finish()
        outs.finish()
        for h in (0, 1):
            scatter.finish(h)

    return call(
        kernel,
        [
            shape((tok, width), f32),
            shape((8, width), f32),
            shape((row, width), bf16),
            shape((row, own_feat), f32),
        ],
        [pltpu.VMEM((row, width), bf16), pltpu.SemaphoreType.DMA((1, ways))]
        + RowScatter.scratch(ways // 2, tok, width)
        + RowGather.scratch(ways // 2),
        [grad_gu, m_mid, branch, grad_out, gain_row],
        ident,
        100,
        (),
        (2,),
    )


def project_back(grad_qkv, m_qkv, grad_hidden, ways, ident):
    tok, width = grad_hidden.shape
    half = tok // 2

    def kernel(left, w_ref, gh_ref, out_ref, *rest):
        line = Line(ways)
        line.greet()
        scatter = RowScatter(line, half, rest[:3], rest[3:7])
        scatter.of(left, w_ref.at[:, pl.ds(0, left.shape[1])], 1024, True)
        for h in (0, 1):
            advance(scatter, h)
        for h in (0, 1):

            def one(strip, h=h):
                at = pl.ds(pl.multiple_of(h * half + strip.start, 16), strip.size)
                out_ref[at, :] = (gh_ref[at, :] + scatter.total(h, strip)).astype(bf16)

            scatter.close(h)
            each_strip(half, 16, one)
        for h in (0, 1):
            scatter.finish(h)

    return call(
        kernel,
        [shape((tok, width), bf16)],
        RowScatter.scratch(ways // 2, tok, width),
        [grad_qkv, m_qkv, grad_hidden],
        ident,
        55,
    )[0]


def exchange(sources, ways, ident, cost):
    rows = sources[0].shape[0]
    widths = [a.shape[1] // ways for a in sources]
    begins = [sum(widths[:i]) for i in range(len(widths))]
    count = len(sources)

    def kernel(*refs):
        ins, out_ref, send, recv, local = refs[:count], *refs[count:]
        me = lax.axis_index("seq")
        barrier = pltpu.get_barrier_semaphore()

        def greet(off, carry):
            pl.semaphore_signal(
                barrier, inc=1, device_id={"seq": (me + off) % ways}, device_id_type=MESH
            )
            return carry

        def move(off, i):
            dest = (me + off) % ways
            return remote(
                ins[i].at[:, rows_at(dest, widths[i])],
                out_ref.at[rows_at(me, rows), pl.ds(begins[i], widths[i])],
                send.at[off * count + i],
                recv.at[off * count + i],
                dest,
            )

        def keep(i):
            return pltpu.make_async_copy(
                ins[i].at[:, rows_at(me, widths[i])],
                out_ref.at[rows_at(me, rows), pl.ds(begins[i], widths[i])],
                local.at[i],
            )

        def each(what):
            def one(off, carry):
                for i in range(count):
                    what(move(off, i))
                return carry

            lax.fori_loop(1, ways, one, 0)

        for i in range(count):
            keep(i).start()
        lax.fori_loop(1, ways, greet, 0)
        pl.semaphore_wait(barrier, ways - 1)
        each(lambda copy: copy.start())
        for i in range(count):
            keep(i).wait()
        each(lambda copy: copy.wait())

    return pl.pallas_call(
        kernel,
        out_shape=shape((ways * rows, sum(widths)), bf16),
        in_specs=[pl.BlockSpec(memory_space=pl.ANY)] * count,
        out_specs=pl.BlockSpec(memory_space=pl.ANY),
        scratch_shapes=[
            pltpu.SemaphoreType.DMA((ways * count,)),
            pltpu.SemaphoreType.DMA((ways * count,)),
            pltpu.SemaphoreType.DMA((count,)),
        ],
        cost_estimate=pl.CostEstimate(
            flops=cost * 10**9, transcendentals=0, bytes_accessed=cost * 3 * 10**6
        ),
        compiler_params=pltpu.CompilerParams(collective_id=ident, has_side_effects=True),
    )(*sources)


def line_sum(terms, ways, ident):
    def kernel(terms_ref, out_ref, slots, send, recv):
        me = lax.axis_index("seq")
        barrier = pltpu.get_barrier_semaphore()
        for off in range(1, ways):
            pl.semaphore_signal(
                barrier, inc=1, device_id={"seq": (me + off) % ways}, device_id_type=MESH
            )
        pl.semaphore_wait(barrier, ways - 1)
        for off in range(1, ways):
            remote(
                terms_ref, slots.at[off], send.at[off], recv.at[off], (me + off) % ways
            ).start()
        total = terms_ref[...]
        for off in range(1, ways):
            remote(terms_ref, slots.at[off], send.at[off], recv.at[off], (me + off) % ways).wait_recv()
            total = total + slots[off]
        out_ref[...] = total
        for off in range(1, ways):
            remote(terms_ref, slots.at[off], send.at[off], recv.at[off], (me + off) % ways).wait_send()

    return call(
        kernel,
        [shape(terms.shape, f32)],
        [
            pltpu.VMEM((ways,) + terms.shape, f32),
            pltpu.SemaphoreType.DMA((ways,)),
            pltpu.SemaphoreType.DMA((ways,)),
        ],
        [terms],
        ident,
        8,
    )[0]


def body(
    tokens,
    w_query,
    w_key,
    w_value,
    w_out,
    w_gate,
    w_up,
    w_down,
    gain_query,
    gain_key,
    gain_attn,
    gain_mlp,
    cotangent,
    key_mask,
    lengths,
    tract_order,
):
    ways, groups = lax.axis_size("seq"), lax.axis_size("dp")
    me = lax.axis_index("seq")
    token_rows = tokens[0]
    tok_count, feat_width = token_rows.shape
    ff_width = w_gate.shape[1]
    own_feat = feat_width // ways
    own_heads = own_feat // HEAD_DIM
    own_ff = ff_width // ways
    row_len = tok_count * ways
    score_scale = HEAD_DIM ** (-0.5)
    half_len = tok_count // 2
    order_pair = tract_order[0]
    slot_index = jnp.arange(tok_count, dtype=jnp.int32)
    local_pos = (
        jnp.where(slot_index < half_len, order_pair[0], order_pair[1]) * half_len
        + slot_index % half_len
    )
    key_ok = ((key_mask[0] == 1) & (local_pos < lengths[0])).astype(jnp.int32)

    gain_local = jnp.stack([gain_query, gain_key, gain_attn, gain_mlp], axis=1)
    gain_pad = jnp.pad(gain_local, ((0, 0), (0, HEAD_DIM - 4)))
    gain_all = jnp.tile(gain_pad, (1, ways))
    p_qkv = exchange([w_query, w_key, w_value, gain_all], ways, 8, 20)
    m_qkv = across(p_qkv)
    p_qkv, w_gate, w_up, w_out_t = lax.optimization_barrier(
        (p_qkv, w_gate, w_up, jnp.transpose(w_out))
    )
    p_mid = exchange([w_gate, w_up, w_out_t], ways, 10, 50)
    m_mid = across(p_mid)
    gains = dot_nt(jnp.eye(8, HEAD_DIM, dtype=bf16), m_qkv[:, 3 * own_feat :])
    gain_q = lax.dynamic_slice_in_dim(gains[0], me * own_feat, own_feat, 0)
    gain_k = lax.dynamic_slice_in_dim(gains[1], me * own_feat, own_feat, 0)

    code_pad = -tok_count % HEAD_DIM
    local_code = jnp.pad(local_pos * 2 + key_ok, (0, code_pad))[None]
    local_code, p_mid = lax.optimization_barrier((local_code, p_mid))
    x_row, codes, qkv = gather_project(token_rows, local_code, m_qkv, ways, 1)
    key_code = codes[:, 0, :tok_count].reshape(ways, 2, half_len)
    key_code = jnp.transpose(key_code, (1, 0, 2)).reshape(row_len)
    pos = key_code // 2
    q_raw, k_raw, v_raw = (qkv[:, i * own_feat : (i + 1) * own_feat] for i in range(3))
    squares = line_sum(
        jnp.stack([jnp.sum(q_raw * q_raw, axis=-1), jnp.sum(k_raw * k_raw, axis=-1)]), ways, 2
    )
    squares, w_down_t = lax.optimization_barrier((squares, jnp.transpose(w_down)))
    p_down = lax.all_to_all(w_down_t, "seq", split_axis=1, concat_axis=0, tiled=True)
    factors = lax.rsqrt(squares / feat_width + norm_eps)
    q_factor, k_factor = factors[0][:, None], factors[1][:, None]
    cosine, sine = rope_tables(pos, HEAD_DIM)
    head_shape = (row_len, own_heads, HEAD_DIM)
    query_low = rotate((q_raw * q_factor * gain_q).reshape(head_shape), cosine, sine).astype(bf16)
    key_low = rotate((k_raw * k_factor * gain_k).reshape(head_shape), cosine, sine).astype(bf16)
    value_low = v_raw.astype(bf16).reshape(head_shape)

    mask = allowed_mask(pos, key_code)[None]
    scores = jnp.einsum("qhd,khd->hqk", query_low, key_low, preferred_element_type=f32) * score_scale
    expo = jnp.where(mask, jnp.exp(scores), 0.0)
    weight_sum = jnp.transpose(jnp.sum(expo, axis=-1))[:, :, None]
    expo_low = expo.astype(bf16)
    attn = jnp.einsum("hqk,khd->qhd", expo_low, value_low, preferred_element_type=f32) / weight_sum
    attn_low = attn.astype(bf16).reshape(row_len, own_feat)

    branch, layer_out, grad_gain_mlp, hidden_low, mixed_low, grad_mlp, grad_gu = attn_out_and_ff(
        attn_low, m_mid, p_down, token_rows, cotangent[0], gains, groups, ways, 3
    )
    d_down = dot_tn(grad_mlp, mixed_low).astype(bf16)
    d_gu = dot_tn(hidden_low, grad_gu).astype(bf16)
    grad_gu, d_down, d_gu = lax.optimization_barrier((grad_gu, d_down, d_gu))
    d_gu = dp_sum(d_gu)
    d_down = dp_sum(d_down)
    grad_hidden, grad_gain_attn, grad_branch, grad_attn = ff_to_attn_back(
        grad_gu, m_mid, branch, cotangent[0], gains[2:3], ways, 5
    )
    grad_attn, d_gu = lax.optimization_barrier((grad_attn, d_gu))
    d_gu = send_home(d_gu, ways)
    grad_attn = grad_attn.reshape(head_shape)
    grad_num = (grad_attn / weight_sum).astype(bf16)
    drop = jnp.transpose(jnp.sum(grad_attn * attn, axis=-1) / weight_sum[:, :, 0])
    grad_expo = jnp.einsum("qhd,khd->hqk", grad_num, value_low, preferred_element_type=f32)
    grad_scores = (expo * (grad_expo - drop[:, :, None])).astype(bf16)
    grad_q = (
        jnp.einsum("hqk,khd->qhd", grad_scores, key_low, preferred_element_type=f32) * score_scale
    )
    grad_k = (
        jnp.einsum("hqk,qhd->khd", grad_scores, query_low, preferred_element_type=f32) * score_scale
    )
    grad_v = jnp.einsum("hqk,qhd->khd", expo_low, grad_num, preferred_element_type=f32)
    grad_q_norm = unrotate(grad_q, cosine, sine).reshape(row_len, own_feat)
    grad_k_norm = unrotate(grad_k, cosine, sine).reshape(row_len, own_feat)
    q_unit, k_unit = q_raw * q_factor, k_raw * k_factor
    grad_gain_query = jnp.sum(grad_q_norm * q_unit, axis=0)
    grad_gain_key = jnp.sum(grad_k_norm * k_unit, axis=0)
    c_q, c_k = grad_q_norm * gain_q, grad_k_norm * gain_k
    terms = jnp.stack([jnp.sum(c_q * q_unit, axis=-1), jnp.sum(c_k * k_unit, axis=-1)])
    terms, d_down, d_gu = lax.optimization_barrier((terms, d_down, d_gu))
    means = line_sum(terms, ways, 6) / feat_width
    d_down = send_home(d_down, ways)
    dw_gu = split_grads(d_gu, [own_ff, own_ff], ways)
    grad_q_raw = q_factor * (c_q - q_unit * means[0][:, None])
    grad_k_raw = k_factor * (c_k - k_unit * means[1][:, None])
    grad_qkv = jnp.concatenate(
        [grad_q_raw, grad_k_raw, grad_v.reshape(row_len, own_feat)], axis=1
    ).astype(bf16)

    own_slot = jnp.zeros((2, feat_width), f32)
    own_slot = lax.dynamic_update_slice(
        own_slot, jnp.stack([grad_gain_query, grad_gain_key]), (0, me * own_feat)
    )
    gain_terms = jnp.concatenate(
        [
            own_slot,
            jnp.sum(grad_gain_attn, axis=0, keepdims=True),
            jnp.sum(grad_gain_mlp, axis=0, keepdims=True),
        ]
    )
    gain_columns = jnp.pad(jnp.transpose(gain_terms), ((0, 0), (0, HEAD_DIM - 4)))
    d_attn = jnp.concatenate(
        [dot_tn(x_row, grad_qkv), dot_tn(grad_branch, attn_low), gain_columns], axis=1
    ).astype(bf16)
    grad_qkv, d_attn, d_down = lax.optimization_barrier((grad_qkv, d_attn, d_down))
    dw_down = split_grads(d_down, [own_ff], ways)
    grad_tokens = project_back(grad_qkv, m_qkv, grad_hidden, ways, 7)
    grad_tokens, d_attn = lax.optimization_barrier((grad_tokens, dp_sum(d_attn)))
    dw_qkv = split_grads(send_home(d_attn, ways), [own_feat] * 4 + [HEAD_DIM], ways)
    gain_grads = jnp.sum(dw_qkv[4].reshape(-1, ways, HEAD_DIM), axis=1)
    gain_grads = jnp.transpose(gain_grads[:, :8])
    return (
        layer_out[None],
        grad_tokens[None],
        dw_qkv[0],
        dw_qkv[1],
        dw_qkv[2],
        jnp.transpose(dw_qkv[3]),
        dw_gu[0],
        dw_gu[1],
        jnp.transpose(dw_down[0]),
        gain_grads[0],
        gain_grads[1],
        gain_grads[2],
        gain_grads[3],
    )


def solution(mesh):
    both = ("dp", "seq")
    in_specs = (
        P("dp", "seq", None),
        P(both, None),
        P(both, None),
        P(both, None),
        P(None, both),
        P(both, None),
        P(both, None),
        P(None, both),
        P(both),
        P(both),
        P(both),
        P(both),
        P("dp", "seq", None),
        P("dp", "seq"),
        P("dp"),
        P("dp", "seq"),
    )
    out_specs = (
        P("dp", "seq", None),
        P("dp", "seq", None),
        P(both, None),
        P(both, None),
        P(both, None),
        P(None, both),
        P(both, None),
        P(both, None),
        P(None, both),
        P(both),
        P(both),
        P(both),
        P(both),
    )
    return jax.shard_map(body, mesh=mesh, in_specs=in_specs, out_specs=out_specs, check_vma=False)
```

```python
import functools

import jax
import jax.numpy as jnp
from jax import lax
from jax.experimental import pallas as pl
from jax.experimental.pallas import tpu as pltpu
from jax.sharding import PartitionSpec as P

MESH = pl.DeviceIdType.MESH

HEAD_DIM = 128

rope_base = 500000.0
norm_eps = 1e-06
LOG2_E = 1.4426950408889634
f32 = jnp.float32
bf16 = jnp.bfloat16


def rms_factor(values):
    return lax.rsqrt(jnp.mean(values * values, axis=-1, keepdims=True) + norm_eps)


def norm_back(grad_normed, raw_values, factor):
    unit_values = raw_values * factor
    return factor * (
        grad_normed - unit_values * jnp.mean(grad_normed * unit_values, axis=-1, keepdims=True)
    )


def rope_tables(positions, head_dim):
    half_dim = head_dim // 2
    steps_f = jnp.arange(half_dim).astype(f32) * (2.0 / head_dim)
    inv_freq = jnp.power(rope_base, -steps_f)
    angle = positions.astype(f32)[:, None] * inv_freq[None, :]
    angle = jnp.concatenate([angle, angle], axis=-1)
    return (jnp.cos(angle), jnp.sin(angle))


def rotate(values, cosine, sine):
    half_dim = values.shape[-1] // 2
    turned = jnp.concatenate([-values[..., half_dim:], values[..., :half_dim]], axis=-1)
    return values * cosine + turned * sine


def unrotate(grads, cosine, sine):
    half_dim = grads.shape[-1] // 2
    moved = grads * sine
    back_part = jnp.concatenate([moved[..., half_dim:], -moved[..., :half_dim]], axis=-1)
    return grads * cosine + back_part


def allowed_mask(query_pos, key_code):
    key_pos = key_code // 2
    usable = key_code % 2 == 1
    causal = key_pos[None, :] <= query_pos[:, None]
    return causal & (usable[None, :] | (key_pos[None, :] == query_pos[:, None]))


def dot_nn(left, right):
    return jnp.dot(left, right, preferred_element_type=f32)


def dot_nt(left, right):
    return lax.dot_general(left, right, (((1,), (1,)), ((), ())), preferred_element_type=f32)


def dot_tn(left, right):
    return lax.dot_general(left, right, (((0,), (0,)), ((), ())), preferred_element_type=f32)


def across(piece):
    return lax.all_gather(piece, "dp", axis=0, tiled=True)


def dp_sum(grad):
    return lax.psum_scatter(grad, "dp", scatter_dimension=0, tiled=True)


class Line:
    def __init__(self, ways):
        self.chips = ways // 2
        self.last = self.chips - 1
        self.me = lax.axis_index("seq")
        self.chip = self.me // 2
        self.core = self.me % 2
        self.sibling = self.me + 1 - 2 * self.core

    def greet(self, groups=1):
        barrier = pltpu.get_barrier_semaphore()
        group = lax.axis_index("dp")
        for off in range(1, groups):
            pl.semaphore_signal(
                barrier, inc=1, device_id={"dp": (group + off) % groups}, device_id_type=MESH
            )
        has_low = jnp.minimum(self.chip, 1)
        has_high = jnp.minimum(self.last - self.chip, 1)
        pl.semaphore_signal(barrier, inc=1, device_id={"seq": self.sibling}, device_id_type=MESH)

        @pl.when(self.chip > 0)
        def _():
            pl.semaphore_signal(barrier, inc=1, device_id={"seq": self.me - 2}, device_id_type=MESH)

        @pl.when(self.chip < self.last)
        def _():
            pl.semaphore_signal(barrier, inc=1, device_id={"seq": self.me + 2}, device_id_type=MESH)

        pl.semaphore_wait(barrier, groups + has_low + has_high)


def remote(src, dst, send_sem, recv_sem, device):
    return pltpu.make_async_remote_copy(
        src_ref=src,
        dst_ref=dst,
        send_sem=send_sem,
        recv_sem=recv_sem,
        device_id={"seq": device},
        device_id_type=MESH,
    )


def rows_at(index, count):
    return pl.ds(pl.multiple_of(index * count, count), count)


def each_strip(tok_count, strip, fn):
    def one(i, carry):
        fn(rows_at(i, strip))
        return carry

    lax.fori_loop(0, tok_count // strip, one, 0)


class RowGather:
    def __init__(self, line, half, buf, sems):
        self.line, self.half, self.buf = line, half, buf
        self.up_send, self.down_send, self.col_recv, self.sib_send, self.sib_recv = sems

    @staticmethod
    def scratch(chips):
        return [pltpu.SemaphoreType.DMA((2 * chips,))] * 5

    def piece(self, src, core, h):
        return self.buf.at[rows_at(h * 2 * self.line.chips + 2 * src + core, self.half)]

    def hop(self, src, h, device, send):
        piece, at = self.piece(src, self.line.core, h), h * self.line.chips + src
        return remote(piece, piece, send.at[at], self.col_recv.at[at], device)

    def swap(self, src, core, h):
        piece, at = self.piece(src, core, h), h * self.line.chips + src
        return remote(piece, piece, self.sib_send.at[at], self.sib_recv.at[at], self.line.sibling)

    def start(self, h):
        line = self.line
        self.forward_up(line.chip, h)
        self.forward_down(line.chip, h)
        self.swap(line.chip, line.core, h).start()

    def forward_up(self, src, h):
        @pl.when(self.line.chip < self.line.last)
        def _():
            self.hop(src, h, self.line.me + 2, self.up_send).start()

    def forward_down(self, src, h):
        @pl.when(self.line.chip > 0)
        def _():
            self.hop(src, h, self.line.me - 2, self.down_send).start()

    def receive(self, away, h):
        line = self.line
        low, high = line.chip - away, line.chip + away

        @pl.when(low >= 0)
        def _():
            self.hop(low, h, line.sibling, self.up_send).wait_recv()
            self.forward_up(low, h)
            self.swap(low, line.core, h).start()

        @pl.when(high <= line.last)
        def _():
            self.hop(high, h, line.sibling, self.down_send).wait_recv()
            self.forward_down(high, h)
            self.swap(high, line.core, h).start()

    def use_at(self, away, h, use):
        line = self.line
        low, high = line.chip - away, line.chip + away

        @pl.when(low >= 0)
        def _():
            self.swap(low, 1 - line.core, h).wait_recv()
            use(low, h)

        @pl.when((high <= line.last) & (away > 0))
        def _():
            self.swap(high, 1 - line.core, h).wait_recv()
            use(high, h)

    def finish(self):
        line = self.line
        for h in (0, 1):

            def one(src, carry, h=h):
                self.swap(src, line.core, h).wait_send()

                @pl.when((src <= line.chip) & (line.chip < line.last))
                def _():
                    self.hop(src, h, line.sibling, self.up_send).wait_send()

                @pl.when((src >= line.chip) & (line.chip > 0))
                def _():
                    self.hop(src, h, line.sibling, self.down_send).wait_send()

                return carry

            lax.fori_loop(0, line.chips, one, 0)


class RowScatter:
    def __init__(self, line, half, bufs, sems):
        self.line, self.half = line, half
        self.pair, self.sib_in, self.acc = bufs
        self.sib_send, self.sib_recv, self.send, self.recv = sems

    @staticmethod
    def scratch(chips, tok, width):
        return [
            pltpu.VMEM((2 * chips * tok, width), bf16),
            pltpu.VMEM((chips * tok, width), bf16),
            pltpu.VMEM(((chips + 1) * tok, width), bf16),
            pltpu.SemaphoreType.DMA((2 * chips,)),
            pltpu.SemaphoreType.DMA((2 * chips,)),
            pltpu.SemaphoreType.DMA((2 * chips,)),
            pltpu.SemaphoreType.DMA((2 * (chips + 1),)),
        ]

    def of(self, left, right, tile, joined, turned=False):
        self.left, self.right, self.tile = left, right, tile
        self.joined, self.turned = joined, turned
        return self

    def swap(self, dest, h):
        half, line = self.half, self.line
        at = h * line.chips + dest
        return remote(
            self.pair.at[rows_at(2 * at + 1 - line.core, half)],
            self.sib_in.at[rows_at(at, half)],
            self.sib_send.at[at],
            self.sib_recv.at[at],
            line.sibling,
        )

    def hop(self, dest, slot, h, device):
        half, slots = self.half, self.line.chips + 1
        return remote(
            self.acc.at[rows_at(h * slots + dest, half)],
            self.acc.at[rows_at(h * slots + slot, half)],
            self.send.at[h * self.line.chips + dest],
            self.recv.at[h * slots + slot],
            device,
        )

    def produce(self, dest, h):
        if self.joined and h:
            return
        spans = [rows_at(h * self.line.chips + dest, 2 * self.half)]
        if self.joined:
            spans.append(rows_at(self.line.chips + dest, 2 * self.half))

        def one(n, carry):
            cols = rows_at(n, self.tile)
            left = [self.left[span, :] for span in spans]
            left = jnp.concatenate(left, axis=0) if self.joined else left[0]
            if self.turned:
                part = dot_nn(left, self.right[:, cols]).astype(bf16)
            else:
                part = dot_nt(left, self.right[cols, :]).astype(bf16)
            for i, span in enumerate(spans):
                self.pair[span, cols] = part[i * 2 * self.half : (i + 1) * 2 * self.half]
            return carry

        lax.fori_loop(0, self.right.shape[1 if self.turned else 0] // self.tile, one, 0)
        for i in range(len(spans)):
            self.swap(dest, h + i).start()

    def strip_of(self, index, strip):
        return pl.ds(pl.multiple_of(index * self.half + strip.start, 16), strip.size)

    def chip_sum(self, dest, h, strip):
        at = h * self.line.chips + dest
        mine = self.pair[self.strip_of(2 * at + self.line.core, strip), :]
        other = self.sib_in[self.strip_of(at, strip), :]
        return mine.astype(f32) + other.astype(f32)

    def legs(self, s):
        line = self.line
        below, above = line.chip, line.last - line.chip
        return (
            (line.last - s + below, 1, below, (s >= below) & (s < line.last)),
            (s - above, -1, above, (s >= above) & (s < line.last)),
        )

    def make(self, s, h):
        for dest, _, _, there in self.legs(s):

            @pl.when(there)
            def _(dest=dest):
                self.produce(dest, h)

    def pass_on(self, s, h):
        line = self.line
        chips, slots = line.chips, line.chips + 1
        for dest, step, behind, there in self.legs(s):
            if step > 0:
                slot = dest
            else:
                ends = 1 - jnp.minimum(line.chip - 1 - dest, 1)
                slot = dest + ends * (chips - dest)

            @pl.when(there)
            def _(dest=dest, behind=behind, slot=slot, step=step):
                self.swap(dest, h).wait_recv()

                @pl.when(behind > 0)
                def _():
                    self.hop(dest, dest, h, line.sibling).wait_recv()

                    def add(strip):
                        at = self.strip_of(h * slots + dest, strip)
                        total = self.chip_sum(dest, h, strip) + self.acc[at, :].astype(f32)
                        self.acc[at, :] = total.astype(bf16)

                    each_strip(self.half, 16, add)

                @pl.when(behind == 0)
                def _():
                    def put(strip):
                        at = self.strip_of(h * slots + dest, strip)
                        self.acc[at, :] = self.chip_sum(dest, h, strip).astype(bf16)

                    each_strip(self.half, 16, put)

                self.hop(dest, slot, h, line.me + 2 * step).start()

    def close(self, h):
        line = self.line
        chips, slots = line.chips, line.chips + 1
        empty = jnp.zeros((self.half, self.acc.shape[1]), bf16)
        self.swap(line.chip, h).wait_recv()

        @pl.when(line.chip > 0)
        def _():
            self.hop(line.chip, line.chip, h, line.sibling).wait_recv()

        @pl.when(line.chip == 0)
        def _():
            self.acc[rows_at(h * slots + line.chip, self.half), :] = empty

        @pl.when(line.chip < line.last)
        def _():
            self.hop(line.chip, chips, h, line.sibling).wait_recv()

        @pl.when(line.chip == line.last)
        def _():
            self.acc[rows_at(h * slots + chips, self.half), :] = empty

    def total(self, h, strip):
        line = self.line
        slots = line.chips + 1
        low = self.acc[self.strip_of(h * slots + line.chip, strip), :].astype(f32)
        high = self.acc[self.strip_of(h * slots + line.chips, strip), :].astype(f32)
        return self.chip_sum(line.chip, h, strip) + (low + high)

    def finish(self, h):
        line = self.line

        def one(dest, carry):
            self.swap(dest, h).wait_send()

            @pl.when(line.chip != dest)
            def _():
                self.hop(dest, dest, h, line.sibling).wait_send()

            return carry

        lax.fori_loop(0, line.chips, one, 0)


def advance(scatter=None, sh=0, gather=None, gh=0, use=None, fill=None):
    line = (scatter or gather).line
    if scatter:
        scatter.make(0, sh)

    def slot(s, carry):
        if gather:

            @pl.when(s > 0)
            def _():
                gather.receive(s, gh)

        if scatter:
            scatter.pass_on(s, sh)
            scatter.make(s + 1, sh)

            @pl.when(s == line.last - 1)
            def _():
                scatter.produce(line.chip, sh)

        if gather:

            @pl.when(s > 0)
            def _():
                gather.use_at(s - 1, gh, use)

        if fill:
            fill(s)
        return carry

    lax.fori_loop(0, line.chips, slot, 0)


def mean_rows(values):
    return jnp.sum(values, axis=-1, keepdims=True) * (1.0 / values.shape[-1])


class Blocks:
    def __init__(self, line, count, pairs, sems):
        self.line, self.count, self.pairs, self.sems = line, count, pairs, sems

    def copy(self, i, index):
        src, dst = self.pairs[i]
        at = rows_at(index, self.count)
        return pltpu.make_async_copy(src.at[at], dst.at[at], self.sems.at[i, index])

    def send(self, i, chip, h):
        self.copy(i, h * self.line.chips + chip).start()

    def finish(self):
        def one(index, carry):
            for i in range(len(self.pairs)):
                self.copy(i, index).wait()
            return carry

        lax.fori_loop(0, 2 * self.line.chips, one, 0)


def call(kernel, outs, scratch, args, ident, cost=1, far_in=(), far_out=()):
    def space(i, far):
        return pl.BlockSpec(memory_space=pl.ANY if i in far else pltpu.VMEM)

    return pl.pallas_call(
        kernel,
        out_shape=outs,
        in_specs=[space(i, far_in) for i in range(len(args))],
        out_specs=[space(i, far_out) for i in range(len(outs))],
        scratch_shapes=scratch,
        cost_estimate=pl.CostEstimate(
            flops=cost * 10**9, transcendentals=0, bytes_accessed=cost * 3 * 10**6
        ),
        compiler_params=pltpu.CompilerParams(
            collective_id=ident, has_side_effects=True, vmem_limit_bytes=63 * 2**20
        ),
    )(*args)


def shape(dims, kind):
    return jax.ShapeDtypeStruct(dims, kind)


def gather_project(rows, codes, weights, ways, ident):
    tok, width = rows.shape
    cols = weights.shape[1] - HEAD_DIM
    half = tok // 2

    def kernel(
        rows_ref, code_ref, w_far, all_far, codes_ref, prod_far,
        w_ref, all_ref, prod_ref, w_sem, out_sem, code_send, code_recv, *sems
    ):
        line = Line(ways)
        w_copy = pltpu.make_async_copy(w_far.at[:, pl.ds(0, cols)], w_ref, w_sem)
        w_copy.start()
        outs = Blocks(line, 2 * half, [(all_ref, all_far), (prod_ref, prod_far)], out_sem)
        me = line.me
        barrier = pltpu.get_barrier_semaphore()
        for off in range(1, ways):
            pl.semaphore_signal(
                barrier, inc=1, device_id={"seq": (me + off) % ways}, device_id_type=MESH
            )
        pl.semaphore_wait(barrier, ways - 1)
        gather = RowGather(line, half, all_ref, sems)
        for h in (0, 1):
            all_ref[rows_at(h * ways + me, half), :] = rows_ref[pl.ds(h * half, half), :]
            gather.start(h)
        codes_ref[me] = code_ref[...]

        def tell(off):
            return remote(
                code_ref, codes_ref.at[me], code_send.at[off], code_recv.at[off], (me + off) % ways
            )

        for off in range(1, ways):
            tell(off).start()

        def use(chip, h):
            at = rows_at(h * line.chips + chip, 2 * half)

            prod_ref[at, :] = dot_nn(all_ref[at, :], w_ref[...])
            outs.send(0, chip, h)
            outs.send(1, chip, h)

        def step(j, carry):
            for h in (0, 1):
                gather.receive(j, h)
                gather.use_at(j - 1, h, use)
            return carry

        w_copy.wait()
        lax.fori_loop(1, line.chips, step, 0)
        for h in (0, 1):
            gather.use_at(line.last, h, use)
        gather.finish()
        outs.finish()
        for off in range(1, ways):
            tell(off).wait()

    return call(
        kernel,
        [
            shape((ways * tok, width), bf16),
            shape((ways,) + codes.shape, jnp.int32),
            shape((ways * tok, cols), f32),
        ],
        [
            pltpu.VMEM((width, cols), bf16),
            pltpu.VMEM((ways * tok, width), bf16),
            pltpu.VMEM((ways * tok, cols), f32),
            pltpu.SemaphoreType.DMA,
            pltpu.SemaphoreType.DMA((2, ways)),
            pltpu.SemaphoreType.DMA((ways,)),
            pltpu.SemaphoreType.DMA((ways,)),
        ]
        + RowGather.scratch(ways // 2),
        [rows, codes, weights],
        ident,
        55,
        (2,),
        (0, 2),
    )


def attn_out_and_ff(attn_low, m_mid, p_down, token_rows, grad_out, gains, groups, ways, ident):
    tok, width = token_rows.shape
    half = tok // 2
    own_feat, own_ff = attn_low.shape[1], p_down.shape[1]
    part = p_down.shape[0]
    row = ways * tok
    tile = min(own_ff, 1024)
    square = width == 2 * own_ff
    square_tile = 256
    squares = width // square_tile

    def kernel(
        left_far, mid_far, down_far, x_far, go_far, gains_ref,
        branch_far, out_ref, gg_ref, hid_far, mix_far, gm_far, dgu_far, first_ref,
        left, mid_ref, down_ref, x_ref, go_ref, branch_ref, hid_ref, mix_ref, gm_ref, dgu_ref,
        down_turned, in_sem, out_sem, branch_sem, down_send, down_recv, *rest
    ):
        line = Line(ways)
        group = lax.axis_index("dp")
        gu_cols, out_cols = pl.ds(0, 2 * own_ff), pl.ds(2 * own_ff, own_feat)
        fetch = [
            pltpu.make_async_copy(src, dst, in_sem.at[i])
            for i, (src, dst) in enumerate(
                [
                    (left_far, left),
                    (mid_far.at[:, out_cols], mid_ref.at[:, out_cols]),
                    (x_far, x_ref),
                    (mid_far.at[:, gu_cols], mid_ref.at[:, gu_cols]),
                    (down_far, down_ref.at[rows_at(group, part)]),
                    (go_far, go_ref),
                ]
            )
        ]
        for copy in fetch:
            copy.start()
        outs = Blocks(
            line,
            2 * half,
            [(hid_ref, hid_far), (mix_ref, mix_far), (gm_ref, gm_far), (dgu_ref, dgu_far)],
            out_sem,
        )
        keep_branch = pltpu.make_async_copy(branch_ref, branch_far, branch_sem)
        line.greet(groups)

        def spread(off):
            return pltpu.make_async_remote_copy(
                src_ref=down_far,
                dst_ref=down_ref.at[rows_at(group, part)],
                send_sem=down_send.at[off],
                recv_sem=down_recv.at[off],
                device_id={"dp": (group + off) % groups},
                device_id_type=MESH,
            )

        for off in range(1, groups):
            spread(off).start()
        scatter = RowScatter(line, half, rest[:3], rest[3:7])
        hidden = RowGather(line, half, hid_ref, rest[7:12])
        back = RowGather(line, half, gm_ref, rest[12:17])
        gg_ref[...] = jnp.zeros_like(gg_ref)
        gain_attn, gain_mlp = gains_ref[2:3, :], gains_ref[3:4, :]

        def own(h, strip):
            return pl.ds(pl.multiple_of((h * ways + line.me) * half + strip.start, 16), strip.size)

        def residual(at):
            branch = branch_ref[at, :]
            factor = lax.rsqrt(mean_rows(branch * branch) + norm_eps)
            return x_ref[at, :].astype(f32) + branch * factor * gain_attn

        def settle_attn(h):
            def one(strip):
                at = pl.ds(pl.multiple_of(h * half + strip.start, 16), strip.size)
                branch_ref[at, :] = scatter.total(h, strip)
                hid_ref[own(h, strip), :] = residual(at).astype(bf16)

            scatter.close(h)
            each_strip(half, 16, one)
            hidden.start(h)
            scatter.finish(h)

        def settle_mlp(h):
            def one(strip):
                at = pl.ds(pl.multiple_of(h * half + strip.start, 16), strip.size)
                mlp = scatter.total(h, strip)
                factor = lax.rsqrt(mean_rows(mlp * mlp) + norm_eps)
                unit = mlp * factor
                grad = go_ref[at, :].astype(f32)
                out_ref[at, :] = (residual(at) + unit * gain_mlp).astype(bf16)
                terms = grad * unit
                gg_ref[...] += terms[:8] + terms[8:]
                lifted = grad * gain_mlp
                turned = factor * (lifted - unit * mean_rows(lifted * unit))
                gm_ref[own(h, strip), :] = turned.astype(bf16)

            scatter.close(h)
            each_strip(half, 16, one)
            back.start(h)
            scatter.finish(h)

        def gate_up(chip, h):
            at = rows_at(h * line.chips + chip, 2 * half)

            outs.send(0, chip, h)

            both = dot_nn(hid_ref[at, :], mid_ref[:, gu_cols])
            gate, up = both[:, :own_ff], both[:, own_ff:]
            dgu_ref[at, :] = both.astype(bf16)
            mix_ref[at, :] = (gate * jax.nn.sigmoid(gate) * up).astype(bf16)
            outs.send(1, chip, h)

        def gate_up_back(chip, h):
            at = rows_at(h * line.chips + chip, 2 * half)

            outs.send(2, chip, h)

            def one(n, carry):
                here, there = rows_at(n, tile), pl.ds(pl.multiple_of(own_ff + n * tile, tile), tile)
                grad = dot_nn(gm_ref[at, :], down_ref[:, here])
                gate, up = dgu_ref[at, here].astype(f32), dgu_ref[at, there].astype(f32)
                sigma = jax.nn.sigmoid(gate)
                dgu_ref[at, here] = (grad * up * sigma * (1.0 + gate * (1.0 - sigma))).astype(bf16)
                dgu_ref[at, there] = (grad * gate * sigma).astype(bf16)
                return carry

            lax.fori_loop(0, own_ff // tile, one, 0)
            outs.send(3, chip, h)

        for copy in fetch[:3]:
            copy.wait()
        scatter.of(left, mid_ref.at[:, out_cols], 1024, True)
        advance(scatter, 0)
        fetch[3].wait()
        settle_attn(0)
        advance(scatter, 1, hidden, 0, gate_up)
        settle_attn(1)
        hidden.use_at(line.last, 0, gate_up)
        def turn_down(i, carry):
            rows = rows_at(i, square_tile)
            down_turned[:, rows] = down_ref[rows, :].T
            return carry

        def turn_square(s):
            def one(i, carry):
                def two(j, carry):
                    rows, cols = rows_at(i, square_tile), rows_at(j, square_tile)
                    block, other = mid_ref[rows, cols], mid_ref[cols, rows]
                    mid_ref[cols, rows] = block.T
                    mid_ref[rows, cols] = other.T
                    return carry

                return lax.fori_loop(i, squares, two, carry)

            lax.fori_loop(s * squares // line.chips, (s + 1) * squares // line.chips, one, 0)

        keep_branch.start()
        for copy in fetch[4:]:
            copy.wait()
        for off in range(1, groups):
            spread(off).wait()
        if square:
            lax.fori_loop(0, squares, turn_down, 0)
            scatter.of(mix_ref, down_turned, 2048, False, True)
        else:
            scatter.of(mix_ref, down_ref, 2048, False)
        advance(scatter, 0, hidden, 1, gate_up)
        settle_mlp(0)
        hidden.use_at(line.last, 1, gate_up)
        advance(scatter, 1, back, 0, gate_up_back, turn_square if square else None)
        settle_mlp(1)
        back.use_at(line.last, 0, gate_up_back)
        scatter.of(dgu_ref, mid_ref.at[:, gu_cols], 1024, False, square)
        advance(scatter, 0, back, 1, gate_up_back)
        back.use_at(line.last, 1, gate_up_back)

        def put(strip):
            first_ref[strip, :] = scatter.total(0, strip)

        scatter.close(0)
        each_strip(half, 16, put)
        scatter.finish(0)
        hidden.finish()
        back.finish()
        keep_branch.wait()
        outs.finish()

    return call(
        kernel,
        [
            shape((tok, width), f32),
            shape((tok, width), bf16),
            shape((8, width), f32),
            shape((row, width), bf16),
            shape((row, own_ff), bf16),
            shape((row, width), bf16),
            shape((row, 2 * own_ff), bf16),
            shape((half, width), f32),
        ],
        [
            pltpu.VMEM((row, own_feat), bf16),
            pltpu.VMEM(m_mid.shape, bf16),
            pltpu.VMEM((groups * part, own_ff), bf16),
            pltpu.VMEM((tok, width), bf16),
            pltpu.VMEM((tok, width), bf16),
            pltpu.VMEM((tok, width), f32),
            pltpu.VMEM((row, width), bf16),
            pltpu.VMEM((row, own_ff), bf16),
            pltpu.VMEM((row, width), bf16),
            pltpu.VMEM((row, 2 * own_ff), bf16),
            pltpu.VMEM((own_ff, width) if square else (16, HEAD_DIM), bf16),
            pltpu.SemaphoreType.DMA((6,)),
            pltpu.SemaphoreType.DMA((4, ways)),
            pltpu.SemaphoreType.DMA,
            pltpu.SemaphoreType.DMA((groups,)),
            pltpu.SemaphoreType.DMA((groups,)),
        ]
        + RowScatter.scratch(ways // 2, tok, width)
        + RowGather.scratch(ways // 2)
        + RowGather.scratch(ways // 2),
        [attn_low, m_mid, p_down, token_rows, grad_out, gains],
        ident,
        150,
        range(5),
        (0, 3, 4, 5, 6),
    )


def ff_to_attn_back(
    grad_gu, first_half, m_mid, branch, grad_out, gain_row, grad_mlp, mixed_low, ways, ident
):
    tok, width = branch.shape
    half = tok // 2
    own_ff = grad_gu.shape[1] // 2
    own_feat = m_mid.shape[1] - 2 * own_ff
    row = ways * tok
    tiles = width // 256

    def kernel(
        left, first_ref, w_ref, br_ref, go_ref, gain_ref, gm_far, mix_far,
        gh_ref, gg_ref, all_far, ga_ref, dd_far,
        all_ref, out_sem, gm_ref, mix_ref, dd_ref, gm_sem, mix_sem, dd_sem, *rest
    ):
        line = Line(ways)
        mix_copy = pltpu.make_async_copy(mix_far, mix_ref, mix_sem)

        def fetch(i):
            return pltpu.make_async_copy(
                gm_far.at[:, pl.ds(i * 256, 256)], gm_ref.at[i % 2], gm_sem.at[i % 2]
            )

        def keep(i):
            rows = pl.ds(i * 256, 256)
            return pltpu.make_async_copy(dd_ref.at[rows], dd_far.at[rows], dd_sem.at[i])

        def down_grad(i):
            fetch(i).wait()
            if i + 1 < tiles:
                fetch(i + 1).start()
            dd_ref[pl.ds(i * 256, 256), :] = dot_tn(gm_ref[i % 2], mix_ref[...]).astype(bf16)
            keep(i).start()

        def fill(s):
            for i in range(tiles):

                @pl.when(s == i * line.chips // tiles)
                def _(i=i):
                    down_grad(i)

        outs = Blocks(line, 2 * half, [(all_ref, all_far)], out_sem)
        line.greet()
        scatter = RowScatter(line, half, rest[:3], rest[3:7])
        gather = RowGather(line, half, all_ref, rest[7:])
        gg_ref[...] = jnp.zeros_like(gg_ref)

        def settle(h):
            def one(strip):
                at = pl.ds(pl.multiple_of(h * half + strip.start, 16), strip.size)
                mine = pl.ds(
                    pl.multiple_of((h * ways + line.me) * half + strip.start, 16), strip.size
                )
                total = scatter.total(h, strip) if h else first_ref[strip, :]
                grad = total + go_ref[at, :].astype(f32)
                branch = br_ref[at, :]
                factor = lax.rsqrt(mean_rows(branch * branch) + norm_eps)
                unit = branch * factor
                gh_ref[at, :] = grad
                terms = grad * unit
                gg_ref[...] += terms[:8] + terms[8:]
                lifted = grad * gain_ref[...]
                turned = factor * (lifted - unit * mean_rows(lifted * unit))
                all_ref[mine, :] = turned.astype(bf16)

            if h:
                scatter.close(h)
            each_strip(half, 16, one)
            gather.start(h)

        def use(chip, h):
            at = rows_at(h * line.chips + chip, 2 * half)
            outs.send(0, chip, h)
            ga_ref[at, :] = dot_nn(all_ref[at, :], w_ref[:, pl.ds(2 * own_ff, own_feat)])

        scatter.of(left, w_ref.at[:, pl.ds(0, 2 * own_ff)], 1024, False)
        settle(0)
        advance(scatter, 1, gather, 0, use)
        settle(1)
        gather.use_at(line.last, 0, use)
        mix_copy.start()
        fetch(0).start()
        mix_copy.wait()
        advance(None, 0, gather, 1, use, fill)
        gather.use_at(line.last, 1, use)
        gather.finish()
        outs.finish()
        for i in range(tiles):
            keep(i).wait()
        scatter.finish(1)

    return call(
        kernel,
        [
            shape((tok, width), f32),
            shape((8, width), f32),
            shape((row, width), bf16),
            shape((row, own_feat), f32),
            shape((width, own_ff), bf16),
        ],
        [
            pltpu.VMEM((row, width), bf16),
            pltpu.SemaphoreType.DMA((1, ways)),
            pltpu.VMEM((2, row, 256), bf16),
            pltpu.VMEM((row, own_ff), bf16),
            pltpu.VMEM((width, own_ff), bf16),
            pltpu.SemaphoreType.DMA((2,)),
            pltpu.SemaphoreType.DMA,
            pltpu.SemaphoreType.DMA((tiles,)),
        ]
        + RowScatter.scratch(ways // 2, tok, width)
        + RowGather.scratch(ways // 2),
        [grad_gu, first_half, m_mid, branch, grad_out, gain_row, grad_mlp, mixed_low],
        ident,
        70,
        (6, 7),
        (2, 4),
    )


def home_copies(me, ways, source, targets, widths, send, recv):
    rows = source.shape[0] // ways
    begins = [sum(widths[:i]) for i in range(len(widths))]
    count = len(widths)

    def part(i, dest):
        return (
            source.at[rows_at(dest, rows), pl.ds(begins[i], widths[i])],
            targets[i].at[:, rows_at(me, widths[i])],
        )

    def move(off, i):
        dest = (me + off) % ways
        return remote(*part(i, dest), send.at[off * count + i], recv.at[off * count + i], dest)

    def keep(i):
        return pltpu.make_async_copy(*part(i, me), send.at[i])

    def each(what):
        def one(off, carry):
            for i in range(count):
                what(move(off, i))
            return carry

        lax.fori_loop(1, ways, one, 0)

    def start():
        for i in range(count):
            keep(i).start()
        each(lambda copy: copy.start())

    def wait():
        for i in range(count):
            keep(i).wait()
        each(lambda copy: copy.wait())

    return start, wait


def greet_line(me, ways):
    barrier = pltpu.get_barrier_semaphore()

    def greet(off, carry):
        pl.semaphore_signal(
            barrier, inc=1, device_id={"seq": (me + off) % ways}, device_id_type=MESH
        )
        return carry

    lax.fori_loop(1, ways, greet, 0)
    pl.semaphore_wait(barrier, ways - 1)


def bring_home(summed, widths, ways, ident):
    rows = summed.shape[0] // ways
    count = len(widths)

    def kernel(*refs):
        source, targets, (send, recv) = refs[0], refs[1 : 1 + count], refs[1 + count :]
        me = lax.axis_index("seq")
        greet_line(me, ways)
        start, wait = home_copies(me, ways, source, targets, widths, send, recv)
        start()
        wait()

    return call(
        kernel,
        [shape((rows, ways * width), bf16) for width in widths],
        [pltpu.SemaphoreType.DMA((ways * count,))] * 2,
        [summed],
        ident,
        30,
        (0,),
        range(count),
    )


def project_back(grad_qkv, m_qkv, grad_hidden, d_down, ways, ident):
    tok, width = grad_hidden.shape
    half = tok // 2
    own_ff = d_down.shape[1]

    def kernel(left, w_ref, gh_ref, dd_ref, out_ref, home_ref, dd_send, dd_recv, *rest):
        line = Line(ways)
        greet_line(line.me, ways)
        start, wait = home_copies(line.me, ways, dd_ref, [home_ref], [own_ff], dd_send, dd_recv)
        start()
        scatter = RowScatter(line, half, rest[:3], rest[3:7])
        scatter.of(left, w_ref.at[:, pl.ds(0, left.shape[1])], 1024, True)
        for h in (0, 1):
            advance(scatter, h)
        for h in (0, 1):

            def one(strip, h=h):
                at = pl.ds(pl.multiple_of(h * half + strip.start, 16), strip.size)
                out_ref[at, :] = (gh_ref[at, :] + scatter.total(h, strip)).astype(bf16)

            scatter.close(h)
            each_strip(half, 16, one)
        for h in (0, 1):
            scatter.finish(h)
        wait()

    return call(
        kernel,
        [
            shape((tok, width), bf16),
            shape((d_down.shape[0] // ways, ways * own_ff), bf16),
        ],
        [pltpu.SemaphoreType.DMA((ways,))] * 2 + RowScatter.scratch(ways // 2, tok, width),
        [grad_qkv, m_qkv, grad_hidden, d_down],
        ident,
        65,
        (3,),
        (1,),
    )


def half_turn(values, sign):
    half_dim = HEAD_DIM // 2
    lane = lax.broadcasted_iota(jnp.int32, values.shape, 1)
    swapped = pltpu.roll(values, half_dim, 1)
    return jnp.where(lane < half_dim, -sign * swapped, sign * swapped)


def attend(parts, block):
    row = parts[0].shape[0]
    width = parts[0].shape[1] // 3
    heads = width // HEAD_DIM
    scale = HEAD_DIM ** (-0.5)

    def kernel(
        qkv_ref, factor_ref, cos_ref, sin_ref, gain_ref, qpos_ref, kpos_ref, kmax_ref,
        q_ref, k_ref, v_ref, at_ref, low_ref, ws_ref
    ):
        def turn(i, carry):
            rows = rows_at(i, block)
            cosine, sine = cos_ref[rows, :], sin_ref[rows, :]
            for which, out_ref in ((0, q_ref), (1, k_ref)):
                factor = factor_ref[rows, pl.ds(which, 1)]
                for head in range(heads):
                    lanes = pl.ds(head * HEAD_DIM, HEAD_DIM)
                    raw = qkv_ref[rows, pl.ds(which * width + head * HEAD_DIM, HEAD_DIM)]
                    normed = raw * factor * gain_ref[which : which + 1, lanes]
                    out_ref[rows, lanes] = (
                        normed * cosine + half_turn(normed, 1.0) * sine
                    ).astype(bf16)
            v_ref[rows, :] = qkv_ref[rows, pl.ds(2 * width, width)].astype(bf16)
            return carry

        lax.fori_loop(0, row // block, turn, 0)

        def one(i, carry):
            rows = rows_at(i, block)
            qpos = qpos_ref[rows, :]
            mask = (kpos_ref[...] <= qpos) & (qpos <= kmax_ref[...])
            for head in range(heads):
                lanes = pl.ds(head * HEAD_DIM, HEAD_DIM)
                scores = dot_nt(q_ref[rows, lanes], k_ref[:, lanes]) * (scale * LOG2_E)
                expo = jnp.where(mask, jnp.exp2(scores), 0.0)
                total = jnp.sum(expo, axis=-1, keepdims=True)
                result = dot_nn(expo.astype(bf16), v_ref[:, lanes]) / total
                ws_ref[rows, pl.ds(head, 1)] = total
                at_ref[rows, lanes] = result
                low_ref[rows, lanes] = result.astype(bf16)
            return carry

        lax.fori_loop(0, row // block, one, 0)

    return pl.pallas_call(
        kernel,
        out_shape=[shape((row, width), bf16)] * 3
        + [shape((row, width), f32), shape((row, width), bf16), shape((row, heads), f32)],
        in_specs=[pl.BlockSpec(memory_space=pltpu.VMEM)] * len(parts),
        out_specs=[pl.BlockSpec(memory_space=pltpu.VMEM)] * 6,
        cost_estimate=pl.CostEstimate(
            flops=4 * row * row * width, transcendentals=row * row * heads, bytes_accessed=60 * 10**6
        ),
        compiler_params=pltpu.CompilerParams(vmem_limit_bytes=60 * 2**20),
    )(*parts)


def attend_back(parts, summed, block, ways, ident):
    row, width = parts[0].shape
    heads = width // HEAD_DIM
    scale = HEAD_DIM ** (-0.5)

    def kernel(
        q_ref, k_ref, v_ref, ga_ref, at_ref, ws_ref, cos_ref, sin_ref, qkv_ref, factor_ref,
        gain_ref, qpos_ref, kpos_ref, kmax_ref, sum_ref,
        cq_ref, ck_ref, dv_ref, terms_ref, gg_ref, home_ref, dk_acc, dv_acc, send, recv
    ):
        me = lax.axis_index("seq")
        greet_line(me, ways)
        start, wait = home_copies(me, ways, sum_ref, [home_ref], [summed.shape[1]], send, recv)
        start()
        gg_ref[...] = jnp.zeros_like(gg_ref)
        dk_acc[...] = jnp.zeros_like(dk_acc)
        dv_acc[...] = jnp.zeros_like(dv_acc)

        def turn_back(grad, rows, which, out_ref, head):
            lanes = pl.ds(head * HEAD_DIM, HEAD_DIM)
            cosine, sine = cos_ref[rows, :], sin_ref[rows, :]
            normed = grad * cosine + half_turn(grad * sine, -1.0)
            raw = qkv_ref[rows, pl.ds(which * width + head * HEAD_DIM, HEAD_DIM)]
            unit = raw * factor_ref[rows, pl.ds(which, 1)]
            gg_ref[which : which + 1, lanes] += jnp.sum(normed * unit, axis=0, keepdims=True)
            lifted = normed * gain_ref[which : which + 1, lanes]
            out_ref[rows, lanes] = lifted
            term = jnp.sum(lifted * unit, axis=-1, keepdims=True)
            column = pl.ds(which, 1)
            if head == 0:
                terms_ref[rows, column] = term
            else:
                terms_ref[rows, column] += term

        def one(i, carry):
            rows = rows_at(i, block)
            qpos = qpos_ref[rows, :]
            mask = (kpos_ref[...] <= qpos) & (qpos <= kmax_ref[...])
            for head in range(heads):
                lanes = pl.ds(head * HEAD_DIM, HEAD_DIM)
                grad = ga_ref[rows, lanes]
                inverse = 1.0 / ws_ref[rows, pl.ds(head, 1)]
                drop = jnp.sum(grad * at_ref[rows, lanes], axis=-1, keepdims=True) * inverse
                grad_num = (grad * inverse).astype(bf16)
                query, keys = q_ref[rows, lanes], k_ref[:, lanes]
                scores = dot_nt(query, keys) * (scale * LOG2_E)
                expo = jnp.where(mask, jnp.exp2(scores), 0.0)
                grad_expo = dot_nt(grad_num, v_ref[:, lanes])
                grad_scores = (expo * (grad_expo - drop)).astype(bf16)
                turn_back(dot_nn(grad_scores, keys) * scale, rows, 0, cq_ref, head)
                dk_acc[:, lanes] += dot_tn(grad_scores, query)
                dv_acc[:, lanes] += dot_tn(expo.astype(bf16), grad_num)
            return carry

        lax.fori_loop(0, row // block, one, 0)

        def last(i, carry):
            rows = rows_at(i, block)
            for head in range(heads):
                lanes = pl.ds(head * HEAD_DIM, HEAD_DIM)
                turn_back(dk_acc[rows, lanes] * scale, rows, 1, ck_ref, head)
                dv_ref[rows, lanes] = dv_acc[rows, lanes].astype(bf16)
            return carry

        lax.fori_loop(0, row // block, last, 0)
        wait()

    return call(
        kernel,
        [
            shape((row, width), f32),
            shape((row, width), f32),
            shape((row, width), bf16),
            shape((row, 2), f32),
            shape((2, width), f32),
            shape((summed.shape[0] // ways, ways * summed.shape[1]), bf16),
        ],
        [pltpu.VMEM((row, width), f32)] * 2 + [pltpu.SemaphoreType.DMA((ways,))] * 2,
        list(parts) + [summed],
        ident,
        25,
        (len(parts),),
        (5,),
    )


def attn_grads(x_row, grad_qkv, grad_branch, attn_low, gain_columns, summed, ways, ident):
    row, width = x_row.shape
    first, second = grad_qkv.shape[1], attn_low.shape[1]
    cols = first + second + gain_columns.shape[1]

    def kernel(
        x_far, dq_ref, gb_far, low_ref, gain_ref, sum_ref, out_far, home_ref,
        x_ref, gb_ref, out_ref, in_sem, out_sem, send, recv
    ):
        me = lax.axis_index("seq")
        fetch = [
            pltpu.make_async_copy(x_far, x_ref, in_sem.at[0]),
            pltpu.make_async_copy(gb_far, gb_ref, in_sem.at[1]),
        ]
        for copy in fetch:
            copy.start()
        greet_line(me, ways)
        start, wait = home_copies(me, ways, sum_ref, [home_ref], [summed.shape[1]], send, recv)
        start()
        for copy in fetch:
            copy.wait()
        tile = 256

        def keep(i):
            rows = rows_at(i, tile)
            return pltpu.make_async_copy(out_ref.at[rows], out_far.at[rows], out_sem.at[i])

        def one(i, carry):
            rows = rows_at(i, tile)
            out_ref[rows, pl.ds(0, first)] = dot_tn(x_ref[:, rows], dq_ref[...]).astype(bf16)
            out_ref[rows, pl.ds(first, second)] = dot_tn(gb_ref[:, rows], low_ref[...]).astype(bf16)
            out_ref[rows, pl.ds(first + second, gain_columns.shape[1])] = gain_ref[rows, :]
            keep(i).start()
            return carry

        lax.fori_loop(0, width // tile, one, 0)

        def kept(i, carry):
            keep(i).wait()
            return carry

        lax.fori_loop(0, width // tile, kept, 0)
        wait()

    return call(
        kernel,
        [
            shape((width, cols), bf16),
            shape((summed.shape[0] // ways, ways * summed.shape[1]), bf16),
        ],
        [
            pltpu.VMEM((row, width), bf16),
            pltpu.VMEM((row, width), bf16),
            pltpu.VMEM((width, cols), bf16),
            pltpu.SemaphoreType.DMA((2,)),
            pltpu.SemaphoreType.DMA((width // 256,)),
            pltpu.SemaphoreType.DMA((ways,)),
            pltpu.SemaphoreType.DMA((ways,)),
        ],
        [x_row, grad_qkv, grad_branch, attn_low, gain_columns, summed],
        ident,
        25,
        (0, 2, 5),
        (0, 1),
    )


def exchange(sources, ways, ident, cost):
    rows = sources[0].shape[0]
    widths = [a.shape[1] // ways for a in sources]
    begins = [sum(widths[:i]) for i in range(len(widths))]
    count = len(sources)

    def kernel(*refs):
        ins, out_ref, send, recv, local = refs[:count], *refs[count:]
        me = lax.axis_index("seq")
        barrier = pltpu.get_barrier_semaphore()

        def greet(off, carry):
            pl.semaphore_signal(
                barrier, inc=1, device_id={"seq": (me + off) % ways}, device_id_type=MESH
            )
            return carry

        def move(off, i):
            dest = (me + off) % ways
            return remote(
                ins[i].at[:, rows_at(dest, widths[i])],
                out_ref.at[rows_at(me, rows), pl.ds(begins[i], widths[i])],
                send.at[off * count + i],
                recv.at[off * count + i],
                dest,
            )

        def keep(i):
            return pltpu.make_async_copy(
                ins[i].at[:, rows_at(me, widths[i])],
                out_ref.at[rows_at(me, rows), pl.ds(begins[i], widths[i])],
                local.at[i],
            )

        def each(what):
            def one(off, carry):
                for i in range(count):
                    what(move(off, i))
                return carry

            lax.fori_loop(1, ways, one, 0)

        for i in range(count):
            keep(i).start()
        lax.fori_loop(1, ways, greet, 0)
        pl.semaphore_wait(barrier, ways - 1)
        each(lambda copy: copy.start())
        for i in range(count):
            keep(i).wait()
        each(lambda copy: copy.wait())

    return pl.pallas_call(
        kernel,
        out_shape=shape((ways * rows, sum(widths)), bf16),
        in_specs=[pl.BlockSpec(memory_space=pl.ANY)] * count,
        out_specs=pl.BlockSpec(memory_space=pl.ANY),
        scratch_shapes=[
            pltpu.SemaphoreType.DMA((ways * count,)),
            pltpu.SemaphoreType.DMA((ways * count,)),
            pltpu.SemaphoreType.DMA((count,)),
        ],
        cost_estimate=pl.CostEstimate(
            flops=cost * 10**9, transcendentals=0, bytes_accessed=cost * 3 * 10**6
        ),
        compiler_params=pltpu.CompilerParams(collective_id=ident, has_side_effects=True),
    )(*sources)


def line_sum(terms, ways, ident):
    def kernel(terms_ref, out_ref, slots, send, recv):
        me = lax.axis_index("seq")
        barrier = pltpu.get_barrier_semaphore()
        for off in range(1, ways):
            pl.semaphore_signal(
                barrier, inc=1, device_id={"seq": (me + off) % ways}, device_id_type=MESH
            )
        pl.semaphore_wait(barrier, ways - 1)
        for off in range(1, ways):
            remote(
                terms_ref, slots.at[off], send.at[off], recv.at[off], (me + off) % ways
            ).start()
        total = terms_ref[...]
        for off in range(1, ways):
            remote(terms_ref, slots.at[off], send.at[off], recv.at[off], (me + off) % ways).wait_recv()
            total = total + slots[off]
        out_ref[...] = total
        for off in range(1, ways):
            remote(terms_ref, slots.at[off], send.at[off], recv.at[off], (me + off) % ways).wait_send()

    return call(
        kernel,
        [shape(terms.shape, f32)],
        [
            pltpu.VMEM((ways,) + terms.shape, f32),
            pltpu.SemaphoreType.DMA((ways,)),
            pltpu.SemaphoreType.DMA((ways,)),
        ],
        [terms],
        ident,
        8,
    )[0]


def body(
    tokens,
    w_query,
    w_key,
    w_value,
    w_out,
    w_gate,
    w_up,
    w_down,
    gain_query,
    gain_key,
    gain_attn,
    gain_mlp,
    cotangent,
    key_mask,
    lengths,
    tract_order,
):
    ways, groups = lax.axis_size("seq"), lax.axis_size("dp")
    me = lax.axis_index("seq")
    token_rows = tokens[0]
    tok_count, feat_width = token_rows.shape
    ff_width = w_gate.shape[1]
    own_feat = feat_width // ways
    own_heads = own_feat // HEAD_DIM
    own_ff = ff_width // ways
    row_len = tok_count * ways
    score_scale = HEAD_DIM ** (-0.5)
    half_len = tok_count // 2
    order_pair = tract_order[0]
    slot_index = jnp.arange(tok_count, dtype=jnp.int32)
    local_pos = (
        jnp.where(slot_index < half_len, order_pair[0], order_pair[1]) * half_len
        + slot_index % half_len
    )
    key_ok = ((key_mask[0] == 1) & (local_pos < lengths[0])).astype(jnp.int32)

    gain_local = jnp.stack([gain_query, gain_key, gain_attn, gain_mlp], axis=1)
    gain_pad = jnp.pad(gain_local, ((0, 0), (0, HEAD_DIM - 4)))
    gain_all = jnp.tile(gain_pad, (1, ways))
    p_qkv = exchange([w_query, w_key, w_value, gain_all], ways, 8, 20)
    m_qkv = across(p_qkv)
    p_qkv, w_gate, w_up, w_out_t = lax.optimization_barrier(
        (p_qkv, w_gate, w_up, jnp.transpose(w_out))
    )
    p_mid = exchange([w_gate, w_up, w_out_t], ways, 10, 50)
    m_mid = across(p_mid)
    gains = dot_nt(jnp.eye(8, HEAD_DIM, dtype=bf16), m_qkv[:, 3 * own_feat :])
    gain_q = lax.dynamic_slice_in_dim(gains[0], me * own_feat, own_feat, 0)
    gain_k = lax.dynamic_slice_in_dim(gains[1], me * own_feat, own_feat, 0)

    code_pad = -tok_count % HEAD_DIM
    local_code = jnp.pad(local_pos * 2 + key_ok, (0, code_pad))[None]
    local_code, p_mid = lax.optimization_barrier((local_code, p_mid))
    x_row, codes, qkv = gather_project(token_rows, local_code, m_qkv, ways, 1)
    key_code = codes[:, 0, :tok_count].reshape(ways, 2, half_len)
    key_code = jnp.transpose(key_code, (1, 0, 2)).reshape(row_len)
    pos = key_code // 2
    q_raw, k_raw, v_raw = (qkv[:, i * own_feat : (i + 1) * own_feat] for i in range(3))
    squares = line_sum(
        jnp.stack([jnp.sum(q_raw * q_raw, axis=-1), jnp.sum(k_raw * k_raw, axis=-1)]), ways, 2
    )
    squares, w_down_t = lax.optimization_barrier((squares, jnp.transpose(w_down)))
    p_down = lax.all_to_all(w_down_t, "seq", split_axis=1, concat_axis=0, tiled=True)
    factors = jnp.transpose(lax.rsqrt(squares / feat_width + norm_eps))
    cosine, sine = rope_tables(pos, HEAD_DIM)
    key_most = jnp.where(key_code % 2 == 1, jnp.int32(2**30), pos)
    places = [pos[:, None], pos[None], key_most[None]]
    gain_qk = jnp.stack([gain_q, gain_k])
    query_low, key_low, value_low, attn, attn_low, weight_sum = attend(
        [qkv, factors, cosine, sine, gain_qk] + places, min(row_len, 320)
    )

    branch, layer_out, grad_gain_mlp, hidden_low, mixed_low, grad_mlp, grad_gu, first_half = (
        attn_out_and_ff(
            attn_low, m_mid, p_down, token_rows, cotangent[0], gains, groups, ways, 3
        )
    )
    d_gate = dot_tn(hidden_low, grad_gu[:, :own_ff]).astype(bf16)
    grad_gu, d_gate = lax.optimization_barrier((grad_gu, d_gate))
    d_up = dot_tn(hidden_low, grad_gu[:, own_ff:]).astype(bf16)
    grad_gu, d_up = lax.optimization_barrier((grad_gu, d_up))
    d_gate, d_up = dp_sum(d_gate), dp_sum(d_up)
    grad_hidden, grad_gain_attn, grad_branch, grad_attn, d_down = ff_to_attn_back(
        grad_gu, first_half, m_mid, branch, cotangent[0], gains[2:3], grad_mlp, mixed_low, ways, 5
    )
    d_down = dp_sum(d_down)
    c_q, c_k, grad_v, terms, gain_part, dw_gate = attend_back(
        [query_low, key_low, value_low, grad_attn, attn, weight_sum]
        + [cosine, sine, qkv, factors, gain_qk]
        + places,
        d_gate,
        min(row_len, 320),
        ways,
        13,
    )
    terms = jnp.transpose(terms)
    means = line_sum(terms, ways, 6) / feat_width
    q_factor, k_factor = factors[:, :1], factors[:, 1:]
    grad_q_raw = q_factor * (c_q - q_raw * q_factor * means[0][:, None])
    grad_k_raw = k_factor * (c_k - k_raw * k_factor * means[1][:, None])
    grad_qkv = jnp.concatenate(
        [grad_q_raw.astype(bf16), grad_k_raw.astype(bf16), grad_v], axis=1
    )

    own_slot = jnp.zeros((2, feat_width), f32)
    own_slot = lax.dynamic_update_slice(own_slot, gain_part, (0, me * own_feat))
    gain_terms = jnp.concatenate(
        [
            own_slot,
            jnp.sum(grad_gain_attn, axis=0, keepdims=True),
            jnp.sum(grad_gain_mlp, axis=0, keepdims=True),
        ]
    )
    gain_columns = jnp.pad(jnp.transpose(gain_terms), ((0, 0), (0, HEAD_DIM - 4)))
    d_attn, dw_up = attn_grads(
        x_row, grad_qkv, grad_branch, attn_low, gain_columns.astype(bf16), d_up, ways, 14
    )
    grad_qkv, d_attn = lax.optimization_barrier((grad_qkv, d_attn))
    grad_tokens, dw_down = project_back(grad_qkv, m_qkv, grad_hidden, d_down, ways, 7)
    grad_tokens, d_attn = lax.optimization_barrier((grad_tokens, dp_sum(d_attn)))
    dw_gu = [dw_gate.astype(f32), dw_up.astype(f32)]
    dw_qkv = bring_home(d_attn, [own_feat] * 4 + [HEAD_DIM], ways, 12)
    dw_qkv = [part.astype(f32) for part in dw_qkv]
    dw_gu = [dw_gate.astype(f32), dw_up.astype(f32)]
    dw_down = [dw_down.astype(f32)]
    gain_grads = jnp.sum(dw_qkv[4].reshape(-1, ways, HEAD_DIM), axis=1)
    gain_grads = jnp.transpose(gain_grads[:, :8])
    return (
        layer_out[None],
        grad_tokens[None],
        dw_qkv[0],
        dw_qkv[1],
        dw_qkv[2],
        jnp.transpose(dw_qkv[3]),
        dw_gu[0],
        dw_gu[1],
        jnp.transpose(dw_down[0]),
        gain_grads[0],
        gain_grads[1],
        gain_grads[2],
        gain_grads[3],
    )


def solution(mesh):
    both = ("dp", "seq")
    in_specs = (
        P("dp", "seq", None),
        P(both, None),
        P(both, None),
        P(both, None),
        P(None, both),
        P(both, None),
        P(both, None),
        P(None, both),
        P(both),
        P(both),
        P(both),
        P(both),
        P("dp", "seq", None),
        P("dp", "seq"),
        P("dp"),
        P("dp", "seq"),
    )
    out_specs = (
        P("dp", "seq", None),
        P("dp", "seq", None),
        P(both, None),
        P(both, None),
        P(both, None),
        P(None, both),
        P(both, None),
        P(both, None),
        P(None, both),
        P(both),
        P(both),
        P(both),
        P(both),
    )
    return jax.shard_map(body, mesh=mesh, in_specs=in_specs, out_specs=out_specs, check_vma=False)
```

```python
import functools

import jax
import jax.numpy as jnp
from jax import lax
from jax.experimental import pallas as pl
from jax.experimental.pallas import tpu as pltpu
from jax.sharding import PartitionSpec as P

MESH = pl.DeviceIdType.MESH

HEAD_DIM = 128

rope_base = 500000.0
norm_eps = 1e-06
LOG2_E = 1.4426950408889634
f32 = jnp.float32
bf16 = jnp.bfloat16


def rope_tables(positions, head_dim):
    half_dim = head_dim // 2
    steps_f = jnp.arange(half_dim).astype(f32) * (2.0 / head_dim)
    inv_freq = jnp.power(rope_base, -steps_f)
    angle = positions.astype(f32)[:, None] * inv_freq[None, :]
    angle = jnp.concatenate([angle, angle], axis=-1)
    return (jnp.cos(angle), jnp.sin(angle))


def dot_nn(left, right):
    return jnp.dot(left, right, preferred_element_type=f32)


def dot_nt(left, right):
    return lax.dot_general(left, right, (((1,), (1,)), ((), ())), preferred_element_type=f32)


def dot_tn(left, right):
    return lax.dot_general(left, right, (((0,), (0,)), ((), ())), preferred_element_type=f32)


def across(piece):
    return lax.all_gather(piece, "dp", axis=0, tiled=True)


def dp_sum(grad):
    return lax.psum_scatter(grad, "dp", scatter_dimension=0, tiled=True)


class Line:
    def __init__(self, ways):
        self.chips = ways // 2
        self.last = self.chips - 1
        self.me = lax.axis_index("seq")
        self.chip = self.me // 2
        self.core = self.me % 2
        self.sibling = self.me + 1 - 2 * self.core

    def greet(self, groups=1):
        barrier = pltpu.get_barrier_semaphore()
        group = lax.axis_index("dp")
        for off in range(1, groups):
            pl.semaphore_signal(
                barrier, inc=1, device_id={"dp": (group + off) % groups}, device_id_type=MESH
            )
        has_low = jnp.minimum(self.chip, 1)
        has_high = jnp.minimum(self.last - self.chip, 1)
        pl.semaphore_signal(barrier, inc=1, device_id={"seq": self.sibling}, device_id_type=MESH)

        @pl.when(self.chip > 0)
        def _():
            pl.semaphore_signal(barrier, inc=1, device_id={"seq": self.me - 2}, device_id_type=MESH)

        @pl.when(self.chip < self.last)
        def _():
            pl.semaphore_signal(barrier, inc=1, device_id={"seq": self.me + 2}, device_id_type=MESH)

        pl.semaphore_wait(barrier, groups + has_low + has_high)


def remote(src, dst, send_sem, recv_sem, device):
    return pltpu.make_async_remote_copy(
        src_ref=src,
        dst_ref=dst,
        send_sem=send_sem,
        recv_sem=recv_sem,
        device_id={"seq": device},
        device_id_type=MESH,
    )


def rows_at(index, count):
    return pl.ds(pl.multiple_of(index * count, count), count)


def each_strip(tok_count, strip, fn):
    def one(i, carry):
        fn(rows_at(i, strip))
        return carry

    lax.fori_loop(0, tok_count // strip, one, 0)


class RowGather:
    def __init__(self, line, half, buf, sems):
        self.line, self.half, self.buf = line, half, buf
        self.up_send, self.down_send, self.col_recv, self.sib_send, self.sib_recv = sems

    @staticmethod
    def scratch(chips):
        return [pltpu.SemaphoreType.DMA((2 * chips,))] * 5

    def piece(self, src, core, h):
        return self.buf.at[rows_at(h * 2 * self.line.chips + 2 * src + core, self.half)]

    def hop(self, src, h, device, send):
        piece, at = self.piece(src, self.line.core, h), h * self.line.chips + src
        return remote(piece, piece, send.at[at], self.col_recv.at[at], device)

    def swap(self, src, core, h):
        piece, at = self.piece(src, core, h), h * self.line.chips + src
        return remote(piece, piece, self.sib_send.at[at], self.sib_recv.at[at], self.line.sibling)

    def start(self, h):
        line = self.line
        self.forward_up(line.chip, h)
        self.forward_down(line.chip, h)
        self.swap(line.chip, line.core, h).start()

    def forward_up(self, src, h):
        @pl.when(self.line.chip < self.line.last)
        def _():
            self.hop(src, h, self.line.me + 2, self.up_send).start()

    def forward_down(self, src, h):
        @pl.when(self.line.chip > 0)
        def _():
            self.hop(src, h, self.line.me - 2, self.down_send).start()

    def receive(self, away, h):
        line = self.line
        low, high = line.chip - away, line.chip + away

        @pl.when(low >= 0)
        def _():
            self.hop(low, h, line.sibling, self.up_send).wait_recv()
            self.forward_up(low, h)
            self.swap(low, line.core, h).start()

        @pl.when(high <= line.last)
        def _():
            self.hop(high, h, line.sibling, self.down_send).wait_recv()
            self.forward_down(high, h)
            self.swap(high, line.core, h).start()

    def use_at(self, away, h, use):
        line = self.line

        def one(side, carry):
            src = line.chip + (2 * side - 1) * away

            @pl.when((src >= 0) & (src <= line.last) & (away + 1 > side))
            def _():
                self.swap(src, 1 - line.core, h).wait_recv()
                use(src, h)

            return carry

        lax.fori_loop(0, 2, one, 0)

    def finish(self):
        line = self.line
        for h in (0, 1):

            def one(src, carry, h=h):
                self.swap(src, line.core, h).wait_send()

                @pl.when((src <= line.chip) & (line.chip < line.last))
                def _():
                    self.hop(src, h, line.sibling, self.up_send).wait_send()

                @pl.when((src >= line.chip) & (line.chip > 0))
                def _():
                    self.hop(src, h, line.sibling, self.down_send).wait_send()

                return carry

            lax.fori_loop(0, line.chips, one, 0)


class RowScatter:
    def __init__(self, line, half, bufs, sems):
        self.line, self.half = line, half
        self.pair, self.sib_in, self.acc = bufs
        self.sib_send, self.sib_recv, self.send, self.recv = sems

    @staticmethod
    def scratch(chips, tok, width):
        return [
            pltpu.VMEM((2 * chips * tok, width), bf16),
            pltpu.VMEM((chips * tok, width), bf16),
            pltpu.VMEM(((chips + 1) * tok, width), bf16),
            pltpu.SemaphoreType.DMA((2 * chips,)),
            pltpu.SemaphoreType.DMA((2 * chips,)),
            pltpu.SemaphoreType.DMA((2 * chips,)),
            pltpu.SemaphoreType.DMA((2 * (chips + 1),)),
        ]

    def of(self, left, right, tile, joined, turned=False):
        self.left, self.right, self.tile = left, right, tile
        self.joined, self.turned = joined, turned
        return self

    def swap(self, dest, h):
        half, line = self.half, self.line
        at = h * line.chips + dest
        return remote(
            self.pair.at[rows_at(2 * at + 1 - line.core, half)],
            self.sib_in.at[rows_at(at, half)],
            self.sib_send.at[at],
            self.sib_recv.at[at],
            line.sibling,
        )

    def hop(self, dest, slot, h, device):
        half, slots = self.half, self.line.chips + 1
        return remote(
            self.acc.at[rows_at(h * slots + dest, half)],
            self.acc.at[rows_at(h * slots + slot, half)],
            self.send.at[h * self.line.chips + dest],
            self.recv.at[h * slots + slot],
            device,
        )

    def produce(self, dest, h):
        if self.joined and h:
            return
        spans = [rows_at(h * self.line.chips + dest, 2 * self.half)]
        if self.joined:
            spans.append(rows_at(self.line.chips + dest, 2 * self.half))

        def one(n, carry):
            cols = rows_at(n, self.tile)
            left = [self.left[span, :] for span in spans]
            left = jnp.concatenate(left, axis=0) if self.joined else left[0]
            if self.turned:
                part = dot_nn(left, self.right[:, cols]).astype(bf16)
            else:
                part = dot_nt(left, self.right[cols, :]).astype(bf16)
            for i, span in enumerate(spans):
                self.pair[span, cols] = part[i * 2 * self.half : (i + 1) * 2 * self.half]
            return carry

        lax.fori_loop(0, self.right.shape[1 if self.turned else 0] // self.tile, one, 0)
        for i in range(len(spans)):
            self.swap(dest, h + i).start()

    def strip_of(self, index, strip):
        return pl.ds(pl.multiple_of(index * self.half + strip.start, 16), strip.size)

    def chip_sum(self, dest, h, strip):
        at = h * self.line.chips + dest
        mine = self.pair[self.strip_of(2 * at + self.line.core, strip), :]
        other = self.sib_in[self.strip_of(at, strip), :]
        return mine.astype(f32) + other.astype(f32)

    def legs(self, s):
        line = self.line
        below, above = line.chip, line.last - line.chip
        return (
            (line.last - s + below, 1, below, (s >= below) & (s < line.last)),
            (s - above, -1, above, (s >= above) & (s < line.last)),
        )

    def make(self, s, h):
        line = self.line
        if self.joined and h:
            return
        (up, _, _, has_up), (down, _, _, has_down) = self.legs(s)

        def one(k, carry):
            own, low = k // 2, k % 2
            dest = own * line.chip + (1 - own) * ((1 - low) * up + low * down)
            there = ((k == 0) & has_up) | ((k == 1) & has_down) | ((k == 2) & (s == line.last))

            @pl.when(there)
            def _():
                self.produce(dest, h)

            return carry

        lax.fori_loop(0, 3, one, 0)

    def pass_on(self, s, h):
        line = self.line
        chips, slots = line.chips, line.chips + 1
        for dest, step, behind, there in self.legs(s):
            if step > 0:
                slot = dest
            else:
                ends = 1 - jnp.minimum(line.chip - 1 - dest, 1)
                slot = dest + ends * (chips - dest)

            @pl.when(there)
            def _(dest=dest, behind=behind, slot=slot, step=step):
                self.swap(dest, h).wait_recv()

                @pl.when(behind > 0)
                def _():
                    self.hop(dest, dest, h, line.sibling).wait_recv()

                    def add(strip):
                        at = self.strip_of(h * slots + dest, strip)
                        total = self.chip_sum(dest, h, strip) + self.acc[at, :].astype(f32)
                        self.acc[at, :] = total.astype(bf16)

                    each_strip(self.half, 16, add)

                @pl.when(behind == 0)
                def _():
                    def put(strip):
                        at = self.strip_of(h * slots + dest, strip)
                        self.acc[at, :] = self.chip_sum(dest, h, strip).astype(bf16)

                    each_strip(self.half, 16, put)

                self.hop(dest, slot, h, line.me + 2 * step).start()

    def close(self, h):
        line = self.line
        chips, slots = line.chips, line.chips + 1
        empty = jnp.zeros((self.half, self.acc.shape[1]), bf16)
        self.swap(line.chip, h).wait_recv()

        @pl.when(line.chip > 0)
        def _():
            self.hop(line.chip, line.chip, h, line.sibling).wait_recv()

        @pl.when(line.chip == 0)
        def _():
            self.acc[rows_at(h * slots + line.chip, self.half), :] = empty

        @pl.when(line.chip < line.last)
        def _():
            self.hop(line.chip, chips, h, line.sibling).wait_recv()

        @pl.when(line.chip == line.last)
        def _():
            self.acc[rows_at(h * slots + chips, self.half), :] = empty

    def total(self, h, strip):
        line = self.line
        slots = line.chips + 1
        low = self.acc[self.strip_of(h * slots + line.chip, strip), :].astype(f32)
        high = self.acc[self.strip_of(h * slots + line.chips, strip), :].astype(f32)
        return self.chip_sum(line.chip, h, strip) + (low + high)

    def finish(self, h):
        line = self.line

        def one(dest, carry):
            self.swap(dest, h).wait_send()

            @pl.when(line.chip != dest)
            def _():
                self.hop(dest, dest, h, line.sibling).wait_send()

            return carry

        lax.fori_loop(0, line.chips, one, 0)


def advance(scatter=None, sh=0, gather=None, gh=0, use=None, fill=None, settle=None):
    line = (scatter or gather).line

    def slot(i, carry):
        s = i - 1
        if gather:

            @pl.when((s > 0) & (s < line.chips))
            def _():
                gather.receive(s, gh)

        if scatter:
            scatter.pass_on(s, sh)
            scatter.make(s + 1, sh)
        if settle:

            @pl.when(s == line.chips)
            def _():
                settle()

        if gather:

            @pl.when(s > 0)
            def _():
                gather.use_at(s - 1, gh, use)

        if fill:

            @pl.when((s >= 0) & (s < line.chips))
            def _():
                fill(s)

        return carry

    lax.fori_loop(0, line.chips + 2, slot, 0)


def mean_rows(values):
    return jnp.sum(values, axis=-1, keepdims=True) * (1.0 / values.shape[-1])


class Blocks:
    def __init__(self, line, count, pairs, sems):
        self.line, self.count, self.pairs, self.sems = line, count, pairs, sems

    def copy(self, i, index):
        src, dst = self.pairs[i]
        at = rows_at(index, self.count)
        return pltpu.make_async_copy(src.at[at], dst.at[at], self.sems.at[i, index])

    def send(self, i, chip, h):
        self.copy(i, h * self.line.chips + chip).start()

    def finish(self):
        def one(index, carry):
            for i in range(len(self.pairs)):
                self.copy(i, index).wait()
            return carry

        lax.fori_loop(0, 2 * self.line.chips, one, 0)


def call(kernel, outs, scratch, args, ident, cost=1, far_in=(), far_out=()):
    def space(i, far):
        return pl.BlockSpec(memory_space=pl.ANY if i in far else pltpu.VMEM)

    return pl.pallas_call(
        kernel,
        out_shape=outs,
        in_specs=[space(i, far_in) for i in range(len(args))],
        out_specs=[space(i, far_out) for i in range(len(outs))],
        scratch_shapes=scratch,
        cost_estimate=pl.CostEstimate(
            flops=cost * 10**9, transcendentals=0, bytes_accessed=cost * 3 * 10**6
        ),
        compiler_params=pltpu.CompilerParams(
            collective_id=ident, has_side_effects=True, vmem_limit_bytes=63 * 2**20
        ),
    )(*args)


def shape(dims, kind):
    return jax.ShapeDtypeStruct(dims, kind)


def gather_project(rows, codes, weights, ways, ident):
    tok, width = rows.shape
    cols = weights.shape[1] - HEAD_DIM
    half = tok // 2

    def kernel(
        rows_ref, code_ref, w_far, all_far, codes_ref, prod_far,
        w_ref, all_ref, prod_ref, w_sem, out_sem, code_send, code_recv, *sems
    ):
        line = Line(ways)
        w_copy = pltpu.make_async_copy(w_far.at[:, pl.ds(0, cols)], w_ref, w_sem)
        w_copy.start()
        outs = Blocks(line, 2 * half, [(all_ref, all_far), (prod_ref, prod_far)], out_sem)
        me = line.me
        barrier = pltpu.get_barrier_semaphore()
        for off in range(1, ways):
            pl.semaphore_signal(
                barrier, inc=1, device_id={"seq": (me + off) % ways}, device_id_type=MESH
            )
        pl.semaphore_wait(barrier, ways - 1)
        gather = RowGather(line, half, all_ref, sems)
        for h in (0, 1):
            all_ref[rows_at(h * ways + me, half), :] = rows_ref[pl.ds(h * half, half), :]
            gather.start(h)
        codes_ref[me] = code_ref[...]

        def tell(off):
            return remote(
                code_ref, codes_ref.at[me], code_send.at[off], code_recv.at[off], (me + off) % ways
            )

        for off in range(1, ways):
            tell(off).start()

        def use(chip, h):
            at = rows_at(h * line.chips + chip, 2 * half)

            prod_ref[at, :] = dot_nn(all_ref[at, :], w_ref[...])
            outs.send(0, chip, h)
            outs.send(1, chip, h)

        def step(j, carry):
            def one(h, carry):
                @pl.when(j < line.chips)
                def _():
                    gather.receive(j, h)

                gather.use_at(j - 1, h, use)
                return carry

            return lax.fori_loop(0, 2, one, carry)

        w_copy.wait()
        lax.fori_loop(1, line.chips + 1, step, 0)
        gather.finish()
        outs.finish()
        for off in range(1, ways):
            tell(off).wait()

    return call(
        kernel,
        [
            shape((ways * tok, width), bf16),
            shape((ways,) + codes.shape, jnp.int32),
            shape((ways * tok, cols), f32),
        ],
        [
            pltpu.VMEM((width, cols), bf16),
            pltpu.VMEM((ways * tok, width), bf16),
            pltpu.VMEM((ways * tok, cols), f32),
            pltpu.SemaphoreType.DMA,
            pltpu.SemaphoreType.DMA((2, ways)),
            pltpu.SemaphoreType.DMA((ways,)),
            pltpu.SemaphoreType.DMA((ways,)),
        ]
        + RowGather.scratch(ways // 2),
        [rows, codes, weights],
        ident,
        55,
        (2,),
        (0, 2),
    )


def attn_out_and_ff(attn_low, m_mid, p_down, token_rows, grad_out, gains, groups, ways, ident):
    tok, width = token_rows.shape
    half = tok // 2
    own_feat, own_ff = attn_low.shape[1], p_down.shape[1]
    part = p_down.shape[0]
    row = ways * tok
    tile = min(own_ff, 1024)
    square = width == 2 * own_ff
    square_tile = 256
    squares = width // square_tile

    def kernel(
        left_far, mid_far, down_far, x_far, go_far, gains_ref,
        branch_far, out_ref, gg_ref, hid_far, mix_far, gm_far, dgu_far, first_ref,
        left, mid_ref, down_ref, x_ref, go_ref, branch_ref, hid_ref, mix_ref, gm_ref, dgu_ref,
        down_turned, in_sem, out_sem, branch_sem, down_send, down_recv, *rest
    ):
        line = Line(ways)
        group = lax.axis_index("dp")
        gu_cols, out_cols = pl.ds(0, 2 * own_ff), pl.ds(2 * own_ff, own_feat)
        fetch = [
            pltpu.make_async_copy(src, dst, in_sem.at[i])
            for i, (src, dst) in enumerate(
                [
                    (left_far, left),
                    (mid_far.at[:, out_cols], mid_ref.at[:, out_cols]),
                    (x_far, x_ref),
                    (mid_far.at[:, gu_cols], mid_ref.at[:, gu_cols]),
                    (down_far, down_ref.at[rows_at(group, part)]),
                    (go_far, go_ref),
                ]
            )
        ]
        for copy in fetch:
            copy.start()
        outs = Blocks(
            line,
            2 * half,
            [(hid_ref, hid_far), (mix_ref, mix_far), (gm_ref, gm_far), (dgu_ref, dgu_far)],
            out_sem,
        )
        keep_branch = pltpu.make_async_copy(branch_ref, branch_far, branch_sem)
        line.greet(groups)

        def spread(off):
            return pltpu.make_async_remote_copy(
                src_ref=down_far,
                dst_ref=down_ref.at[rows_at(group, part)],
                send_sem=down_send.at[off],
                recv_sem=down_recv.at[off],
                device_id={"dp": (group + off) % groups},
                device_id_type=MESH,
            )

        for off in range(1, groups):
            spread(off).start()
        scatter = RowScatter(line, half, rest[:3], rest[3:7])
        hidden = RowGather(line, half, hid_ref, rest[7:12])
        back = RowGather(line, half, gm_ref, rest[12:17])
        gg_ref[...] = jnp.zeros_like(gg_ref)
        gain_attn, gain_mlp = gains_ref[2:3, :], gains_ref[3:4, :]

        def own(h, strip):
            return pl.ds(pl.multiple_of((h * ways + line.me) * half + strip.start, 16), strip.size)

        def residual(at):
            branch = branch_ref[at, :]
            factor = lax.rsqrt(mean_rows(branch * branch) + norm_eps)
            return x_ref[at, :].astype(f32) + branch * factor * gain_attn

        def settle_attn(h):
            def one(strip):
                at = pl.ds(pl.multiple_of(h * half + strip.start, 16), strip.size)
                branch_ref[at, :] = scatter.total(h, strip)
                hid_ref[own(h, strip), :] = residual(at).astype(bf16)

            scatter.close(h)
            each_strip(half, 16, one)
            hidden.start(h)
            scatter.finish(h)

        def settle_mlp(h):
            def one(strip):
                at = pl.ds(pl.multiple_of(h * half + strip.start, 16), strip.size)
                mlp = scatter.total(h, strip)
                factor = lax.rsqrt(mean_rows(mlp * mlp) + norm_eps)
                unit = mlp * factor
                lifted = go_ref[at, :].astype(f32) * gain_mlp
                turned = factor * (lifted - unit * mean_rows(lifted * unit))
                gm_ref[own(h, strip), :] = turned.astype(bf16)

            def rest_of(strip):
                at = pl.ds(pl.multiple_of(h * half + strip.start, 16), strip.size)
                mlp = scatter.total(h, strip)
                unit = mlp * lax.rsqrt(mean_rows(mlp * mlp) + norm_eps)
                out_ref[at, :] = (residual(at) + unit * gain_mlp).astype(bf16)
                terms = go_ref[at, :].astype(f32) * unit
                gg_ref[...] += terms[:8] + terms[8:]

            scatter.close(h)
            each_strip(half, 16, one)
            back.start(h)
            each_strip(half, 16, rest_of)
            scatter.finish(h)

        def gate_up(chip, h):
            at = rows_at(h * line.chips + chip, 2 * half)

            outs.send(0, chip, h)

            both = dot_nn(hid_ref[at, :], mid_ref[:, gu_cols])
            gate, up = both[:, :own_ff], both[:, own_ff:]
            dgu_ref[at, :] = both.astype(bf16)
            mix_ref[at, :] = (gate * jax.nn.sigmoid(gate) * up).astype(bf16)
            outs.send(1, chip, h)

        def gate_up_back(chip, h):
            at = rows_at(h * line.chips + chip, 2 * half)

            outs.send(2, chip, h)

            def one(n, carry):
                here, there = rows_at(n, tile), pl.ds(pl.multiple_of(own_ff + n * tile, tile), tile)
                grad = dot_nn(gm_ref[at, :], down_ref[:, here])
                gate, up = dgu_ref[at, here].astype(f32), dgu_ref[at, there].astype(f32)
                sigma = jax.nn.sigmoid(gate)
                dgu_ref[at, here] = (grad * up * sigma * (1.0 + gate * (1.0 - sigma))).astype(bf16)
                dgu_ref[at, there] = (grad * gate * sigma).astype(bf16)
                return carry

            lax.fori_loop(0, own_ff // tile, one, 0)
            outs.send(3, chip, h)

        for copy in fetch[:3]:
            copy.wait()
        scatter.of(left, mid_ref.at[:, out_cols], 1024, True)
        advance(scatter, 0, settle=lambda: settle_attn(0))
        fetch[3].wait()
        advance(scatter, 1, hidden, 0, gate_up, settle=lambda: settle_attn(1))

        def turn_down(i, carry):
            rows = rows_at(i, square_tile)
            down_turned[:, rows] = down_ref[rows, :].T
            return carry

        def turn_square(s):
            def one(i, carry):
                def two(j, carry):
                    rows, cols = rows_at(i, square_tile), rows_at(j, square_tile)
                    block, other = mid_ref[rows, cols], mid_ref[cols, rows]
                    mid_ref[cols, rows] = block.T
                    mid_ref[rows, cols] = other.T
                    return carry

                return lax.fori_loop(i, squares, two, carry)

            lax.fori_loop(s * squares // line.chips, (s + 1) * squares // line.chips, one, 0)

        keep_branch.start()
        for copy in fetch[4:]:
            copy.wait()
        for off in range(1, groups):
            spread(off).wait()
        if square:
            lax.fori_loop(0, squares, turn_down, 0)
            scatter.of(mix_ref, down_turned, 2048, False, True)
        else:
            scatter.of(mix_ref, down_ref, 2048, False)
        advance(scatter, 0, hidden, 1, gate_up, settle=lambda: settle_mlp(0))
        advance(
            scatter, 1, back, 0, gate_up_back, turn_square if square else None, lambda: settle_mlp(1)
        )
        scatter.of(dgu_ref, mid_ref.at[:, gu_cols], 1024, False, square)

        def keep_first():
            def put(strip):
                first_ref[strip, :] = scatter.total(0, strip)

            scatter.close(0)
            each_strip(half, 16, put)
            scatter.finish(0)

        advance(scatter, 0, back, 1, gate_up_back, settle=keep_first)
        hidden.finish()
        back.finish()
        keep_branch.wait()
        outs.finish()

    return call(
        kernel,
        [
            shape((tok, width), f32),
            shape((tok, width), bf16),
            shape((8, width), f32),
            shape((row, width), bf16),
            shape((row, own_ff), bf16),
            shape((row, width), bf16),
            shape((row, 2 * own_ff), bf16),
            shape((half, width), f32),
        ],
        [
            pltpu.VMEM((row, own_feat), bf16),
            pltpu.VMEM(m_mid.shape, bf16),
            pltpu.VMEM((groups * part, own_ff), bf16),
            pltpu.VMEM((tok, width), bf16),
            pltpu.VMEM((tok, width), bf16),
            pltpu.VMEM((tok, width), f32),
            pltpu.VMEM((row, width), bf16),
            pltpu.VMEM((row, own_ff), bf16),
            pltpu.VMEM((row, width), bf16),
            pltpu.VMEM((row, 2 * own_ff), bf16),
            pltpu.VMEM((own_ff, width) if square else (16, HEAD_DIM), bf16),
            pltpu.SemaphoreType.DMA((6,)),
            pltpu.SemaphoreType.DMA((4, ways)),
            pltpu.SemaphoreType.DMA,
            pltpu.SemaphoreType.DMA((groups,)),
            pltpu.SemaphoreType.DMA((groups,)),
        ]
        + RowScatter.scratch(ways // 2, tok, width)
        + RowGather.scratch(ways // 2)
        + RowGather.scratch(ways // 2),
        [attn_low, m_mid, p_down, token_rows, grad_out, gains],
        ident,
        150,
        range(5),
        (0, 3, 4, 5, 6),
    )


def ff_to_attn_back(
    grad_gu, first_half, m_mid, branch, grad_out, gain_row, grad_mlp, mixed_low, ways, ident
):
    tok, width = branch.shape
    half = tok // 2
    own_ff = grad_gu.shape[1] // 2
    own_feat = m_mid.shape[1] - 2 * own_ff
    row = ways * tok
    tiles = width // 256

    def kernel(
        left, first_ref, w_ref, br_ref, go_ref, gain_ref, gm_far, mix_far,
        gh_ref, gg_ref, all_far, ga_ref, dd_far,
        all_ref, out_sem, gm_ref, mix_ref, dd_ref, gm_sem, mix_sem, dd_sem, *rest
    ):
        line = Line(ways)
        mix_copy = pltpu.make_async_copy(mix_far, mix_ref, mix_sem)

        def fetch(i):
            return pltpu.make_async_copy(
                gm_far.at[:, rows_at(i, 256)], gm_ref.at[i % 2], gm_sem.at[i % 2]
            )

        def keep(i):
            rows = rows_at(i, 256)
            return pltpu.make_async_copy(dd_ref.at[rows], dd_far.at[rows], dd_sem.at[i])

        def down_grad(i, carry):
            fetch(i).wait()

            @pl.when(i + 1 < tiles)
            def _():
                fetch(i + 1).start()

            dd_ref[rows_at(i, 256), :] = dot_tn(gm_ref[i % 2], mix_ref[...]).astype(bf16)
            keep(i).start()
            return carry

        def fill(s):
            lax.fori_loop(s * tiles // line.chips, (s + 1) * tiles // line.chips, down_grad, 0)

        outs = Blocks(line, 2 * half, [(all_ref, all_far)], out_sem)
        line.greet()
        scatter = RowScatter(line, half, rest[:3], rest[3:7])
        gather = RowGather(line, half, all_ref, rest[7:])
        gg_ref[...] = jnp.zeros_like(gg_ref)

        def settle(h):
            def one(strip):
                at = pl.ds(pl.multiple_of(h * half + strip.start, 16), strip.size)
                mine = pl.ds(
                    pl.multiple_of((h * ways + line.me) * half + strip.start, 16), strip.size
                )
                total = scatter.total(h, strip) if h else first_ref[strip, :]
                grad = total + go_ref[at, :].astype(f32)
                branch = br_ref[at, :]
                factor = lax.rsqrt(mean_rows(branch * branch) + norm_eps)
                unit = branch * factor
                gh_ref[at, :] = grad
                terms = grad * unit
                gg_ref[...] += terms[:8] + terms[8:]
                lifted = grad * gain_ref[...]
                turned = factor * (lifted - unit * mean_rows(lifted * unit))
                all_ref[mine, :] = turned.astype(bf16)

            if h:
                scatter.close(h)
            each_strip(half, 16, one)
            gather.start(h)

        def use(chip, h):
            at = rows_at(h * line.chips + chip, 2 * half)
            outs.send(0, chip, h)
            ga_ref[at, :] = dot_nn(all_ref[at, :], w_ref[:, pl.ds(2 * own_ff, own_feat)])

        scatter.of(left, w_ref.at[:, pl.ds(0, 2 * own_ff)], 1024, False)
        settle(0)
        advance(scatter, 1, gather, 0, use, settle=lambda: settle(1))
        mix_copy.start()
        fetch(0).start()
        mix_copy.wait()
        advance(None, 0, gather, 1, use, fill)
        gather.finish()
        outs.finish()
        for i in range(tiles):
            keep(i).wait()
        scatter.finish(1)

    return call(
        kernel,
        [
            shape((tok, width), f32),
            shape((8, width), f32),
            shape((row, width), bf16),
            shape((row, own_feat), f32),
            shape((width, own_ff), bf16),
        ],
        [
            pltpu.VMEM((row, width), bf16),
            pltpu.SemaphoreType.DMA((1, ways)),
            pltpu.VMEM((2, row, 256), bf16),
            pltpu.VMEM((row, own_ff), bf16),
            pltpu.VMEM((width, own_ff), bf16),
            pltpu.SemaphoreType.DMA((2,)),
            pltpu.SemaphoreType.DMA,
            pltpu.SemaphoreType.DMA((tiles,)),
        ]
        + RowScatter.scratch(ways // 2, tok, width)
        + RowGather.scratch(ways // 2),
        [grad_gu, first_half, m_mid, branch, grad_out, gain_row, grad_mlp, mixed_low],
        ident,
        70,
        (6, 7),
        (2, 4),
    )


def home_copies(me, ways, source, targets, widths, send, recv):
    rows = source.shape[0] // ways
    begins = [sum(widths[:i]) for i in range(len(widths))]
    count = len(widths)

    def part(i, dest):
        return (
            source.at[rows_at(dest, rows), pl.ds(begins[i], widths[i])],
            targets[i].at[:, rows_at(me, widths[i])],
        )

    def move(off, i):
        dest = (me + off) % ways
        return remote(*part(i, dest), send.at[off * count + i], recv.at[off * count + i], dest)

    def keep(i):
        return pltpu.make_async_copy(*part(i, me), send.at[i])

    def each(what):
        def one(off, carry):
            for i in range(count):
                what(move(off, i))
            return carry

        lax.fori_loop(1, ways, one, 0)

    def start():
        for i in range(count):
            keep(i).start()
        each(lambda copy: copy.start())

    def wait():
        for i in range(count):
            keep(i).wait()
        each(lambda copy: copy.wait())

    return start, wait


def greet_line(me, ways):
    barrier = pltpu.get_barrier_semaphore()

    def greet(off, carry):
        pl.semaphore_signal(
            barrier, inc=1, device_id={"seq": (me + off) % ways}, device_id_type=MESH
        )
        return carry

    lax.fori_loop(1, ways, greet, 0)
    pl.semaphore_wait(barrier, ways - 1)


def bring_home(summed, widths, ways, ident):
    rows = summed.shape[0] // ways
    count = len(widths)

    def kernel(*refs):
        source, targets, (send, recv) = refs[0], refs[1 : 1 + count], refs[1 + count :]
        me = lax.axis_index("seq")
        greet_line(me, ways)
        start, wait = home_copies(me, ways, source, targets, widths, send, recv)
        start()
        wait()

    return call(
        kernel,
        [shape((rows, ways * width), bf16) for width in widths],
        [pltpu.SemaphoreType.DMA((ways * count,))] * 2,
        [summed],
        ident,
        30,
        (0,),
        range(count),
    )


def project_back(grad_qkv, m_qkv, grad_hidden, d_down, ways, ident):
    tok, width = grad_hidden.shape
    half = tok // 2
    own_ff = d_down.shape[1]

    def kernel(left, w_ref, gh_ref, dd_ref, out_ref, home_ref, dd_send, dd_recv, *rest):
        line = Line(ways)
        greet_line(line.me, ways)
        start, wait = home_copies(line.me, ways, dd_ref, [home_ref], [own_ff], dd_send, dd_recv)
        start()
        scatter = RowScatter(line, half, rest[:3], rest[3:7])
        scatter.of(left, w_ref.at[:, pl.ds(0, left.shape[1])], 1024, True)
        for h in (0, 1):
            advance(scatter, h)
        for h in (0, 1):

            def one(strip, h=h):
                at = pl.ds(pl.multiple_of(h * half + strip.start, 16), strip.size)
                out_ref[at, :] = (gh_ref[at, :] + scatter.total(h, strip)).astype(bf16)

            scatter.close(h)
            each_strip(half, 16, one)
        for h in (0, 1):
            scatter.finish(h)
        wait()

    return call(
        kernel,
        [
            shape((tok, width), bf16),
            shape((d_down.shape[0] // ways, ways * own_ff), bf16),
        ],
        [pltpu.SemaphoreType.DMA((ways,))] * 2 + RowScatter.scratch(ways // 2, tok, width),
        [grad_qkv, m_qkv, grad_hidden, d_down],
        ident,
        65,
        (3,),
        (1,),
    )


def half_turn(values, sign):
    half_dim = HEAD_DIM // 2
    lane = lax.broadcasted_iota(jnp.int32, values.shape, 1)
    swapped = pltpu.roll(values, half_dim, 1)
    return jnp.where(lane < half_dim, -sign * swapped, sign * swapped)


def attend(parts, block):
    row = parts[0].shape[0]
    width = parts[0].shape[1] // 3
    heads = width // HEAD_DIM
    scale = HEAD_DIM ** (-0.5)

    def kernel(
        qkv_ref, factor_ref, cos_ref, sin_ref, gain_ref, qpos_ref, kpos_ref, kmax_ref,
        q_ref, k_ref, v_ref, at_ref, low_ref, ws_ref
    ):
        def turn(i, carry):
            rows = rows_at(i, block)
            cosine, sine = cos_ref[rows, :], sin_ref[rows, :]
            for which, out_ref in ((0, q_ref), (1, k_ref)):
                factor = factor_ref[rows, pl.ds(which, 1)]
                for head in range(heads):
                    lanes = pl.ds(head * HEAD_DIM, HEAD_DIM)
                    raw = qkv_ref[rows, pl.ds(which * width + head * HEAD_DIM, HEAD_DIM)]
                    normed = raw * factor * gain_ref[which : which + 1, lanes]
                    out_ref[rows, lanes] = (
                        normed * cosine + half_turn(normed, 1.0) * sine
                    ).astype(bf16)
            v_ref[rows, :] = qkv_ref[rows, pl.ds(2 * width, width)].astype(bf16)
            return carry

        lax.fori_loop(0, row // block, turn, 0)

        def one(i, carry):
            rows = rows_at(i, block)
            qpos = qpos_ref[rows, :]
            mask = (kpos_ref[...] <= qpos) & (qpos <= kmax_ref[...])
            for head in range(heads):
                lanes = pl.ds(head * HEAD_DIM, HEAD_DIM)
                scores = dot_nt(q_ref[rows, lanes], k_ref[:, lanes]) * (scale * LOG2_E)
                expo = jnp.where(mask, jnp.exp2(scores), 0.0)
                total = jnp.sum(expo, axis=-1, keepdims=True)
                result = dot_nn(expo.astype(bf16), v_ref[:, lanes]) / total
                ws_ref[rows, pl.ds(head, 1)] = total
                at_ref[rows, lanes] = result
                low_ref[rows, lanes] = result.astype(bf16)
            return carry

        lax.fori_loop(0, row // block, one, 0)

    return pl.pallas_call(
        kernel,
        out_shape=[shape((row, width), bf16)] * 3
        + [shape((row, width), f32), shape((row, width), bf16), shape((row, heads), f32)],
        in_specs=[pl.BlockSpec(memory_space=pltpu.VMEM)] * len(parts),
        out_specs=[pl.BlockSpec(memory_space=pltpu.VMEM)] * 6,
        cost_estimate=pl.CostEstimate(
            flops=4 * row * row * width, transcendentals=row * row * heads, bytes_accessed=60 * 10**6
        ),
        compiler_params=pltpu.CompilerParams(vmem_limit_bytes=60 * 2**20),
    )(*parts)


def attend_back(parts, summed, block, ways, ident):
    row, width = parts[0].shape
    heads = width // HEAD_DIM
    scale = HEAD_DIM ** (-0.5)

    def kernel(
        q_ref, k_ref, v_ref, ga_ref, at_ref, ws_ref, cos_ref, sin_ref, qkv_ref, factor_ref,
        gain_ref, qpos_ref, kpos_ref, kmax_ref, sum_ref,
        cq_ref, ck_ref, dv_ref, terms_ref, gg_ref, home_ref, dk_acc, dv_acc, send, recv
    ):
        me = lax.axis_index("seq")
        greet_line(me, ways)
        start, wait = home_copies(me, ways, sum_ref, [home_ref], [summed.shape[1]], send, recv)
        start()
        gg_ref[...] = jnp.zeros_like(gg_ref)
        dk_acc[...] = jnp.zeros_like(dk_acc)
        dv_acc[...] = jnp.zeros_like(dv_acc)

        def turn_back(grad, rows, which, out_ref, head):
            lanes = pl.ds(head * HEAD_DIM, HEAD_DIM)
            cosine, sine = cos_ref[rows, :], sin_ref[rows, :]
            normed = grad * cosine + half_turn(grad * sine, -1.0)
            raw = qkv_ref[rows, pl.ds(which * width + head * HEAD_DIM, HEAD_DIM)]
            unit = raw * factor_ref[rows, pl.ds(which, 1)]
            gg_ref[which : which + 1, lanes] += jnp.sum(normed * unit, axis=0, keepdims=True)
            lifted = normed * gain_ref[which : which + 1, lanes]
            out_ref[rows, lanes] = lifted
            term = jnp.sum(lifted * unit, axis=-1, keepdims=True)
            column = pl.ds(which, 1)
            if head == 0:
                terms_ref[rows, column] = term
            else:
                terms_ref[rows, column] += term

        def one(i, carry):
            rows = rows_at(i, block)
            qpos = qpos_ref[rows, :]
            mask = (kpos_ref[...] <= qpos) & (qpos <= kmax_ref[...])
            for head in range(heads):
                lanes = pl.ds(head * HEAD_DIM, HEAD_DIM)
                grad = ga_ref[rows, lanes]
                inverse = 1.0 / ws_ref[rows, pl.ds(head, 1)]
                drop = jnp.sum(grad * at_ref[rows, lanes], axis=-1, keepdims=True) * inverse
                grad_num = (grad * inverse).astype(bf16)
                query, keys = q_ref[rows, lanes], k_ref[:, lanes]
                scores = dot_nt(query, keys) * (scale * LOG2_E)
                expo = jnp.where(mask, jnp.exp2(scores), 0.0)
                grad_expo = dot_nt(grad_num, v_ref[:, lanes])
                grad_scores = (expo * (grad_expo - drop)).astype(bf16)
                turn_back(dot_nn(grad_scores, keys) * scale, rows, 0, cq_ref, head)
                dk_acc[:, lanes] += dot_tn(grad_scores, query)
                dv_acc[:, lanes] += dot_tn(expo.astype(bf16), grad_num)
            return carry

        lax.fori_loop(0, row // block, one, 0)

        def last(i, carry):
            rows = rows_at(i, block)
            for head in range(heads):
                lanes = pl.ds(head * HEAD_DIM, HEAD_DIM)
                turn_back(dk_acc[rows, lanes] * scale, rows, 1, ck_ref, head)
                dv_ref[rows, lanes] = dv_acc[rows, lanes].astype(bf16)
            return carry

        lax.fori_loop(0, row // block, last, 0)
        wait()

    return call(
        kernel,
        [
            shape((row, width), f32),
            shape((row, width), f32),
            shape((row, width), bf16),
            shape((row, 2), f32),
            shape((2, width), f32),
            shape((summed.shape[0] // ways, ways * summed.shape[1]), bf16),
        ],
        [pltpu.VMEM((row, width), f32)] * 2 + [pltpu.SemaphoreType.DMA((ways,))] * 2,
        list(parts) + [summed],
        ident,
        25,
        (len(parts),),
        (5,),
    )


def attn_grads(x_row, grad_qkv, grad_branch, attn_low, gain_columns, summed, ways, ident):
    row, width = x_row.shape
    first, second = grad_qkv.shape[1], attn_low.shape[1]
    cols = first + second + gain_columns.shape[1]

    def kernel(
        x_far, dq_ref, gb_far, low_ref, gain_ref, sum_ref, out_far, home_ref,
        x_ref, gb_ref, out_ref, in_sem, out_sem, send, recv
    ):
        me = lax.axis_index("seq")
        fetch = [
            pltpu.make_async_copy(x_far, x_ref, in_sem.at[0]),
            pltpu.make_async_copy(gb_far, gb_ref, in_sem.at[1]),
        ]
        for copy in fetch:
            copy.start()
        greet_line(me, ways)
        start, wait = home_copies(me, ways, sum_ref, [home_ref], [summed.shape[1]], send, recv)
        start()
        for copy in fetch:
            copy.wait()
        tile = 256

        def keep(i):
            rows = rows_at(i, tile)
            return pltpu.make_async_copy(out_ref.at[rows], out_far.at[rows], out_sem.at[i])

        def one(i, carry):
            rows = rows_at(i, tile)
            out_ref[rows, pl.ds(0, first)] = dot_tn(x_ref[:, rows], dq_ref[...]).astype(bf16)
            out_ref[rows, pl.ds(first, second)] = dot_tn(gb_ref[:, rows], low_ref[...]).astype(bf16)
            out_ref[rows, pl.ds(first + second, gain_columns.shape[1])] = gain_ref[rows, :]
            keep(i).start()
            return carry

        lax.fori_loop(0, width // tile, one, 0)

        def kept(i, carry):
            keep(i).wait()
            return carry

        lax.fori_loop(0, width // tile, kept, 0)
        wait()

    return call(
        kernel,
        [
            shape((width, cols), bf16),
            shape((summed.shape[0] // ways, ways * summed.shape[1]), bf16),
        ],
        [
            pltpu.VMEM((row, width), bf16),
            pltpu.VMEM((row, width), bf16),
            pltpu.VMEM((width, cols), bf16),
            pltpu.SemaphoreType.DMA((2,)),
            pltpu.SemaphoreType.DMA((width // 256,)),
            pltpu.SemaphoreType.DMA((ways,)),
            pltpu.SemaphoreType.DMA((ways,)),
        ],
        [x_row, grad_qkv, grad_branch, attn_low, gain_columns, summed],
        ident,
        25,
        (0, 2, 5),
        (0, 1),
    )


def exchange(sources, ways, ident, cost):
    rows = sources[0].shape[0]
    widths = [a.shape[1] // ways for a in sources]
    begins = [sum(widths[:i]) for i in range(len(widths))]
    count = len(sources)

    def kernel(*refs):
        ins, out_ref, send, recv, local = refs[:count], *refs[count:]
        me = lax.axis_index("seq")
        barrier = pltpu.get_barrier_semaphore()

        def greet(off, carry):
            pl.semaphore_signal(
                barrier, inc=1, device_id={"seq": (me + off) % ways}, device_id_type=MESH
            )
            return carry

        def move(off, i):
            dest = (me + off) % ways
            return remote(
                ins[i].at[:, rows_at(dest, widths[i])],
                out_ref.at[rows_at(me, rows), pl.ds(begins[i], widths[i])],
                send.at[off * count + i],
                recv.at[off * count + i],
                dest,
            )

        def keep(i):
            return pltpu.make_async_copy(
                ins[i].at[:, rows_at(me, widths[i])],
                out_ref.at[rows_at(me, rows), pl.ds(begins[i], widths[i])],
                local.at[i],
            )

        def each(what):
            def one(off, carry):
                for i in range(count):
                    what(move(off, i))
                return carry

            lax.fori_loop(1, ways, one, 0)

        for i in range(count):
            keep(i).start()
        lax.fori_loop(1, ways, greet, 0)
        pl.semaphore_wait(barrier, ways - 1)
        each(lambda copy: copy.start())
        for i in range(count):
            keep(i).wait()
        each(lambda copy: copy.wait())

    return pl.pallas_call(
        kernel,
        out_shape=shape((ways * rows, sum(widths)), bf16),
        in_specs=[pl.BlockSpec(memory_space=pl.ANY)] * count,
        out_specs=pl.BlockSpec(memory_space=pl.ANY),
        scratch_shapes=[
            pltpu.SemaphoreType.DMA((ways * count,)),
            pltpu.SemaphoreType.DMA((ways * count,)),
            pltpu.SemaphoreType.DMA((count,)),
        ],
        cost_estimate=pl.CostEstimate(
            flops=cost * 10**9, transcendentals=0, bytes_accessed=cost * 3 * 10**6
        ),
        compiler_params=pltpu.CompilerParams(collective_id=ident, has_side_effects=True),
    )(*sources)


def finish_grads(grads, kept, gains, ways):
    rows, count = gains.shape[0], len(grads)
    parts = list(grads) + list(kept) + [gains]

    def kernel(*refs):
        ins, outs = refs[: len(parts)], refs[len(parts) :]
        for i in range(len(parts) - 1):
            outs[i][...] = ins[i][...].astype(outs[i].dtype)
        total = ins[-1][:, pl.ds(0, HEAD_DIM)].astype(f32)
        for off in range(1, ways):
            total = total + ins[-1][:, pl.ds(off * HEAD_DIM, HEAD_DIM)].astype(f32)
        outs[-1][...] = total.T[:8, :]

    return pl.pallas_call(
        kernel,
        out_shape=[shape(part.shape, f32 if i < count else part.dtype) for i, part in enumerate(parts[:-1])]
        + [shape((8, rows), f32)],
        in_specs=[pl.BlockSpec(memory_space=pltpu.VMEM)] * len(parts),
        out_specs=[pl.BlockSpec(memory_space=pltpu.VMEM)] * len(parts),
        cost_estimate=pl.CostEstimate(flops=10**6, transcendentals=0, bytes_accessed=10**7),
        compiler_params=pltpu.CompilerParams(vmem_limit_bytes=60 * 2**20),
    )(*parts)


def line_sum(terms, ways, ident):
    def kernel(terms_ref, out_ref, slots, send, recv):
        me = lax.axis_index("seq")
        barrier = pltpu.get_barrier_semaphore()
        for off in range(1, ways):
            pl.semaphore_signal(
                barrier, inc=1, device_id={"seq": (me + off) % ways}, device_id_type=MESH
            )
        pl.semaphore_wait(barrier, ways - 1)
        for off in range(1, ways):
            remote(
                terms_ref, slots.at[off], send.at[off], recv.at[off], (me + off) % ways
            ).start()
        total = terms_ref[...]
        for off in range(1, ways):
            remote(terms_ref, slots.at[off], send.at[off], recv.at[off], (me + off) % ways).wait_recv()
            total = total + slots[off]
        out_ref[...] = total
        for off in range(1, ways):
            remote(terms_ref, slots.at[off], send.at[off], recv.at[off], (me + off) % ways).wait_send()

    return call(
        kernel,
        [shape(terms.shape, f32)],
        [
            pltpu.VMEM((ways,) + terms.shape, f32),
            pltpu.SemaphoreType.DMA((ways,)),
            pltpu.SemaphoreType.DMA((ways,)),
        ],
        [terms],
        ident,
        8,
    )[0]


def body(
    tokens,
    w_query,
    w_key,
    w_value,
    w_out,
    w_gate,
    w_up,
    w_down,
    gain_query,
    gain_key,
    gain_attn,
    gain_mlp,
    cotangent,
    key_mask,
    lengths,
    tract_order,
):
    ways, groups = lax.axis_size("seq"), lax.axis_size("dp")
    me = lax.axis_index("seq")
    token_rows = tokens[0]
    tok_count, feat_width = token_rows.shape
    ff_width = w_gate.shape[1]
    own_feat = feat_width // ways
    own_heads = own_feat // HEAD_DIM
    own_ff = ff_width // ways
    row_len = tok_count * ways
    score_scale = HEAD_DIM ** (-0.5)
    half_len = tok_count // 2
    order_pair = tract_order[0]
    slot_index = jnp.arange(tok_count, dtype=jnp.int32)
    local_pos = (
        jnp.where(slot_index < half_len, order_pair[0], order_pair[1]) * half_len
        + slot_index % half_len
    )
    key_ok = ((key_mask[0] == 1) & (local_pos < lengths[0])).astype(jnp.int32)

    gain_local = jnp.stack([gain_query, gain_key, gain_attn, gain_mlp], axis=1)
    gain_pad = jnp.pad(gain_local, ((0, 0), (0, HEAD_DIM - 4)))
    gain_all = jnp.tile(gain_pad, (1, ways))
    p_qkv = exchange([w_query, w_key, w_value, gain_all], ways, 8, 20)
    m_qkv = across(p_qkv)
    p_qkv, w_gate, w_up, w_out_t = lax.optimization_barrier(
        (p_qkv, w_gate, w_up, jnp.transpose(w_out))
    )
    p_mid = exchange([w_gate, w_up, w_out_t], ways, 10, 50)
    m_mid = across(p_mid)
    gains = dot_nt(jnp.eye(8, HEAD_DIM, dtype=bf16), m_qkv[:, 3 * own_feat :])
    gain_q = lax.dynamic_slice_in_dim(gains[0], me * own_feat, own_feat, 0)
    gain_k = lax.dynamic_slice_in_dim(gains[1], me * own_feat, own_feat, 0)

    code_pad = -tok_count % HEAD_DIM
    local_code = jnp.pad(local_pos * 2 + key_ok, (0, code_pad))[None]
    local_code, p_mid = lax.optimization_barrier((local_code, p_mid))
    x_row, codes, qkv = gather_project(token_rows, local_code, m_qkv, ways, 1)
    key_code = codes[:, 0, :tok_count].reshape(ways, 2, half_len)
    key_code = jnp.transpose(key_code, (1, 0, 2)).reshape(row_len)
    pos = key_code // 2
    q_raw, k_raw, v_raw = (qkv[:, i * own_feat : (i + 1) * own_feat] for i in range(3))
    squares = line_sum(
        jnp.stack([jnp.sum(q_raw * q_raw, axis=-1), jnp.sum(k_raw * k_raw, axis=-1)]), ways, 2
    )
    squares, w_down_t = lax.optimization_barrier((squares, jnp.transpose(w_down)))
    p_down = lax.all_to_all(w_down_t, "seq", split_axis=1, concat_axis=0, tiled=True)
    factors = jnp.transpose(lax.rsqrt(squares / feat_width + norm_eps))
    cosine, sine = rope_tables(pos, HEAD_DIM)
    key_most = jnp.where(key_code % 2 == 1, jnp.int32(2**30), pos)
    places = [pos[:, None], pos[None], key_most[None]]
    gain_qk = jnp.stack([gain_q, gain_k])
    query_low, key_low, value_low, attn, attn_low, weight_sum = attend(
        [qkv, factors, cosine, sine, gain_qk] + places, min(row_len, 160)
    )

    branch, layer_out, grad_gain_mlp, hidden_low, mixed_low, grad_mlp, grad_gu, first_half = (
        attn_out_and_ff(
            attn_low, m_mid, p_down, token_rows, cotangent[0], gains, groups, ways, 3
        )
    )
    d_gate = dot_tn(hidden_low, grad_gu[:, :own_ff]).astype(bf16)
    grad_gu, d_gate = lax.optimization_barrier((grad_gu, d_gate))
    d_up = dot_tn(hidden_low, grad_gu[:, own_ff:]).astype(bf16)
    grad_gu, d_up = lax.optimization_barrier((grad_gu, d_up))
    d_gate, d_up = dp_sum(d_gate), dp_sum(d_up)
    grad_hidden, grad_gain_attn, grad_branch, grad_attn, d_down = ff_to_attn_back(
        grad_gu, first_half, m_mid, branch, cotangent[0], gains[2:3], grad_mlp, mixed_low, ways, 5
    )
    d_down = dp_sum(d_down)
    c_q, c_k, grad_v, terms, gain_part, dw_gate = attend_back(
        [query_low, key_low, value_low, grad_attn, attn, weight_sum]
        + [cosine, sine, qkv, factors, gain_qk]
        + places,
        d_gate,
        min(row_len, 160),
        ways,
        13,
    )
    terms = jnp.transpose(terms)
    means = line_sum(terms, ways, 6) / feat_width
    q_factor, k_factor = factors[:, :1], factors[:, 1:]
    grad_q_raw = q_factor * (c_q - q_raw * q_factor * means[0][:, None])
    grad_k_raw = k_factor * (c_k - k_raw * k_factor * means[1][:, None])
    grad_qkv = jnp.concatenate(
        [grad_q_raw.astype(bf16), grad_k_raw.astype(bf16), grad_v], axis=1
    )

    own_slot = jnp.zeros((2, feat_width), f32)
    own_slot = lax.dynamic_update_slice(own_slot, gain_part, (0, me * own_feat))
    gain_terms = jnp.concatenate(
        [
            own_slot,
            jnp.sum(grad_gain_attn, axis=0, keepdims=True),
            jnp.sum(grad_gain_mlp, axis=0, keepdims=True),
        ]
    )
    gain_columns = jnp.pad(jnp.transpose(gain_terms), ((0, 0), (0, HEAD_DIM - 4)))
    d_attn, dw_up = attn_grads(
        x_row, grad_qkv, grad_branch, attn_low, gain_columns.astype(bf16), d_up, ways, 14
    )
    dw_gu = [dw_gate.astype(f32), dw_up.astype(f32)]
    grad_qkv, d_attn, dw_gu = lax.optimization_barrier((grad_qkv, d_attn, dw_gu))
    grad_tokens, dw_down = project_back(grad_qkv, m_qkv, grad_hidden, d_down, ways, 7)
    grad_tokens, d_attn = lax.optimization_barrier((grad_tokens, dp_sum(d_attn)))
    dw_gu = [dw_gate.astype(f32), dw_up.astype(f32)]
    dw_qkv = bring_home(d_attn, [own_feat] * 4 + [HEAD_DIM], ways, 12)
    d_query, d_key, d_value, d_out, d_down, layer_out, grad_tokens, gain_grads = finish_grads(
        list(dw_qkv[:4]) + [dw_down], [layer_out, grad_tokens], dw_qkv[4], ways
    )
    return (
        layer_out[None],
        grad_tokens[None],
        d_query,
        d_key,
        d_value,
        jnp.transpose(d_out),
        dw_gu[0],
        dw_gu[1],
        jnp.transpose(d_down),
        gain_grads[0],
        gain_grads[1],
        gain_grads[2],
        gain_grads[3],
    )


def solution(mesh):
    both = ("dp", "seq")
    in_specs = (
        P("dp", "seq", None),
        P(both, None),
        P(both, None),
        P(both, None),
        P(None, both),
        P(both, None),
        P(both, None),
        P(None, both),
        P(both),
        P(both),
        P(both),
        P(both),
        P("dp", "seq", None),
        P("dp", "seq"),
        P("dp"),
        P("dp", "seq"),
    )
    out_specs = (
        P("dp", "seq", None),
        P("dp", "seq", None),
        P(both, None),
        P(both, None),
        P(both, None),
        P(None, both),
        P(both, None),
        P(both, None),
        P(None, both),
        P(both),
        P(both),
        P(both),
        P(both),
    )
    return jax.shard_map(body, mesh=mesh, in_specs=in_specs, out_specs=out_specs, check_vma=False)
```

```python
import functools

import jax
import jax.numpy as jnp
from jax import lax
from jax.experimental import pallas as pl
from jax.experimental.pallas import tpu as pltpu
from jax.sharding import PartitionSpec as P

MESH = pl.DeviceIdType.MESH

HEAD_DIM = 128

rope_base = 500000.0
norm_eps = 1e-06
LOG2_E = 1.4426950408889634
f32 = jnp.float32
bf16 = jnp.bfloat16


def rope_tables(positions, head_dim):
    half_dim = head_dim // 2
    steps_f = jnp.arange(half_dim).astype(f32) * (2.0 / head_dim)
    inv_freq = jnp.power(rope_base, -steps_f)
    angle = positions.astype(f32)[:, None] * inv_freq[None, :]
    angle = jnp.concatenate([angle, angle], axis=-1)
    return (jnp.cos(angle), jnp.sin(angle))


def dot_nn(left, right):
    return jnp.dot(left, right, preferred_element_type=f32)


def dot_nt(left, right):
    return lax.dot_general(left, right, (((1,), (1,)), ((), ())), preferred_element_type=f32)


def dot_tn(left, right):
    return lax.dot_general(left, right, (((0,), (0,)), ((), ())), preferred_element_type=f32)


def across(piece):
    return lax.all_gather(piece, "dp", axis=0, tiled=True)


def dp_sum(grad):
    return lax.psum_scatter(grad, "dp", scatter_dimension=0, tiled=True)


class Line:
    def __init__(self, ways):
        self.chips = ways // 2
        self.last = self.chips - 1
        self.me = lax.axis_index("seq")
        self.chip = self.me // 2
        self.core = self.me % 2
        self.sibling = self.me + 1 - 2 * self.core

    def greet(self, groups=1):
        barrier = pltpu.get_barrier_semaphore()
        group = lax.axis_index("dp")
        for off in range(1, groups):
            pl.semaphore_signal(
                barrier, inc=1, device_id={"dp": (group + off) % groups}, device_id_type=MESH
            )
        has_low = jnp.minimum(self.chip, 1)
        has_high = jnp.minimum(self.last - self.chip, 1)
        pl.semaphore_signal(barrier, inc=1, device_id={"seq": self.sibling}, device_id_type=MESH)

        @pl.when(self.chip > 0)
        def _():
            pl.semaphore_signal(barrier, inc=1, device_id={"seq": self.me - 2}, device_id_type=MESH)

        @pl.when(self.chip < self.last)
        def _():
            pl.semaphore_signal(barrier, inc=1, device_id={"seq": self.me + 2}, device_id_type=MESH)

        pl.semaphore_wait(barrier, groups + has_low + has_high)


def remote(src, dst, send_sem, recv_sem, device):
    return pltpu.make_async_remote_copy(
        src_ref=src,
        dst_ref=dst,
        send_sem=send_sem,
        recv_sem=recv_sem,
        device_id={"seq": device},
        device_id_type=MESH,
    )


def rows_at(index, count):
    return pl.ds(pl.multiple_of(index * count, count), count)


def each_strip(tok_count, strip, fn):
    def one(i, carry):
        fn(rows_at(i, strip))
        return carry

    lax.fori_loop(0, tok_count // strip, one, 0)


class RowGather:
    def __init__(self, line, half, buf, sems):
        self.line, self.half, self.buf = line, half, buf
        self.up_send, self.down_send, self.col_recv, self.sib_send, self.sib_recv = sems

    @staticmethod
    def scratch(chips):
        return [pltpu.SemaphoreType.DMA((2 * chips,))] * 5

    def piece(self, src, core, h):
        return self.buf.at[rows_at(h * 2 * self.line.chips + 2 * src + core, self.half)]

    def hop(self, src, h, device, send):
        piece, at = self.piece(src, self.line.core, h), h * self.line.chips + src
        return remote(piece, piece, send.at[at], self.col_recv.at[at], device)

    def swap(self, src, core, h):
        piece, at = self.piece(src, core, h), h * self.line.chips + src
        return remote(piece, piece, self.sib_send.at[at], self.sib_recv.at[at], self.line.sibling)

    def start(self, h):
        line = self.line
        self.forward_up(line.chip, h)
        self.forward_down(line.chip, h)
        self.swap(line.chip, line.core, h).start()

    def forward_up(self, src, h):
        @pl.when(self.line.chip < self.line.last)
        def _():
            self.hop(src, h, self.line.me + 2, self.up_send).start()

    def forward_down(self, src, h):
        @pl.when(self.line.chip > 0)
        def _():
            self.hop(src, h, self.line.me - 2, self.down_send).start()

    def receive(self, away, h):
        line = self.line
        low, high = line.chip - away, line.chip + away

        @pl.when(low >= 0)
        def _():
            self.hop(low, h, line.sibling, self.up_send).wait_recv()
            self.forward_up(low, h)
            self.swap(low, line.core, h).start()

        @pl.when(high <= line.last)
        def _():
            self.hop(high, h, line.sibling, self.down_send).wait_recv()
            self.forward_down(high, h)
            self.swap(high, line.core, h).start()

    def use_at(self, away, h, use):
        line = self.line

        def one(side, carry):
            src = line.chip + (2 * side - 1) * away

            @pl.when((src >= 0) & (src <= line.last) & (away + 1 > side))
            def _():
                self.swap(src, 1 - line.core, h).wait_recv()
                use(src, h)

            return carry

        lax.fori_loop(0, 2, one, 0)

    def finish(self):
        line = self.line
        for h in (0, 1):

            def one(src, carry, h=h):
                self.swap(src, line.core, h).wait_send()

                @pl.when((src <= line.chip) & (line.chip < line.last))
                def _():
                    self.hop(src, h, line.sibling, self.up_send).wait_send()

                @pl.when((src >= line.chip) & (line.chip > 0))
                def _():
                    self.hop(src, h, line.sibling, self.down_send).wait_send()

                return carry

            lax.fori_loop(0, line.chips, one, 0)


class RowScatter:
    def __init__(self, line, half, bufs, sems):
        self.line, self.half = line, half
        self.pair, self.sib_in, self.acc = bufs
        self.sib_send, self.sib_recv, self.send, self.recv = sems

    @staticmethod
    def scratch(chips, tok, width):
        return [
            pltpu.VMEM((2 * chips * tok, width), bf16),
            pltpu.VMEM((chips * tok, width), bf16),
            pltpu.VMEM(((chips + 1) * tok, width), bf16),
            pltpu.SemaphoreType.DMA((2 * chips,)),
            pltpu.SemaphoreType.DMA((2 * chips,)),
            pltpu.SemaphoreType.DMA((2 * chips,)),
            pltpu.SemaphoreType.DMA((2 * (chips + 1),)),
        ]

    def of(self, left, right, tile, joined, turned=False):
        self.left, self.right, self.tile = left, right, tile
        self.joined, self.turned = joined, turned
        return self

    def swap(self, dest, h):
        half, line = self.half, self.line
        at = h * line.chips + dest
        return remote(
            self.pair.at[rows_at(2 * at + 1 - line.core, half)],
            self.sib_in.at[rows_at(at, half)],
            self.sib_send.at[at],
            self.sib_recv.at[at],
            line.sibling,
        )

    def hop(self, dest, slot, h, device):
        half, slots = self.half, self.line.chips + 1
        return remote(
            self.acc.at[rows_at(h * slots + dest, half)],
            self.acc.at[rows_at(h * slots + slot, half)],
            self.send.at[h * self.line.chips + dest],
            self.recv.at[h * slots + slot],
            device,
        )

    def produce(self, dest, h):
        if self.joined and h:
            return
        spans = [rows_at(h * self.line.chips + dest, 2 * self.half)]
        if self.joined:
            spans.append(rows_at(self.line.chips + dest, 2 * self.half))

        def one(n, carry):
            cols = rows_at(n, self.tile)
            left = [self.left[span, :] for span in spans]
            left = jnp.concatenate(left, axis=0) if self.joined else left[0]
            if self.turned:
                part = dot_nn(left, self.right[:, cols]).astype(bf16)
            else:
                part = dot_nt(left, self.right[cols, :]).astype(bf16)
            for i, span in enumerate(spans):
                self.pair[span, cols] = part[i * 2 * self.half : (i + 1) * 2 * self.half]
            return carry

        lax.fori_loop(0, self.right.shape[1 if self.turned else 0] // self.tile, one, 0)
        for i in range(len(spans)):
            self.swap(dest, h + i).start()

    def strip_of(self, index, strip):
        return pl.ds(pl.multiple_of(index * self.half + strip.start, 16), strip.size)

    def chip_sum(self, dest, h, strip):
        at = h * self.line.chips + dest
        mine = self.pair[self.strip_of(2 * at + self.line.core, strip), :]
        other = self.sib_in[self.strip_of(at, strip), :]
        return mine.astype(f32) + other.astype(f32)

    def legs(self, s):
        line = self.line
        below, above = line.chip, line.last - line.chip
        return (
            (line.last - s + below, 1, below, (s >= below) & (s < line.last)),
            (s - above, -1, above, (s >= above) & (s < line.last)),
        )

    def make(self, s, h):
        line = self.line
        if self.joined and h:
            return
        (up, _, _, has_up), (down, _, _, has_down) = self.legs(s)

        def one(k, carry):
            own, low = k // 2, k % 2
            dest = own * line.chip + (1 - own) * ((1 - low) * up + low * down)
            there = ((k == 0) & has_up) | ((k == 1) & has_down) | ((k == 2) & (s == line.last))

            @pl.when(there)
            def _():
                self.produce(dest, h)

            return carry

        lax.fori_loop(0, 3, one, 0)

    def pass_on(self, s, h):
        line = self.line
        chips, slots = line.chips, line.chips + 1
        for dest, step, behind, there in self.legs(s):
            if step > 0:
                slot = dest
            else:
                ends = 1 - jnp.minimum(line.chip - 1 - dest, 1)
                slot = dest + ends * (chips - dest)

            @pl.when(there)
            def _(dest=dest, behind=behind, slot=slot, step=step):
                self.swap(dest, h).wait_recv()

                @pl.when(behind > 0)
                def _():
                    self.hop(dest, dest, h, line.sibling).wait_recv()

                    def add(strip):
                        at = self.strip_of(h * slots + dest, strip)
                        total = self.chip_sum(dest, h, strip) + self.acc[at, :].astype(f32)
                        self.acc[at, :] = total.astype(bf16)

                    each_strip(self.half, 16, add)

                @pl.when(behind == 0)
                def _():
                    def put(strip):
                        at = self.strip_of(h * slots + dest, strip)
                        self.acc[at, :] = self.chip_sum(dest, h, strip).astype(bf16)

                    each_strip(self.half, 16, put)

                self.hop(dest, slot, h, line.me + 2 * step).start()

    def close(self, h):
        line = self.line
        chips, slots = line.chips, line.chips + 1
        empty = jnp.zeros((self.half, self.acc.shape[1]), bf16)
        self.swap(line.chip, h).wait_recv()

        @pl.when(line.chip > 0)
        def _():
            self.hop(line.chip, line.chip, h, line.sibling).wait_recv()

        @pl.when(line.chip == 0)
        def _():
            self.acc[rows_at(h * slots + line.chip, self.half), :] = empty

        @pl.when(line.chip < line.last)
        def _():
            self.hop(line.chip, chips, h, line.sibling).wait_recv()

        @pl.when(line.chip == line.last)
        def _():
            self.acc[rows_at(h * slots + chips, self.half), :] = empty

    def total(self, h, strip):
        line = self.line
        slots = line.chips + 1
        low = self.acc[self.strip_of(h * slots + line.chip, strip), :].astype(f32)
        high = self.acc[self.strip_of(h * slots + line.chips, strip), :].astype(f32)
        return self.chip_sum(line.chip, h, strip) + (low + high)

    def finish(self, h):
        line = self.line

        def one(dest, carry):
            self.swap(dest, h).wait_send()

            @pl.when(line.chip != dest)
            def _():
                self.hop(dest, dest, h, line.sibling).wait_send()

            return carry

        lax.fori_loop(0, line.chips, one, 0)


def advance(scatter=None, sh=0, gather=None, gh=0, use=None, fill=None, settle=None):
    line = (scatter or gather).line

    def slot(i, carry):
        s = i - 1
        if gather:

            @pl.when((s > 0) & (s < line.chips))
            def _():
                gather.receive(s, gh)

        if scatter:
            scatter.pass_on(s, sh)
            scatter.make(s + 1, sh)
        if settle:

            @pl.when(s == line.chips)
            def _():
                settle()

        if gather:

            @pl.when(s > 0)
            def _():
                gather.use_at(s - 1, gh, use)

        if fill:

            @pl.when((s >= 0) & (s < line.chips))
            def _():
                fill(s)

        return carry

    lax.fori_loop(0, line.chips + 2, slot, 0)


def mean_rows(values):
    return jnp.sum(values, axis=-1, keepdims=True) * (1.0 / values.shape[-1])


class Blocks:
    def __init__(self, line, count, pairs, sems):
        self.line, self.count, self.pairs, self.sems = line, count, pairs, sems

    def copy(self, i, index):
        src, dst = self.pairs[i]
        at = rows_at(index, self.count)
        return pltpu.make_async_copy(src.at[at], dst.at[at], self.sems.at[i, index])

    def send(self, i, chip, h):
        self.copy(i, h * self.line.chips + chip).start()

    def finish(self):
        def one(index, carry):
            for i in range(len(self.pairs)):
                self.copy(i, index).wait()
            return carry

        lax.fori_loop(0, 2 * self.line.chips, one, 0)


def call(kernel, outs, scratch, args, ident, cost=1, far_in=(), far_out=()):
    def space(i, far):
        return pl.BlockSpec(memory_space=pl.ANY if i in far else pltpu.VMEM)

    return pl.pallas_call(
        kernel,
        out_shape=outs,
        in_specs=[space(i, far_in) for i in range(len(args))],
        out_specs=[space(i, far_out) for i in range(len(outs))],
        scratch_shapes=scratch,
        cost_estimate=pl.CostEstimate(
            flops=cost * 10**9, transcendentals=0, bytes_accessed=cost * 3 * 10**6
        ),
        compiler_params=pltpu.CompilerParams(
            collective_id=ident, has_side_effects=True, vmem_limit_bytes=63 * 2**20
        ),
    )(*args)


def shape(dims, kind):
    return jax.ShapeDtypeStruct(dims, kind)


def gather_project(rows, codes, weights, ways, ident):
    tok, width = rows.shape
    cols = weights.shape[1] - HEAD_DIM
    half = tok // 2

    def kernel(
        rows_ref, code_ref, w_far, all_far, codes_ref, prod_far,
        w_ref, all_ref, prod_ref, w_sem, out_sem, code_send, code_recv, *sems
    ):
        line = Line(ways)
        w_copy = pltpu.make_async_copy(w_far.at[:, pl.ds(0, cols)], w_ref, w_sem)
        w_copy.start()
        outs = Blocks(line, 2 * half, [(all_ref, all_far), (prod_ref, prod_far)], out_sem)
        me = line.me
        barrier = pltpu.get_barrier_semaphore()
        for off in range(1, ways):
            pl.semaphore_signal(
                barrier, inc=1, device_id={"seq": (me + off) % ways}, device_id_type=MESH
            )
        pl.semaphore_wait(barrier, ways - 1)
        gather = RowGather(line, half, all_ref, sems)
        for h in (0, 1):
            all_ref[rows_at(h * ways + me, half), :] = rows_ref[pl.ds(h * half, half), :]
            gather.start(h)
        codes_ref[me] = code_ref[...]

        def tell(off):
            return remote(
                code_ref, codes_ref.at[me], code_send.at[off], code_recv.at[off], (me + off) % ways
            )

        for off in range(1, ways):
            tell(off).start()

        def use(chip, h):
            at = rows_at(h * line.chips + chip, 2 * half)

            prod_ref[at, :] = dot_nn(all_ref[at, :], w_ref[...])
            outs.send(0, chip, h)
            outs.send(1, chip, h)

        def step(j, carry):
            def one(h, carry):
                @pl.when(j < line.chips)
                def _():
                    gather.receive(j, h)

                gather.use_at(j - 1, h, use)
                return carry

            return lax.fori_loop(0, 2, one, carry)

        w_copy.wait()
        lax.fori_loop(1, line.chips + 1, step, 0)
        gather.finish()
        outs.finish()
        for off in range(1, ways):
            tell(off).wait()

    return call(
        kernel,
        [
            shape((ways * tok, width), bf16),
            shape((ways,) + codes.shape, jnp.int32),
            shape((ways * tok, cols), f32),
        ],
        [
            pltpu.VMEM((width, cols), bf16),
            pltpu.VMEM((ways * tok, width), bf16),
            pltpu.VMEM((ways * tok, cols), f32),
            pltpu.SemaphoreType.DMA,
            pltpu.SemaphoreType.DMA((2, ways)),
            pltpu.SemaphoreType.DMA((ways,)),
            pltpu.SemaphoreType.DMA((ways,)),
        ]
        + RowGather.scratch(ways // 2),
        [rows, codes, weights],
        ident,
        55,
        (2,),
        (0, 2),
    )


def attn_out_and_ff(attn_low, m_mid, p_down, token_rows, grad_out, gains, groups, ways, ident):
    tok, width = token_rows.shape
    half = tok // 2
    own_feat, own_ff = attn_low.shape[1], p_down.shape[1]
    part = p_down.shape[0]
    row = ways * tok
    tile = min(own_ff, 1024)
    square = width == 2 * own_ff
    square_tile = 256
    squares = width // square_tile

    def kernel(
        left_far, mid_far, down_far, x_far, go_far, gains_ref,
        branch_far, out_ref, gg_ref, hid_far, mix_far, gm_far, dgu_far, first_ref, turned_far,
        left, mid_ref, down_ref, x_ref, go_ref, branch_ref, hid_ref, mix_ref, gm_ref, dgu_ref,
        down_turned, turned_sem, in_sem, out_sem, branch_sem, down_send, down_recv, *rest
    ):
        line = Line(ways)
        group = lax.axis_index("dp")
        gu_cols, out_cols = pl.ds(0, 2 * own_ff), pl.ds(2 * own_ff, own_feat)
        fetch = [
            pltpu.make_async_copy(src, dst, in_sem.at[i])
            for i, (src, dst) in enumerate(
                [
                    (left_far, left),
                    (mid_far.at[:, out_cols], mid_ref.at[:, out_cols]),
                    (x_far, x_ref),
                    (mid_far.at[:, gu_cols], mid_ref.at[:, gu_cols]),
                    (down_far, down_ref.at[rows_at(group, part)]),
                    (go_far, go_ref),
                ]
            )
        ]
        for copy in fetch:
            copy.start()
        outs = Blocks(
            line,
            2 * half,
            [(hid_ref, hid_far), (mix_ref, mix_far), (gm_ref, gm_far), (dgu_ref, dgu_far)],
            out_sem,
        )
        keep_branch = pltpu.make_async_copy(branch_ref, branch_far, branch_sem)
        line.greet(groups)

        def spread(off):
            return pltpu.make_async_remote_copy(
                src_ref=down_far,
                dst_ref=down_ref.at[rows_at(group, part)],
                send_sem=down_send.at[off],
                recv_sem=down_recv.at[off],
                device_id={"dp": (group + off) % groups},
                device_id_type=MESH,
            )

        for off in range(1, groups):
            spread(off).start()
        scatter = RowScatter(line, half, rest[:3], rest[3:7])
        hidden = RowGather(line, half, hid_ref, rest[7:12])
        back = RowGather(line, half, gm_ref, rest[12:17])
        gg_ref[...] = jnp.zeros_like(gg_ref)
        gain_attn, gain_mlp = gains_ref[2:3, :], gains_ref[3:4, :]

        def own(h, strip):
            return pl.ds(pl.multiple_of((h * ways + line.me) * half + strip.start, 16), strip.size)

        def residual(at):
            branch = branch_ref[at, :]
            factor = lax.rsqrt(mean_rows(branch * branch) + norm_eps)
            return x_ref[at, :].astype(f32) + branch * factor * gain_attn

        def settle_attn(h):
            def one(strip):
                at = pl.ds(pl.multiple_of(h * half + strip.start, 16), strip.size)
                branch_ref[at, :] = scatter.total(h, strip)
                hid_ref[own(h, strip), :] = residual(at).astype(bf16)

            scatter.close(h)
            each_strip(half, 16, one)
            hidden.start(h)
            scatter.finish(h)

        def settle_mlp(h):
            def one(strip):
                at = pl.ds(pl.multiple_of(h * half + strip.start, 16), strip.size)
                mlp = scatter.total(h, strip)
                factor = lax.rsqrt(mean_rows(mlp * mlp) + norm_eps)
                unit = mlp * factor
                lifted = go_ref[at, :].astype(f32) * gain_mlp
                turned = factor * (lifted - unit * mean_rows(lifted * unit))
                gm_ref[own(h, strip), :] = turned.astype(bf16)

            def rest_of(strip):
                at = pl.ds(pl.multiple_of(h * half + strip.start, 16), strip.size)
                mlp = scatter.total(h, strip)
                unit = mlp * lax.rsqrt(mean_rows(mlp * mlp) + norm_eps)
                out_ref[at, :] = (residual(at) + unit * gain_mlp).astype(bf16)
                terms = go_ref[at, :].astype(f32) * unit
                gg_ref[...] += terms[:8] + terms[8:]

            scatter.close(h)
            each_strip(half, 16, one)
            back.start(h)
            each_strip(half, 16, rest_of)
            scatter.finish(h)

        def gate_up(chip, h):
            at = rows_at(h * line.chips + chip, 2 * half)

            outs.send(0, chip, h)

            both = dot_nn(hid_ref[at, :], mid_ref[:, gu_cols])
            gate, up = both[:, :own_ff], both[:, own_ff:]
            dgu_ref[at, :] = both.astype(bf16)
            mix_ref[at, :] = (gate * jax.nn.sigmoid(gate) * up).astype(bf16)
            outs.send(1, chip, h)

        def gate_up_back(chip, h):
            at = rows_at(h * line.chips + chip, 2 * half)

            outs.send(2, chip, h)

            def one(n, carry):
                here, there = rows_at(n, tile), pl.ds(pl.multiple_of(own_ff + n * tile, tile), tile)
                grad = dot_nn(gm_ref[at, :], down_ref[:, here])
                gate, up = dgu_ref[at, here].astype(f32), dgu_ref[at, there].astype(f32)
                sigma = jax.nn.sigmoid(gate)
                dgu_ref[at, here] = (grad * up * sigma * (1.0 + gate * (1.0 - sigma))).astype(bf16)
                dgu_ref[at, there] = (grad * gate * sigma).astype(bf16)
                return carry

            lax.fori_loop(0, own_ff // tile, one, 0)
            outs.send(3, chip, h)

        for copy in fetch[:3]:
            copy.wait()
        scatter.of(left, mid_ref.at[:, out_cols], 1024, True)
        advance(scatter, 0, settle=lambda: settle_attn(0))
        fetch[3].wait()
        advance(scatter, 1, hidden, 0, gate_up, settle=lambda: settle_attn(1))

        def turn_down(i, carry):
            rows = rows_at(i, square_tile)
            down_turned[:, rows] = down_ref[rows, :].T
            return carry

        def turn_square(s):
            def one(i, carry):
                def two(j, carry):
                    rows, cols = rows_at(i, square_tile), rows_at(j, square_tile)
                    block, other = mid_ref[rows, cols], mid_ref[cols, rows]
                    mid_ref[cols, rows] = block.T
                    mid_ref[rows, cols] = other.T
                    return carry

                return lax.fori_loop(i, squares, two, carry)

            lax.fori_loop(s * squares // line.chips, (s + 1) * squares // line.chips, one, 0)

        keep_branch.start()
        for copy in fetch[4:]:
            copy.wait()
        for off in range(1, groups):
            spread(off).wait()
        if square:
            lax.fori_loop(0, squares, turn_down, 0)
            scatter.of(mix_ref, down_turned, 2048, False, True)
        else:
            scatter.of(mix_ref, down_ref, 2048, False)
        advance(scatter, 0, hidden, 1, gate_up, settle=lambda: settle_mlp(0))
        advance(
            scatter, 1, back, 0, gate_up_back, turn_square if square else None, lambda: settle_mlp(1)
        )
        keep_turned = pltpu.make_async_copy(mid_ref.at[:, gu_cols], turned_far, turned_sem)
        keep_turned.start()
        scatter.of(dgu_ref, mid_ref.at[:, gu_cols], 1024, False, square)

        def keep_first():
            def put(strip):
                first_ref[strip, :] = scatter.total(0, strip)

            scatter.close(0)
            each_strip(half, 16, put)
            scatter.finish(0)

        advance(scatter, 0, back, 1, gate_up_back, settle=keep_first)
        hidden.finish()
        back.finish()
        keep_branch.wait()
        keep_turned.wait()
        outs.finish()

    return call(
        kernel,
        [
            shape((tok, width), f32),
            shape((tok, width), bf16),
            shape((8, width), f32),
            shape((row, width), bf16),
            shape((row, own_ff), bf16),
            shape((row, width), bf16),
            shape((row, 2 * own_ff), bf16),
            shape((half, width), f32),
            shape((width, 2 * own_ff), bf16),
        ],
        [
            pltpu.VMEM((row, own_feat), bf16),
            pltpu.VMEM(m_mid.shape, bf16),
            pltpu.VMEM((groups * part, own_ff), bf16),
            pltpu.VMEM((tok, width), bf16),
            pltpu.VMEM((tok, width), bf16),
            pltpu.VMEM((tok, width), f32),
            pltpu.VMEM((row, width), bf16),
            pltpu.VMEM((row, own_ff), bf16),
            pltpu.VMEM((row, width), bf16),
            pltpu.VMEM((row, 2 * own_ff), bf16),
            pltpu.VMEM((own_ff, width) if square else (16, HEAD_DIM), bf16),
            pltpu.SemaphoreType.DMA,
            pltpu.SemaphoreType.DMA((6,)),
            pltpu.SemaphoreType.DMA((4, ways)),
            pltpu.SemaphoreType.DMA,
            pltpu.SemaphoreType.DMA((groups,)),
            pltpu.SemaphoreType.DMA((groups,)),
        ]
        + RowScatter.scratch(ways // 2, tok, width)
        + RowGather.scratch(ways // 2)
        + RowGather.scratch(ways // 2),
        [attn_low, m_mid, p_down, token_rows, grad_out, gains],
        ident,
        150,
        range(5),
        (0, 3, 4, 5, 6, 8),
    )


def ff_to_attn_back(
    grad_gu, first_half, turned, m_mid, branch, grad_out, gain_row, grad_mlp, mixed_low, ways, ident
):
    tok, width = branch.shape
    half = tok // 2
    own_ff = grad_gu.shape[1] // 2
    own_feat = m_mid.shape[1] - 2 * own_ff
    row = ways * tok
    tiles = width // 256

    def kernel(
        left_far, first_ref, turned_far, w_far, br_ref, go_ref, gain_ref, gm_far, mix_far,
        gh_ref, gg_ref, all_far, ga_ref, dd_far,
        left, turned_ref, w_ref, in_sem, all_ref, out_sem, gm_ref, mix_ref, dd_ref, gm_sem, mix_sem, dd_sem, *rest
    ):
        line = Line(ways)
        wanted = [
            pltpu.make_async_copy(w_far.at[:, pl.ds(2 * own_ff, own_feat)], w_ref, in_sem.at[0]),
            pltpu.make_async_copy(turned_far, turned_ref, in_sem.at[2]),
            pltpu.make_async_copy(left_far, left, in_sem.at[1]),
        ]
        for copy in wanted:
            copy.start()
        mix_copy = pltpu.make_async_copy(mix_far, mix_ref, mix_sem)

        def fetch(i):
            return pltpu.make_async_copy(
                gm_far.at[:, rows_at(i, 256)], gm_ref.at[i % 2], gm_sem.at[i % 2]
            )

        def keep(i):
            rows = rows_at(i, 256)
            return pltpu.make_async_copy(dd_ref.at[rows], dd_far.at[rows], dd_sem.at[i])

        def down_grad(i, carry):
            fetch(i).wait()

            @pl.when(i + 1 < tiles)
            def _():
                fetch(i + 1).start()

            dd_ref[rows_at(i, 256), :] = dot_tn(gm_ref[i % 2], mix_ref[...]).astype(bf16)
            keep(i).start()
            return carry

        def fill(s):
            lax.fori_loop(s * tiles // line.chips, (s + 1) * tiles // line.chips, down_grad, 0)

        outs = Blocks(line, 2 * half, [(all_ref, all_far)], out_sem)
        line.greet()
        scatter = RowScatter(line, half, rest[:3], rest[3:7])
        gather = RowGather(line, half, all_ref, rest[7:])
        gg_ref[...] = jnp.zeros_like(gg_ref)

        def settle(h):
            def one(strip):
                at = pl.ds(pl.multiple_of(h * half + strip.start, 16), strip.size)
                mine = pl.ds(
                    pl.multiple_of((h * ways + line.me) * half + strip.start, 16), strip.size
                )
                total = scatter.total(h, strip) if h else first_ref[strip, :]
                grad = total + go_ref[at, :].astype(f32)
                branch = br_ref[at, :]
                factor = lax.rsqrt(mean_rows(branch * branch) + norm_eps)
                unit = branch * factor
                gh_ref[at, :] = grad
                terms = grad * unit
                gg_ref[...] += terms[:8] + terms[8:]
                lifted = grad * gain_ref[...]
                turned = factor * (lifted - unit * mean_rows(lifted * unit))
                all_ref[mine, :] = turned.astype(bf16)

            if h:
                scatter.close(h)
            each_strip(half, 16, one)
            gather.start(h)

        def use(chip, h):
            at = rows_at(h * line.chips + chip, 2 * half)
            outs.send(0, chip, h)
            ga_ref[at, :] = dot_nn(all_ref[at, :], w_ref[...])

        scatter.of(left, turned_ref, 1024, False, width == 2 * own_ff)
        settle(0)
        for copy in wanted:
            copy.wait()
        advance(scatter, 1, gather, 0, use, settle=lambda: settle(1))
        mix_copy.start()
        fetch(0).start()
        mix_copy.wait()
        advance(None, 0, gather, 1, use, fill)
        gather.finish()
        outs.finish()
        for i in range(tiles):
            keep(i).wait()
        scatter.finish(1)

    return call(
        kernel,
        [
            shape((tok, width), f32),
            shape((8, width), f32),
            shape((row, width), bf16),
            shape((row, own_feat), f32),
            shape((width, own_ff), bf16),
        ],
        [
            pltpu.VMEM(grad_gu.shape, bf16),
            pltpu.VMEM(turned.shape, bf16),
            pltpu.VMEM((width, own_feat), bf16),
            pltpu.SemaphoreType.DMA((3,)),
            pltpu.VMEM((row, width), bf16),
            pltpu.SemaphoreType.DMA((1, ways)),
            pltpu.VMEM((2, row, 256), bf16),
            pltpu.VMEM((row, own_ff), bf16),
            pltpu.VMEM((width, own_ff), bf16),
            pltpu.SemaphoreType.DMA((2,)),
            pltpu.SemaphoreType.DMA,
            pltpu.SemaphoreType.DMA((tiles,)),
        ]
        + RowScatter.scratch(ways // 2, tok, width)
        + RowGather.scratch(ways // 2),
        [grad_gu, first_half, turned, m_mid, branch, grad_out, gain_row, grad_mlp, mixed_low],
        ident,
        70,
        (0, 2, 3, 7, 8),
        (2, 4),
    )


def home_copies(me, ways, source, targets, widths, send, recv):
    rows = source.shape[0] // ways
    begins = [sum(widths[:i]) for i in range(len(widths))]
    count = len(widths)

    def part(i, dest):
        return (
            source.at[rows_at(dest, rows), pl.ds(begins[i], widths[i])],
            targets[i].at[:, rows_at(me, widths[i])],
        )

    def move(off, i):
        dest = (me + off) % ways
        return remote(*part(i, dest), send.at[off * count + i], recv.at[off * count + i], dest)

    def keep(i):
        return pltpu.make_async_copy(*part(i, me), send.at[i])

    def each(what):
        def one(off, carry):
            for i in range(count):
                what(move(off, i))
            return carry

        lax.fori_loop(1, ways, one, 0)

    def start():
        for i in range(count):
            keep(i).start()
        each(lambda copy: copy.start())

    def wait():
        for i in range(count):
            keep(i).wait()
        each(lambda copy: copy.wait())

    return start, wait


def greet_line(me, ways):
    barrier = pltpu.get_barrier_semaphore()

    def greet(off, carry):
        pl.semaphore_signal(
            barrier, inc=1, device_id={"seq": (me + off) % ways}, device_id_type=MESH
        )
        return carry

    lax.fori_loop(1, ways, greet, 0)
    pl.semaphore_wait(barrier, ways - 1)


def bring_home(summed, widths, ways, ident):
    rows = summed.shape[0] // ways
    count = len(widths)

    def kernel(*refs):
        source, targets, (send, recv) = refs[0], refs[1 : 1 + count], refs[1 + count :]
        me = lax.axis_index("seq")
        greet_line(me, ways)
        start, wait = home_copies(me, ways, source, targets, widths, send, recv)
        start()
        wait()

    return call(
        kernel,
        [shape((rows, ways * width), bf16) for width in widths],
        [pltpu.SemaphoreType.DMA((ways * count,))] * 2,
        [summed],
        ident,
        30,
        (0,),
        range(count),
    )


def project_back(grad_qkv, m_qkv, grad_hidden, d_down, ways, ident):
    tok, width = grad_hidden.shape
    half = tok // 2
    own_ff = d_down.shape[1]

    def kernel(left, w_ref, gh_ref, dd_ref, out_ref, home_ref, dd_send, dd_recv, *rest):
        line = Line(ways)
        greet_line(line.me, ways)
        start, wait = home_copies(line.me, ways, dd_ref, [home_ref], [own_ff], dd_send, dd_recv)
        start()
        scatter = RowScatter(line, half, rest[:3], rest[3:7])
        scatter.of(left, w_ref.at[:, pl.ds(0, left.shape[1])], 1024, True)
        for h in (0, 1):
            advance(scatter, h)
        for h in (0, 1):

            def one(strip, h=h):
                at = pl.ds(pl.multiple_of(h * half + strip.start, 16), strip.size)
                out_ref[at, :] = (gh_ref[at, :] + scatter.total(h, strip)).astype(bf16)

            scatter.close(h)
            each_strip(half, 16, one)
        for h in (0, 1):
            scatter.finish(h)
        wait()

    return call(
        kernel,
        [
            shape((tok, width), bf16),
            shape((d_down.shape[0] // ways, ways * own_ff), bf16),
        ],
        [pltpu.SemaphoreType.DMA((ways,))] * 2 + RowScatter.scratch(ways // 2, tok, width),
        [grad_qkv, m_qkv, grad_hidden, d_down],
        ident,
        65,
        (3,),
        (1,),
    )


def half_turn(values, sign):
    half_dim = HEAD_DIM // 2
    lane = lax.broadcasted_iota(jnp.int32, values.shape, 1)
    swapped = pltpu.roll(values, half_dim, 1)
    return jnp.where(lane < half_dim, -sign * swapped, sign * swapped)


def attend(parts, block):
    row = parts[0].shape[0]
    width = parts[0].shape[1] // 3
    heads = width // HEAD_DIM
    scale = HEAD_DIM ** (-0.5)

    def kernel(
        qkv_ref, factor_ref, cos_ref, sin_ref, gain_ref, qpos_ref, kpos_ref, kmax_ref,
        q_ref, k_ref, v_ref, at_ref, low_ref, ws_ref
    ):
        def turn(i, carry):
            rows = rows_at(i, block)
            cosine, sine = cos_ref[rows, :], sin_ref[rows, :]
            for which, out_ref in ((0, q_ref), (1, k_ref)):
                factor = factor_ref[rows, pl.ds(which, 1)]
                for head in range(heads):
                    lanes = pl.ds(head * HEAD_DIM, HEAD_DIM)
                    raw = qkv_ref[rows, pl.ds(which * width + head * HEAD_DIM, HEAD_DIM)]
                    normed = raw * factor * gain_ref[which : which + 1, lanes]
                    out_ref[rows, lanes] = (
                        normed * cosine + half_turn(normed, 1.0) * sine
                    ).astype(bf16)
            v_ref[rows, :] = qkv_ref[rows, pl.ds(2 * width, width)].astype(bf16)
            return carry

        lax.fori_loop(0, row // block, turn, 0)

        def one(i, carry):
            rows = rows_at(i, block)
            qpos = qpos_ref[rows, :]
            mask = (kpos_ref[...] <= qpos) & (qpos <= kmax_ref[...])
            for head in range(heads):
                lanes = pl.ds(head * HEAD_DIM, HEAD_DIM)
                scores = dot_nt(q_ref[rows, lanes], k_ref[:, lanes]) * (scale * LOG2_E)
                expo = jnp.where(mask, jnp.exp2(scores), 0.0)
                total = jnp.sum(expo, axis=-1, keepdims=True)
                result = dot_nn(expo.astype(bf16), v_ref[:, lanes]) / total
                ws_ref[rows, pl.ds(head, 1)] = total
                at_ref[rows, lanes] = result
                low_ref[rows, lanes] = result.astype(bf16)
            return carry

        lax.fori_loop(0, row // block, one, 0)

    return pl.pallas_call(
        kernel,
        out_shape=[shape((row, width), bf16)] * 3
        + [shape((row, width), f32), shape((row, width), bf16), shape((row, heads), f32)],
        in_specs=[pl.BlockSpec(memory_space=pltpu.VMEM)] * len(parts),
        out_specs=[pl.BlockSpec(memory_space=pltpu.VMEM)] * 6,
        cost_estimate=pl.CostEstimate(
            flops=4 * row * row * width, transcendentals=row * row * heads, bytes_accessed=60 * 10**6
        ),
        compiler_params=pltpu.CompilerParams(vmem_limit_bytes=60 * 2**20),
    )(*parts)


def attend_back(parts, summed, block, ways, ident):
    row, width = parts[0].shape
    heads = width // HEAD_DIM
    scale = HEAD_DIM ** (-0.5)

    def kernel(
        q_ref, k_ref, v_ref, ga_ref, at_ref, ws_ref, cos_ref, sin_ref, qkv_ref, factor_ref,
        gain_ref, qpos_ref, kpos_ref, kmax_ref, sum_ref,
        cq_ref, ck_ref, dv_ref, terms_ref, gg_ref, home_ref, dk_acc, dv_acc, send, recv
    ):
        me = lax.axis_index("seq")
        greet_line(me, ways)
        start, wait = home_copies(me, ways, sum_ref, [home_ref], [summed.shape[1]], send, recv)
        start()
        gg_ref[...] = jnp.zeros_like(gg_ref)
        dk_acc[...] = jnp.zeros_like(dk_acc)
        dv_acc[...] = jnp.zeros_like(dv_acc)

        def turn_back(grad, rows, which, out_ref, head):
            lanes = pl.ds(head * HEAD_DIM, HEAD_DIM)
            cosine, sine = cos_ref[rows, :], sin_ref[rows, :]
            normed = grad * cosine + half_turn(grad * sine, -1.0)
            raw = qkv_ref[rows, pl.ds(which * width + head * HEAD_DIM, HEAD_DIM)]
            unit = raw * factor_ref[rows, pl.ds(which, 1)]
            gg_ref[which : which + 1, lanes] += jnp.sum(normed * unit, axis=0, keepdims=True)
            lifted = normed * gain_ref[which : which + 1, lanes]
            out_ref[rows, lanes] = lifted
            term = jnp.sum(lifted * unit, axis=-1, keepdims=True)
            column = pl.ds(which, 1)
            if head == 0:
                terms_ref[rows, column] = term
            else:
                terms_ref[rows, column] += term

        def one(i, carry):
            rows = rows_at(i, block)
            qpos = qpos_ref[rows, :]
            mask = (kpos_ref[...] <= qpos) & (qpos <= kmax_ref[...])
            for head in range(heads):
                lanes = pl.ds(head * HEAD_DIM, HEAD_DIM)
                grad = ga_ref[rows, lanes]
                inverse = 1.0 / ws_ref[rows, pl.ds(head, 1)]
                drop = jnp.sum(grad * at_ref[rows, lanes], axis=-1, keepdims=True) * inverse
                grad_num = (grad * inverse).astype(bf16)
                query, keys = q_ref[rows, lanes], k_ref[:, lanes]
                scores = dot_nt(query, keys) * (scale * LOG2_E)
                expo = jnp.where(mask, jnp.exp2(scores), 0.0)
                grad_expo = dot_nt(grad_num, v_ref[:, lanes])
                grad_scores = (expo * (grad_expo - drop)).astype(bf16)
                turn_back(dot_nn(grad_scores, keys) * scale, rows, 0, cq_ref, head)
                dk_acc[:, lanes] += dot_tn(grad_scores, query)
                dv_acc[:, lanes] += dot_tn(expo.astype(bf16), grad_num)
            return carry

        lax.fori_loop(0, row // block, one, 0)

        def last(i, carry):
            rows = rows_at(i, block)
            for head in range(heads):
                lanes = pl.ds(head * HEAD_DIM, HEAD_DIM)
                turn_back(dk_acc[rows, lanes] * scale, rows, 1, ck_ref, head)
                dv_ref[rows, lanes] = dv_acc[rows, lanes].astype(bf16)
            return carry

        lax.fori_loop(0, row // block, last, 0)
        wait()

    return call(
        kernel,
        [
            shape((row, width), f32),
            shape((row, width), f32),
            shape((row, width), bf16),
            shape((row, 2), f32),
            shape((2, width), f32),
            shape((summed.shape[0] // ways, ways * summed.shape[1]), bf16),
        ],
        [pltpu.VMEM((row, width), f32)] * 2 + [pltpu.SemaphoreType.DMA((ways,))] * 2,
        list(parts) + [summed],
        ident,
        25,
        (len(parts),),
        (5,),
    )


def attn_grads(x_row, grad_qkv, grad_branch, attn_low, gain_columns, summed, ways, ident):
    row, width = x_row.shape
    first, second = grad_qkv.shape[1], attn_low.shape[1]
    cols = first + second + gain_columns.shape[1]

    def kernel(
        x_far, dq_ref, gb_far, low_ref, gain_ref, sum_ref, out_far, home_ref,
        x_ref, gb_ref, out_ref, in_sem, out_sem, send, recv
    ):
        me = lax.axis_index("seq")
        fetch = [
            pltpu.make_async_copy(x_far, x_ref, in_sem.at[0]),
            pltpu.make_async_copy(gb_far, gb_ref, in_sem.at[1]),
        ]
        for copy in fetch:
            copy.start()
        greet_line(me, ways)
        start, wait = home_copies(me, ways, sum_ref, [home_ref], [summed.shape[1]], send, recv)
        start()
        for copy in fetch:
            copy.wait()
        tile = 256

        def keep(i):
            rows = rows_at(i, tile)
            return pltpu.make_async_copy(out_ref.at[rows], out_far.at[rows], out_sem.at[i])

        def one(i, carry):
            rows = rows_at(i, tile)
            out_ref[rows, pl.ds(0, first)] = dot_tn(x_ref[:, rows], dq_ref[...]).astype(bf16)
            out_ref[rows, pl.ds(first, second)] = dot_tn(gb_ref[:, rows], low_ref[...]).astype(bf16)
            out_ref[rows, pl.ds(first + second, gain_columns.shape[1])] = gain_ref[rows, :]
            keep(i).start()
            return carry

        lax.fori_loop(0, width // tile, one, 0)

        def kept(i, carry):
            keep(i).wait()
            return carry

        lax.fori_loop(0, width // tile, kept, 0)
        wait()

    return call(
        kernel,
        [
            shape((width, cols), bf16),
            shape((summed.shape[0] // ways, ways * summed.shape[1]), bf16),
        ],
        [
            pltpu.VMEM((row, width), bf16),
            pltpu.VMEM((row, width), bf16),
            pltpu.VMEM((width, cols), bf16),
            pltpu.SemaphoreType.DMA((2,)),
            pltpu.SemaphoreType.DMA((width // 256,)),
            pltpu.SemaphoreType.DMA((ways,)),
            pltpu.SemaphoreType.DMA((ways,)),
        ],
        [x_row, grad_qkv, grad_branch, attn_low, gain_columns, summed],
        ident,
        25,
        (0, 2, 5),
        (0, 1),
    )


def exchange(sources, ways, ident, cost):
    rows = sources[0].shape[0]
    widths = [a.shape[1] // ways for a in sources]
    begins = [sum(widths[:i]) for i in range(len(widths))]
    count = len(sources)

    def kernel(*refs):
        ins, out_ref, send, recv, local = refs[:count], *refs[count:]
        me = lax.axis_index("seq")
        barrier = pltpu.get_barrier_semaphore()

        def greet(off, carry):
            pl.semaphore_signal(
                barrier, inc=1, device_id={"seq": (me + off) % ways}, device_id_type=MESH
            )
            return carry

        def move(off, i):
            dest = (me + off) % ways
            return remote(
                ins[i].at[:, rows_at(dest, widths[i])],
                out_ref.at[rows_at(me, rows), pl.ds(begins[i], widths[i])],
                send.at[off * count + i],
                recv.at[off * count + i],
                dest,
            )

        def keep(i):
            return pltpu.make_async_copy(
                ins[i].at[:, rows_at(me, widths[i])],
                out_ref.at[rows_at(me, rows), pl.ds(begins[i], widths[i])],
                local.at[i],
            )

        def each(what):
            def one(off, carry):
                for i in range(count):
                    what(move(off, i))
                return carry

            lax.fori_loop(1, ways, one, 0)

        for i in range(count):
            keep(i).start()
        lax.fori_loop(1, ways, greet, 0)
        pl.semaphore_wait(barrier, ways - 1)
        each(lambda copy: copy.start())
        for i in range(count):
            keep(i).wait()
        each(lambda copy: copy.wait())

    return pl.pallas_call(
        kernel,
        out_shape=shape((ways * rows, sum(widths)), bf16),
        in_specs=[pl.BlockSpec(memory_space=pl.ANY)] * count,
        out_specs=pl.BlockSpec(memory_space=pl.ANY),
        scratch_shapes=[
            pltpu.SemaphoreType.DMA((ways * count,)),
            pltpu.SemaphoreType.DMA((ways * count,)),
            pltpu.SemaphoreType.DMA((count,)),
        ],
        cost_estimate=pl.CostEstimate(
            flops=cost * 10**9, transcendentals=0, bytes_accessed=cost * 3 * 10**6
        ),
        compiler_params=pltpu.CompilerParams(collective_id=ident, has_side_effects=True),
    )(*sources)


def finish_grads(grads, kept, gains, ways):
    rows, count = gains.shape[0], len(grads)
    parts = list(grads) + list(kept) + [gains]

    def kernel(*refs):
        ins, outs = refs[: len(parts)], refs[len(parts) :]
        for i in range(len(parts) - 1):
            outs[i][...] = ins[i][...].astype(outs[i].dtype)
        total = ins[-1][:, pl.ds(0, HEAD_DIM)].astype(f32)
        for off in range(1, ways):
            total = total + ins[-1][:, pl.ds(off * HEAD_DIM, HEAD_DIM)].astype(f32)
        outs[-1][...] = total.T[:8, :]

    return pl.pallas_call(
        kernel,
        out_shape=[shape(part.shape, f32 if i < count else part.dtype) for i, part in enumerate(parts[:-1])]
        + [shape((8, rows), f32)],
        in_specs=[pl.BlockSpec(memory_space=pltpu.VMEM)] * len(parts),
        out_specs=[pl.BlockSpec(memory_space=pltpu.VMEM)] * len(parts),
        cost_estimate=pl.CostEstimate(flops=10**6, transcendentals=0, bytes_accessed=10**7),
        compiler_params=pltpu.CompilerParams(vmem_limit_bytes=60 * 2**20),
    )(*parts)


def line_sum(terms, ways, ident):
    def kernel(terms_ref, out_ref, slots, send, recv):
        me = lax.axis_index("seq")
        barrier = pltpu.get_barrier_semaphore()
        for off in range(1, ways):
            pl.semaphore_signal(
                barrier, inc=1, device_id={"seq": (me + off) % ways}, device_id_type=MESH
            )
        pl.semaphore_wait(barrier, ways - 1)
        for off in range(1, ways):
            remote(
                terms_ref, slots.at[off], send.at[off], recv.at[off], (me + off) % ways
            ).start()
        total = terms_ref[...]
        for off in range(1, ways):
            remote(terms_ref, slots.at[off], send.at[off], recv.at[off], (me + off) % ways).wait_recv()
            total = total + slots[off]
        out_ref[...] = total
        for off in range(1, ways):
            remote(terms_ref, slots.at[off], send.at[off], recv.at[off], (me + off) % ways).wait_send()

    return call(
        kernel,
        [shape(terms.shape, f32)],
        [
            pltpu.VMEM((ways,) + terms.shape, f32),
            pltpu.SemaphoreType.DMA((ways,)),
            pltpu.SemaphoreType.DMA((ways,)),
        ],
        [terms],
        ident,
        8,
    )[0]


def body(
    tokens,
    w_query,
    w_key,
    w_value,
    w_out,
    w_gate,
    w_up,
    w_down,
    gain_query,
    gain_key,
    gain_attn,
    gain_mlp,
    cotangent,
    key_mask,
    lengths,
    tract_order,
):
    ways, groups = lax.axis_size("seq"), lax.axis_size("dp")
    me = lax.axis_index("seq")
    token_rows = tokens[0]
    tok_count, feat_width = token_rows.shape
    ff_width = w_gate.shape[1]
    own_feat = feat_width // ways
    own_heads = own_feat // HEAD_DIM
    own_ff = ff_width // ways
    row_len = tok_count * ways
    score_scale = HEAD_DIM ** (-0.5)
    half_len = tok_count // 2
    order_pair = tract_order[0]
    slot_index = jnp.arange(tok_count, dtype=jnp.int32)
    local_pos = (
        jnp.where(slot_index < half_len, order_pair[0], order_pair[1]) * half_len
        + slot_index % half_len
    )
    key_ok = ((key_mask[0] == 1) & (local_pos < lengths[0])).astype(jnp.int32)

    gain_local = jnp.stack([gain_query, gain_key, gain_attn, gain_mlp], axis=1)
    gain_pad = jnp.pad(gain_local, ((0, 0), (0, HEAD_DIM - 4)))
    gain_all = jnp.tile(gain_pad, (1, ways))
    p_qkv = exchange([w_query, w_key, w_value, gain_all], ways, 8, 20)
    m_qkv = across(p_qkv)
    p_qkv, w_gate, w_up, w_out_t = lax.optimization_barrier(
        (p_qkv, w_gate, w_up, jnp.transpose(w_out))
    )
    p_mid = exchange([w_gate, w_up, w_out_t], ways, 10, 50)
    m_mid = across(p_mid)
    gains = dot_nt(jnp.eye(8, HEAD_DIM, dtype=bf16), m_qkv[:, 3 * own_feat :])
    gain_q = lax.dynamic_slice_in_dim(gains[0], me * own_feat, own_feat, 0)
    gain_k = lax.dynamic_slice_in_dim(gains[1], me * own_feat, own_feat, 0)

    code_pad = -tok_count % HEAD_DIM
    local_code = jnp.pad(local_pos * 2 + key_ok, (0, code_pad))[None]
    local_code, p_mid = lax.optimization_barrier((local_code, p_mid))
    x_row, codes, qkv = gather_project(token_rows, local_code, m_qkv, ways, 1)
    key_code = codes[:, 0, :tok_count].reshape(ways, 2, half_len)
    key_code = jnp.transpose(key_code, (1, 0, 2)).reshape(row_len)
    pos = key_code // 2
    q_raw, k_raw, v_raw = (qkv[:, i * own_feat : (i + 1) * own_feat] for i in range(3))
    squares = line_sum(
        jnp.stack([jnp.sum(q_raw * q_raw, axis=-1), jnp.sum(k_raw * k_raw, axis=-1)]), ways, 2
    )
    squares, w_down_t = lax.optimization_barrier((squares, jnp.transpose(w_down)))
    p_down = lax.all_to_all(w_down_t, "seq", split_axis=1, concat_axis=0, tiled=True)
    factors = jnp.transpose(lax.rsqrt(squares / feat_width + norm_eps))
    cosine, sine = rope_tables(pos, HEAD_DIM)
    key_most = jnp.where(key_code % 2 == 1, jnp.int32(2**30), pos)
    places = [pos[:, None], pos[None], key_most[None]]
    gain_qk = jnp.stack([gain_q, gain_k])
    query_low, key_low, value_low, attn, attn_low, weight_sum = attend(
        [qkv, factors, cosine, sine, gain_qk] + places, min(row_len, 160)
    )

    branch, layer_out, grad_gain_mlp, hidden_low, mixed_low, grad_mlp, grad_gu, first_half, turned = (
        attn_out_and_ff(
            attn_low, m_mid, p_down, token_rows, cotangent[0], gains, groups, ways, 3
        )
    )
    d_gate = dot_tn(hidden_low, grad_gu[:, :own_ff]).astype(bf16)
    grad_gu, d_gate = lax.optimization_barrier((grad_gu, d_gate))
    d_up = dot_tn(hidden_low, grad_gu[:, own_ff:]).astype(bf16)
    grad_gu, d_up = lax.optimization_barrier((grad_gu, d_up))
    d_gate, d_up = dp_sum(d_gate), dp_sum(d_up)
    grad_hidden, grad_gain_attn, grad_branch, grad_attn, d_down = ff_to_attn_back(
        grad_gu, first_half, turned, m_mid, branch, cotangent[0], gains[2:3], grad_mlp, mixed_low, ways, 5
    )
    d_down = dp_sum(d_down)
    c_q, c_k, grad_v, terms, gain_part, dw_gate = attend_back(
        [query_low, key_low, value_low, grad_attn, attn, weight_sum]
        + [cosine, sine, qkv, factors, gain_qk]
        + places,
        d_gate,
        min(row_len, 160),
        ways,
        13,
    )
    terms = jnp.transpose(terms)
    means = line_sum(terms, ways, 6) / feat_width
    q_factor, k_factor = factors[:, :1], factors[:, 1:]
    grad_q_raw = q_factor * (c_q - q_raw * q_factor * means[0][:, None])
    grad_k_raw = k_factor * (c_k - k_raw * k_factor * means[1][:, None])
    grad_qkv = jnp.concatenate(
        [grad_q_raw.astype(bf16), grad_k_raw.astype(bf16), grad_v], axis=1
    )

    own_slot = jnp.zeros((2, feat_width), f32)
    own_slot = lax.dynamic_update_slice(own_slot, gain_part, (0, me * own_feat))
    gain_terms = jnp.concatenate(
        [
            own_slot,
            jnp.sum(grad_gain_attn, axis=0, keepdims=True),
            jnp.sum(grad_gain_mlp, axis=0, keepdims=True),
        ]
    )
    gain_columns = jnp.pad(jnp.transpose(gain_terms), ((0, 0), (0, HEAD_DIM - 4)))
    d_attn, dw_up = attn_grads(
        x_row, grad_qkv, grad_branch, attn_low, gain_columns.astype(bf16), d_up, ways, 14
    )
    dw_gu = [dw_gate.astype(f32), dw_up.astype(f32)]
    grad_qkv, d_attn, dw_gu = lax.optimization_barrier((grad_qkv, d_attn, dw_gu))
    grad_tokens, dw_down = project_back(grad_qkv, m_qkv, grad_hidden, d_down, ways, 7)
    grad_tokens, d_attn = lax.optimization_barrier((grad_tokens, dp_sum(d_attn)))
    dw_gu = [dw_gate.astype(f32), dw_up.astype(f32)]
    dw_qkv = bring_home(d_attn, [own_feat] * 4 + [HEAD_DIM], ways, 12)
    d_query, d_key, d_value, d_out, d_down, layer_out, grad_tokens, gain_grads = finish_grads(
        list(dw_qkv[:4]) + [dw_down], [layer_out, grad_tokens], dw_qkv[4], ways
    )
    return (
        layer_out[None],
        grad_tokens[None],
        d_query,
        d_key,
        d_value,
        jnp.transpose(d_out),
        dw_gu[0],
        dw_gu[1],
        jnp.transpose(d_down),
        gain_grads[0],
        gain_grads[1],
        gain_grads[2],
        gain_grads[3],
    )


def solution(mesh):
    both = ("dp", "seq")
    in_specs = (
        P("dp", "seq", None),
        P(both, None),
        P(both, None),
        P(both, None),
        P(None, both),
        P(both, None),
        P(both, None),
        P(None, both),
        P(both),
        P(both),
        P(both),
        P(both),
        P("dp", "seq", None),
        P("dp", "seq"),
        P("dp"),
        P("dp", "seq"),
    )
    out_specs = (
        P("dp", "seq", None),
        P("dp", "seq", None),
        P(both, None),
        P(both, None),
        P(both, None),
        P(None, both),
        P(both, None),
        P(both, None),
        P(None, both),
        P(both),
        P(both),
        P(both),
        P(both),
    )
    return jax.shard_map(body, mesh=mesh, in_specs=in_specs, out_specs=out_specs, check_vma=False)
```

```python
import functools

import jax
import jax.numpy as jnp
from jax import lax
from jax.experimental import pallas as pl
from jax.experimental.pallas import tpu as pltpu
from jax.sharding import PartitionSpec as P

MESH = pl.DeviceIdType.MESH

HEAD_DIM = 128

rope_base = 500000.0
norm_eps = 1e-06
LOG2_E = 1.4426950408889634
f32 = jnp.float32
bf16 = jnp.bfloat16


def rope_tables(positions, head_dim):
    half_dim = head_dim // 2
    steps_f = jnp.arange(half_dim).astype(f32) * (2.0 / head_dim)
    inv_freq = jnp.power(rope_base, -steps_f)
    angle = positions.astype(f32)[:, None] * inv_freq[None, :]
    angle = jnp.concatenate([angle, angle], axis=-1)
    return (jnp.cos(angle), jnp.sin(angle))


def dot_nn(left, right):
    return jnp.dot(left, right, preferred_element_type=f32)


def dot_nt(left, right):
    return lax.dot_general(left, right, (((1,), (1,)), ((), ())), preferred_element_type=f32)


def dot_tn(left, right):
    return lax.dot_general(left, right, (((0,), (0,)), ((), ())), preferred_element_type=f32)


def across(piece):
    return lax.all_gather(piece, "dp", axis=0, tiled=True)


def dp_sum(grad):
    return lax.psum_scatter(grad, "dp", scatter_dimension=0, tiled=True)


class Line:
    def __init__(self, ways):
        self.chips = ways // 2
        self.last = self.chips - 1
        self.me = lax.axis_index("seq")
        self.chip = self.me // 2
        self.core = self.me % 2
        self.sibling = self.me + 1 - 2 * self.core

    def greet(self, groups=1):
        barrier = pltpu.get_barrier_semaphore()
        group = lax.axis_index("dp")
        for off in range(1, groups):
            pl.semaphore_signal(
                barrier, inc=1, device_id={"dp": (group + off) % groups}, device_id_type=MESH
            )
        has_low = jnp.minimum(self.chip, 1)
        has_high = jnp.minimum(self.last - self.chip, 1)
        pl.semaphore_signal(barrier, inc=1, device_id={"seq": self.sibling}, device_id_type=MESH)

        @pl.when(self.chip > 0)
        def _():
            pl.semaphore_signal(barrier, inc=1, device_id={"seq": self.me - 2}, device_id_type=MESH)

        @pl.when(self.chip < self.last)
        def _():
            pl.semaphore_signal(barrier, inc=1, device_id={"seq": self.me + 2}, device_id_type=MESH)

        pl.semaphore_wait(barrier, groups + has_low + has_high)


def remote(src, dst, send_sem, recv_sem, device):
    return pltpu.make_async_remote_copy(
        src_ref=src,
        dst_ref=dst,
        send_sem=send_sem,
        recv_sem=recv_sem,
        device_id={"seq": device},
        device_id_type=MESH,
    )


def rows_at(index, count):
    return pl.ds(pl.multiple_of(index * count, count), count)


def each_strip(tok_count, strip, fn):
    def one(i, carry):
        fn(rows_at(i, strip))
        return carry

    lax.fori_loop(0, tok_count // strip, one, 0)


class RowGather:
    def __init__(self, line, half, buf, sems):
        self.line, self.half, self.buf = line, half, buf
        self.up_send, self.down_send, self.col_recv, self.sib_send, self.sib_recv = sems

    @staticmethod
    def scratch(chips):
        return [pltpu.SemaphoreType.DMA((2 * chips,))] * 5

    def piece(self, src, core, h):
        return self.buf.at[rows_at(h * 2 * self.line.chips + 2 * src + core, self.half)]

    def hop(self, src, h, device, send):
        piece, at = self.piece(src, self.line.core, h), h * self.line.chips + src
        return remote(piece, piece, send.at[at], self.col_recv.at[at], device)

    def swap(self, src, core, h):
        piece, at = self.piece(src, core, h), h * self.line.chips + src
        return remote(piece, piece, self.sib_send.at[at], self.sib_recv.at[at], self.line.sibling)

    def start(self, h):
        line = self.line
        self.forward_up(line.chip, h)
        self.forward_down(line.chip, h)
        self.swap(line.chip, line.core, h).start()

    def forward_up(self, src, h):
        @pl.when(self.line.chip < self.line.last)
        def _():
            self.hop(src, h, self.line.me + 2, self.up_send).start()

    def forward_down(self, src, h):
        @pl.when(self.line.chip > 0)
        def _():
            self.hop(src, h, self.line.me - 2, self.down_send).start()

    def receive(self, away, h):
        line = self.line
        low, high = line.chip - away, line.chip + away

        @pl.when(low >= 0)
        def _():
            self.hop(low, h, line.sibling, self.up_send).wait_recv()
            self.forward_up(low, h)
            self.swap(low, line.core, h).start()

        @pl.when(high <= line.last)
        def _():
            self.hop(high, h, line.sibling, self.down_send).wait_recv()
            self.forward_down(high, h)
            self.swap(high, line.core, h).start()

    def use_at(self, away, h, use):
        line = self.line

        def one(side, carry):
            src = line.chip + (2 * side - 1) * away

            @pl.when((src >= 0) & (src <= line.last) & (away + 1 > side))
            def _():
                self.swap(src, 1 - line.core, h).wait_recv()
                use(src, h)

            return carry

        lax.fori_loop(0, 2, one, 0)

    def finish(self):
        line = self.line
        for h in (0, 1):

            def one(src, carry, h=h):
                self.swap(src, line.core, h).wait_send()

                @pl.when((src <= line.chip) & (line.chip < line.last))
                def _():
                    self.hop(src, h, line.sibling, self.up_send).wait_send()

                @pl.when((src >= line.chip) & (line.chip > 0))
                def _():
                    self.hop(src, h, line.sibling, self.down_send).wait_send()

                return carry

            lax.fori_loop(0, line.chips, one, 0)


class RowScatter:
    def __init__(self, line, half, bufs, sems):
        self.line, self.half = line, half
        self.pair, self.sib_in, self.acc = bufs
        self.sib_send, self.sib_recv, self.send, self.recv = sems

    @staticmethod
    def scratch(chips, tok, width):
        return [
            pltpu.VMEM((2 * chips * tok, width), bf16),
            pltpu.VMEM((chips * tok, width), bf16),
            pltpu.VMEM(((chips + 1) * tok, width), bf16),
            pltpu.SemaphoreType.DMA((2 * chips,)),
            pltpu.SemaphoreType.DMA((2 * chips,)),
            pltpu.SemaphoreType.DMA((2 * chips,)),
            pltpu.SemaphoreType.DMA((2 * (chips + 1),)),
        ]

    def of(self, left, right, tile, joined, turned=False):
        self.left, self.right, self.tile = left, right, tile
        self.joined, self.turned = joined, turned
        return self

    def swap(self, dest, h):
        half, line = self.half, self.line
        at = h * line.chips + dest
        return remote(
            self.pair.at[rows_at(2 * at + 1 - line.core, half)],
            self.sib_in.at[rows_at(at, half)],
            self.sib_send.at[at],
            self.sib_recv.at[at],
            line.sibling,
        )

    def hop(self, dest, slot, h, device):
        half, slots = self.half, self.line.chips + 1
        return remote(
            self.acc.at[rows_at(h * slots + dest, half)],
            self.acc.at[rows_at(h * slots + slot, half)],
            self.send.at[h * self.line.chips + dest],
            self.recv.at[h * slots + slot],
            device,
        )

    def produce(self, dest, h):
        if self.joined and h:
            return
        spans = [rows_at(h * self.line.chips + dest, 2 * self.half)]
        if self.joined:
            spans.append(rows_at(self.line.chips + dest, 2 * self.half))

        def one(n, carry):
            cols = rows_at(n, self.tile)
            left = [self.left[span, :] for span in spans]
            left = jnp.concatenate(left, axis=0) if self.joined else left[0]
            if self.turned:
                part = dot_nn(left, self.right[:, cols]).astype(bf16)
            else:
                part = dot_nt(left, self.right[cols, :]).astype(bf16)
            for i, span in enumerate(spans):
                self.pair[span, cols] = part[i * 2 * self.half : (i + 1) * 2 * self.half]
            return carry

        lax.fori_loop(0, self.right.shape[1 if self.turned else 0] // self.tile, one, 0)
        for i in range(len(spans)):
            self.swap(dest, h + i).start()

    def strip_of(self, index, strip):
        return pl.ds(pl.multiple_of(index * self.half + strip.start, 16), strip.size)

    def chip_sum(self, dest, h, strip):
        at = h * self.line.chips + dest
        mine = self.pair[self.strip_of(2 * at + self.line.core, strip), :]
        other = self.sib_in[self.strip_of(at, strip), :]
        return mine.astype(f32) + other.astype(f32)

    def legs(self, s):
        line = self.line
        below, above = line.chip, line.last - line.chip
        return (
            (line.last - s + below, 1, below, (s >= below) & (s < line.last)),
            (s - above, -1, above, (s >= above) & (s < line.last)),
        )

    def make(self, s, h):
        line = self.line
        if self.joined and h:
            return
        (up, _, _, has_up), (down, _, _, has_down) = self.legs(s)

        def one(k, carry):
            own, low = k // 2, k % 2
            dest = own * line.chip + (1 - own) * ((1 - low) * up + low * down)
            there = ((k == 0) & has_up) | ((k == 1) & has_down) | ((k == 2) & (s == line.last))

            @pl.when(there)
            def _():
                self.produce(dest, h)

            return carry

        lax.fori_loop(0, 3, one, 0)

    def pass_on(self, s, h):
        line = self.line
        chips, slots = line.chips, line.chips + 1
        for dest, step, behind, there in self.legs(s):
            if step > 0:
                slot = dest
            else:
                ends = 1 - jnp.minimum(line.chip - 1 - dest, 1)
                slot = dest + ends * (chips - dest)

            @pl.when(there)
            def _(dest=dest, behind=behind, slot=slot, step=step):
                self.swap(dest, h).wait_recv()

                @pl.when(behind > 0)
                def _():
                    self.hop(dest, dest, h, line.sibling).wait_recv()

                    def add(strip):
                        at = self.strip_of(h * slots + dest, strip)
                        total = self.chip_sum(dest, h, strip) + self.acc[at, :].astype(f32)
                        self.acc[at, :] = total.astype(bf16)

                    each_strip(self.half, 16, add)

                @pl.when(behind == 0)
                def _():
                    def put(strip):
                        at = self.strip_of(h * slots + dest, strip)
                        self.acc[at, :] = self.chip_sum(dest, h, strip).astype(bf16)

                    each_strip(self.half, 16, put)

                self.hop(dest, slot, h, line.me + 2 * step).start()

    def close(self, h):
        line = self.line
        chips, slots = line.chips, line.chips + 1
        empty = jnp.zeros((self.half, self.acc.shape[1]), bf16)
        self.swap(line.chip, h).wait_recv()

        @pl.when(line.chip > 0)
        def _():
            self.hop(line.chip, line.chip, h, line.sibling).wait_recv()

        @pl.when(line.chip == 0)
        def _():
            self.acc[rows_at(h * slots + line.chip, self.half), :] = empty

        @pl.when(line.chip < line.last)
        def _():
            self.hop(line.chip, chips, h, line.sibling).wait_recv()

        @pl.when(line.chip == line.last)
        def _():
            self.acc[rows_at(h * slots + chips, self.half), :] = empty

    def total(self, h, strip):
        line = self.line
        slots = line.chips + 1
        low = self.acc[self.strip_of(h * slots + line.chip, strip), :].astype(f32)
        high = self.acc[self.strip_of(h * slots + line.chips, strip), :].astype(f32)
        return self.chip_sum(line.chip, h, strip) + (low + high)

    def finish(self, h):
        line = self.line

        def one(dest, carry):
            self.swap(dest, h).wait_send()

            @pl.when(line.chip != dest)
            def _():
                self.hop(dest, dest, h, line.sibling).wait_send()

            return carry

        lax.fori_loop(0, line.chips, one, 0)


def advance(scatter=None, sh=0, gather=None, gh=0, use=None, fill=None, settle=None):
    line = (scatter or gather).line

    def slot(i, carry):
        s = i - 1
        if gather:

            @pl.when((s > 0) & (s < line.chips))
            def _():
                gather.receive(s, gh)

        if scatter:
            scatter.pass_on(s, sh)
            scatter.make(s + 1, sh)
        if settle:

            @pl.when(s == line.chips)
            def _():
                settle()

        if gather:

            @pl.when(s > 0)
            def _():
                gather.use_at(s - 1, gh, use)

        if fill:

            @pl.when((s >= 0) & (s < line.chips))
            def _():
                fill(s)

        return carry

    lax.fori_loop(0, line.chips + 2, slot, 0)


def mean_rows(values):
    return jnp.sum(values, axis=-1, keepdims=True) * (1.0 / values.shape[-1])


class Blocks:
    def __init__(self, line, count, pairs, sems):
        self.line, self.count, self.pairs, self.sems = line, count, pairs, sems

    def copy(self, i, index):
        src, dst = self.pairs[i]
        at = rows_at(index, self.count)
        return pltpu.make_async_copy(src.at[at], dst.at[at], self.sems.at[i, index])

    def send(self, i, chip, h):
        self.copy(i, h * self.line.chips + chip).start()

    def finish(self):
        def one(index, carry):
            for i in range(len(self.pairs)):
                self.copy(i, index).wait()
            return carry

        lax.fori_loop(0, 2 * self.line.chips, one, 0)


def call(kernel, outs, scratch, args, ident, cost=1, far_in=(), far_out=()):
    def space(i, far):
        return pl.BlockSpec(memory_space=pl.ANY if i in far else pltpu.VMEM)

    return pl.pallas_call(
        kernel,
        out_shape=outs,
        in_specs=[space(i, far_in) for i in range(len(args))],
        out_specs=[space(i, far_out) for i in range(len(outs))],
        scratch_shapes=scratch,
        cost_estimate=pl.CostEstimate(
            flops=cost * 10**9, transcendentals=0, bytes_accessed=cost * 3 * 10**6
        ),
        compiler_params=pltpu.CompilerParams(
            collective_id=ident, has_side_effects=True, vmem_limit_bytes=63 * 2**20
        ),
    )(*args)


def shape(dims, kind):
    return jax.ShapeDtypeStruct(dims, kind)


def gather_project(rows, codes, weights, ways, ident):
    tok, width = rows.shape
    cols = weights.shape[1] - HEAD_DIM
    half = tok // 2

    def kernel(
        rows_ref, code_ref, w_far, all_far, codes_ref, prod_far,
        w_ref, all_ref, prod_ref, w_sem, out_sem, code_send, code_recv, *sems
    ):
        line = Line(ways)
        w_copy = pltpu.make_async_copy(w_far.at[:, pl.ds(0, cols)], w_ref, w_sem)
        w_copy.start()
        outs = Blocks(line, 2 * half, [(all_ref, all_far), (prod_ref, prod_far)], out_sem)
        me = line.me
        barrier = pltpu.get_barrier_semaphore()
        for off in range(1, ways):
            pl.semaphore_signal(
                barrier, inc=1, device_id={"seq": (me + off) % ways}, device_id_type=MESH
            )
        pl.semaphore_wait(barrier, ways - 1)
        gather = RowGather(line, half, all_ref, sems)
        for h in (0, 1):
            all_ref[rows_at(h * ways + me, half), :] = rows_ref[pl.ds(h * half, half), :]
            gather.start(h)
        codes_ref[me] = code_ref[...]

        def tell(off):
            return remote(
                code_ref, codes_ref.at[me], code_send.at[off], code_recv.at[off], (me + off) % ways
            )

        for off in range(1, ways):
            tell(off).start()

        def use(chip, h):
            at = rows_at(h * line.chips + chip, 2 * half)

            prod_ref[at, :] = dot_nn(all_ref[at, :], w_ref[...])
            outs.send(0, chip, h)
            outs.send(1, chip, h)

        def step(j, carry):
            def one(h, carry):
                @pl.when(j < line.chips)
                def _():
                    gather.receive(j, h)

                gather.use_at(j - 1, h, use)
                return carry

            return lax.fori_loop(0, 2, one, carry)

        w_copy.wait()
        lax.fori_loop(1, line.chips + 1, step, 0)
        gather.finish()
        outs.finish()
        for off in range(1, ways):
            tell(off).wait()

    return call(
        kernel,
        [
            shape((ways * tok, width), bf16),
            shape((ways,) + codes.shape, jnp.int32),
            shape((ways * tok, cols), f32),
        ],
        [
            pltpu.VMEM((width, cols), bf16),
            pltpu.VMEM((ways * tok, width), bf16),
            pltpu.VMEM((ways * tok, cols), f32),
            pltpu.SemaphoreType.DMA,
            pltpu.SemaphoreType.DMA((2, ways)),
            pltpu.SemaphoreType.DMA((ways,)),
            pltpu.SemaphoreType.DMA((ways,)),
        ]
        + RowGather.scratch(ways // 2),
        [rows, codes, weights],
        ident,
        55,
        (2,),
        (0, 2),
    )


def attn_out_and_ff(attn_low, m_mid, p_down, token_rows, grad_out, gains, groups, ways, ident):
    tok, width = token_rows.shape
    half = tok // 2
    own_feat, own_ff = attn_low.shape[1], p_down.shape[1]
    part = p_down.shape[0]
    row = ways * tok
    tile = min(own_ff, 1024)
    square = width == 2 * own_ff
    square_tile = 256
    squares = width // square_tile

    def kernel(
        left_far, mid_far, down_far, x_far, go_far, gains_ref,
        branch_far, out_ref, gg_ref, hid_far, mix_far, gm_far, dgu_far, first_ref, turned_far,
        left, mid_ref, down_ref, x_ref, go_ref, branch_ref, hid_ref, mix_ref, gm_ref, dgu_ref,
        down_turned, turned_sem, in_sem, out_sem, branch_sem, down_send, down_recv, *rest
    ):
        line = Line(ways)
        group = lax.axis_index("dp")
        gu_cols, out_cols = pl.ds(0, 2 * own_ff), pl.ds(2 * own_ff, own_feat)
        fetch = [
            pltpu.make_async_copy(src, dst, in_sem.at[i])
            for i, (src, dst) in enumerate(
                [
                    (left_far, left),
                    (mid_far.at[:, out_cols], mid_ref.at[:, out_cols]),
                    (x_far, x_ref),
                    (mid_far.at[:, gu_cols], mid_ref.at[:, gu_cols]),
                    (down_far, down_ref.at[rows_at(group, part)]),
                    (go_far, go_ref),
                ]
            )
        ]
        for copy in fetch:
            copy.start()
        outs = Blocks(
            line,
            2 * half,
            [(hid_ref, hid_far), (mix_ref, mix_far), (gm_ref, gm_far), (dgu_ref, dgu_far)],
            out_sem,
        )
        keep_branch = pltpu.make_async_copy(branch_ref, branch_far, branch_sem)
        line.greet(groups)

        def spread(off):
            return pltpu.make_async_remote_copy(
                src_ref=down_far,
                dst_ref=down_ref.at[rows_at(group, part)],
                send_sem=down_send.at[off],
                recv_sem=down_recv.at[off],
                device_id={"dp": (group + off) % groups},
                device_id_type=MESH,
            )

        for off in range(1, groups):
            spread(off).start()
        scatter = RowScatter(line, half, rest[:3], rest[3:7])
        hidden = RowGather(line, half, hid_ref, rest[7:12])
        back = RowGather(line, half, gm_ref, rest[12:17])
        gg_ref[...] = jnp.zeros_like(gg_ref)
        gain_attn, gain_mlp = gains_ref[2:3, :], gains_ref[3:4, :]

        def own(h, strip):
            return pl.ds(pl.multiple_of((h * ways + line.me) * half + strip.start, 16), strip.size)

        def residual(at):
            branch = branch_ref[at, :]
            factor = lax.rsqrt(mean_rows(branch * branch) + norm_eps)
            return x_ref[at, :].astype(f32) + branch * factor * gain_attn

        def settle_attn(h):
            def one(strip):
                at = pl.ds(pl.multiple_of(h * half + strip.start, 16), strip.size)
                branch_ref[at, :] = scatter.total(h, strip)
                hid_ref[own(h, strip), :] = residual(at).astype(bf16)

            scatter.close(h)
            each_strip(half, 16, one)
            hidden.start(h)
            scatter.finish(h)

        def settle_mlp(h):
            def one(strip):
                at = pl.ds(pl.multiple_of(h * half + strip.start, 16), strip.size)
                mlp = scatter.total(h, strip)
                factor = lax.rsqrt(mean_rows(mlp * mlp) + norm_eps)
                unit = mlp * factor
                lifted = go_ref[at, :].astype(f32) * gain_mlp
                turned = factor * (lifted - unit * mean_rows(lifted * unit))
                gm_ref[own(h, strip), :] = turned.astype(bf16)

            def rest_of(strip):
                at = pl.ds(pl.multiple_of(h * half + strip.start, 16), strip.size)
                mlp = scatter.total(h, strip)
                unit = mlp * lax.rsqrt(mean_rows(mlp * mlp) + norm_eps)
                out_ref[at, :] = (residual(at) + unit * gain_mlp).astype(bf16)
                terms = go_ref[at, :].astype(f32) * unit
                gg_ref[...] += terms[:8] + terms[8:]

            scatter.close(h)
            each_strip(half, 16, one)
            back.start(h)
            each_strip(half, 16, rest_of)
            scatter.finish(h)

        def gate_up(chip, h):
            at = rows_at(h * line.chips + chip, 2 * half)

            outs.send(0, chip, h)

            both = dot_nn(hid_ref[at, :], mid_ref[:, gu_cols])
            gate, up = both[:, :own_ff], both[:, own_ff:]
            dgu_ref[at, :] = both.astype(bf16)
            mix_ref[at, :] = (gate * jax.nn.sigmoid(gate) * up).astype(bf16)
            outs.send(1, chip, h)

        def gate_up_back(chip, h):
            at = rows_at(h * line.chips + chip, 2 * half)

            outs.send(2, chip, h)

            def one(n, carry):
                here, there = rows_at(n, tile), pl.ds(pl.multiple_of(own_ff + n * tile, tile), tile)
                grad = dot_nn(gm_ref[at, :], down_ref[:, here])
                gate, up = dgu_ref[at, here].astype(f32), dgu_ref[at, there].astype(f32)
                sigma = jax.nn.sigmoid(gate)
                dgu_ref[at, here] = (grad * up * sigma * (1.0 + gate * (1.0 - sigma))).astype(bf16)
                dgu_ref[at, there] = (grad * gate * sigma).astype(bf16)
                return carry

            lax.fori_loop(0, own_ff // tile, one, 0)
            outs.send(3, chip, h)

        for copy in fetch[:3]:
            copy.wait()
        scatter.of(left, mid_ref.at[:, out_cols], 1024, True)
        advance(scatter, 0, settle=lambda: settle_attn(0))
        fetch[3].wait()
        advance(scatter, 1, hidden, 0, gate_up, settle=lambda: settle_attn(1))

        def turn_down(i, carry):
            rows = rows_at(i, square_tile)
            down_turned[:, rows] = down_ref[rows, :].T
            return carry

        def turn_square(s):
            def one(i, carry):
                def two(j, carry):
                    rows, cols = rows_at(i, square_tile), rows_at(j, square_tile)
                    block, other = mid_ref[rows, cols], mid_ref[cols, rows]
                    mid_ref[cols, rows] = block.T
                    mid_ref[rows, cols] = other.T
                    return carry

                return lax.fori_loop(i, squares, two, carry)

            lax.fori_loop(s * squares // line.chips, (s + 1) * squares // line.chips, one, 0)

        keep_branch.start()
        for copy in fetch[4:]:
            copy.wait()
        for off in range(1, groups):
            spread(off).wait()
        if square:
            lax.fori_loop(0, squares, turn_down, 0)
            scatter.of(mix_ref, down_turned, 2048, False, True)
        else:
            scatter.of(mix_ref, down_ref, 2048, False)
        advance(scatter, 0, hidden, 1, gate_up, settle=lambda: settle_mlp(0))
        advance(
            scatter, 1, back, 0, gate_up_back, turn_square if square else None, lambda: settle_mlp(1)
        )
        keep_turned = pltpu.make_async_copy(mid_ref.at[:, gu_cols], turned_far, turned_sem)
        keep_turned.start()
        scatter.of(dgu_ref, mid_ref.at[:, gu_cols], 1024, False, square)

        def keep_first():
            def put(strip):
                first_ref[strip, :] = scatter.total(0, strip)

            scatter.close(0)
            each_strip(half, 16, put)
            scatter.finish(0)

        advance(scatter, 0, back, 1, gate_up_back, settle=keep_first)
        hidden.finish()
        back.finish()
        keep_branch.wait()
        keep_turned.wait()
        outs.finish()

    return call(
        kernel,
        [
            shape((tok, width), f32),
            shape((tok, width), bf16),
            shape((8, width), f32),
            shape((row, width), bf16),
            shape((row, own_ff), bf16),
            shape((row, width), bf16),
            shape((row, 2 * own_ff), bf16),
            shape((half, width), f32),
            shape((width, 2 * own_ff), bf16),
        ],
        [
            pltpu.VMEM((row, own_feat), bf16),
            pltpu.VMEM(m_mid.shape, bf16),
            pltpu.VMEM((groups * part, own_ff), bf16),
            pltpu.VMEM((tok, width), bf16),
            pltpu.VMEM((tok, width), bf16),
            pltpu.VMEM((tok, width), f32),
            pltpu.VMEM((row, width), bf16),
            pltpu.VMEM((row, own_ff), bf16),
            pltpu.VMEM((row, width), bf16),
            pltpu.VMEM((row, 2 * own_ff), bf16),
            pltpu.VMEM((own_ff, width) if square else (16, HEAD_DIM), bf16),
            pltpu.SemaphoreType.DMA,
            pltpu.SemaphoreType.DMA((6,)),
            pltpu.SemaphoreType.DMA((4, ways)),
            pltpu.SemaphoreType.DMA,
            pltpu.SemaphoreType.DMA((groups,)),
            pltpu.SemaphoreType.DMA((groups,)),
        ]
        + RowScatter.scratch(ways // 2, tok, width)
        + RowGather.scratch(ways // 2)
        + RowGather.scratch(ways // 2),
        [attn_low, m_mid, p_down, token_rows, grad_out, gains],
        ident,
        150,
        range(5),
        (0, 3, 4, 5, 6, 8),
    )


def ff_to_attn_back(
    grad_gu, first_half, turned, m_mid, branch, grad_out, gain_row, grad_mlp, mixed_low, ways, ident
):
    tok, width = branch.shape
    half = tok // 2
    own_ff = grad_gu.shape[1] // 2
    own_feat = m_mid.shape[1] - 2 * own_ff
    row = ways * tok
    tiles = width // 256

    def kernel(
        left_far, first_ref, turned_far, w_far, br_ref, go_ref, gain_ref, gm_far, mix_far,
        gh_ref, gg_ref, all_far, ga_ref, dd_far,
        left, turned_ref, w_ref, in_sem, all_ref, out_sem, gm_ref, mix_ref, dd_ref, gm_sem, mix_sem, dd_sem, *rest
    ):
        line = Line(ways)
        wanted = [
            pltpu.make_async_copy(w_far.at[:, pl.ds(2 * own_ff, own_feat)], w_ref, in_sem.at[0]),
            pltpu.make_async_copy(turned_far, turned_ref, in_sem.at[2]),
            pltpu.make_async_copy(left_far, left, in_sem.at[1]),
        ]
        for copy in wanted:
            copy.start()
        mix_copy = pltpu.make_async_copy(mix_far, mix_ref, mix_sem)

        def fetch(i):
            return pltpu.make_async_copy(
                gm_far.at[:, rows_at(i, 256)], gm_ref.at[i % 2], gm_sem.at[i % 2]
            )

        def keep(i):
            rows = rows_at(i, 256)
            return pltpu.make_async_copy(dd_ref.at[rows], dd_far.at[rows], dd_sem.at[i])

        def down_grad(i, carry):
            fetch(i).wait()

            @pl.when(i + 1 < tiles)
            def _():
                fetch(i + 1).start()

            dd_ref[rows_at(i, 256), :] = dot_tn(gm_ref[i % 2], mix_ref[...]).astype(bf16)
            keep(i).start()
            return carry

        def fill(s):
            lax.fori_loop(s * tiles // line.chips, (s + 1) * tiles // line.chips, down_grad, 0)

        outs = Blocks(line, 2 * half, [(all_ref, all_far)], out_sem)
        line.greet()
        scatter = RowScatter(line, half, rest[:3], rest[3:7])
        gather = RowGather(line, half, all_ref, rest[7:])
        gg_ref[...] = jnp.zeros_like(gg_ref)

        def settle(h):
            def one(strip):
                at = pl.ds(pl.multiple_of(h * half + strip.start, 16), strip.size)
                mine = pl.ds(
                    pl.multiple_of((h * ways + line.me) * half + strip.start, 16), strip.size
                )
                total = scatter.total(h, strip) if h else first_ref[strip, :]
                grad = total + go_ref[at, :].astype(f32)
                branch = br_ref[at, :]
                factor = lax.rsqrt(mean_rows(branch * branch) + norm_eps)
                unit = branch * factor
                gh_ref[at, :] = grad
                terms = grad * unit
                gg_ref[...] += terms[:8] + terms[8:]
                lifted = grad * gain_ref[...]
                turned = factor * (lifted - unit * mean_rows(lifted * unit))
                all_ref[mine, :] = turned.astype(bf16)

            if h:
                scatter.close(h)
            each_strip(half, 16, one)
            gather.start(h)

        def use(chip, h):
            at = rows_at(h * line.chips + chip, 2 * half)
            outs.send(0, chip, h)
            ga_ref[at, :] = dot_nn(all_ref[at, :], w_ref[...])

        scatter.of(left, turned_ref, 1024, False, width == 2 * own_ff)
        settle(0)
        for copy in wanted:
            copy.wait()
        advance(scatter, 1, gather, 0, use, settle=lambda: settle(1))
        mix_copy.start()
        fetch(0).start()
        mix_copy.wait()
        advance(None, 0, gather, 1, use, fill)
        gather.finish()
        outs.finish()
        for i in range(tiles):
            keep(i).wait()
        scatter.finish(1)

    return call(
        kernel,
        [
            shape((tok, width), f32),
            shape((8, width), f32),
            shape((row, width), bf16),
            shape((row, own_feat), f32),
            shape((width, own_ff), bf16),
        ],
        [
            pltpu.VMEM(grad_gu.shape, bf16),
            pltpu.VMEM(turned.shape, bf16),
            pltpu.VMEM((width, own_feat), bf16),
            pltpu.SemaphoreType.DMA((3,)),
            pltpu.VMEM((row, width), bf16),
            pltpu.SemaphoreType.DMA((1, ways)),
            pltpu.VMEM((2, row, 256), bf16),
            pltpu.VMEM((row, own_ff), bf16),
            pltpu.VMEM((width, own_ff), bf16),
            pltpu.SemaphoreType.DMA((2,)),
            pltpu.SemaphoreType.DMA,
            pltpu.SemaphoreType.DMA((tiles,)),
        ]
        + RowScatter.scratch(ways // 2, tok, width)
        + RowGather.scratch(ways // 2),
        [grad_gu, first_half, turned, m_mid, branch, grad_out, gain_row, grad_mlp, mixed_low],
        ident,
        70,
        (0, 2, 3, 7, 8),
        (2, 4),
    )


def home_copies(me, ways, source, targets, widths, send, recv):
    rows = source.shape[0] // ways
    begins = [sum(widths[:i]) for i in range(len(widths))]
    count = len(widths)

    def part(i, dest):
        return (
            source.at[rows_at(dest, rows), pl.ds(begins[i], widths[i])],
            targets[i].at[:, rows_at(me, widths[i])],
        )

    def move(off, i):
        dest = (me + off) % ways
        return remote(*part(i, dest), send.at[off * count + i], recv.at[off * count + i], dest)

    def keep(i):
        return pltpu.make_async_copy(*part(i, me), send.at[i])

    def each(what):
        def one(off, carry):
            for i in range(count):
                what(move(off, i))
            return carry

        lax.fori_loop(1, ways, one, 0)

    def start():
        for i in range(count):
            keep(i).start()
        each(lambda copy: copy.start())

    def wait():
        for i in range(count):
            keep(i).wait()
        each(lambda copy: copy.wait())

    return start, wait


def greet_line(me, ways):
    barrier = pltpu.get_barrier_semaphore()

    def greet(off, carry):
        pl.semaphore_signal(
            barrier, inc=1, device_id={"seq": (me + off) % ways}, device_id_type=MESH
        )
        return carry

    lax.fori_loop(1, ways, greet, 0)
    pl.semaphore_wait(barrier, ways - 1)


def bring_home(summed, widths, ways, ident):
    rows = summed.shape[0] // ways
    count = len(widths)

    def kernel(*refs):
        source, targets, (send, recv) = refs[0], refs[1 : 1 + count], refs[1 + count :]
        me = lax.axis_index("seq")
        greet_line(me, ways)
        start, wait = home_copies(me, ways, source, targets, widths, send, recv)
        start()
        wait()

    return call(
        kernel,
        [shape((rows, ways * width), bf16) for width in widths],
        [pltpu.SemaphoreType.DMA((ways * count,))] * 2,
        [summed],
        ident,
        30,
        (0,),
        range(count),
    )


def project_back(grad_qkv, m_qkv, grad_hidden, d_down, ways, ident):
    tok, width = grad_hidden.shape
    half = tok // 2
    own_ff = d_down.shape[1]

    def kernel(left, w_ref, gh_ref, dd_ref, out_ref, home_ref, dd_send, dd_recv, *rest):
        line = Line(ways)
        greet_line(line.me, ways)
        start, wait = home_copies(line.me, ways, dd_ref, [home_ref], [own_ff], dd_send, dd_recv)
        start()
        scatter = RowScatter(line, half, rest[:3], rest[3:7])
        scatter.of(left, w_ref.at[:, pl.ds(0, left.shape[1])], 1024, True)
        for h in (0, 1):
            advance(scatter, h)
        for h in (0, 1):

            def one(strip, h=h):
                at = pl.ds(pl.multiple_of(h * half + strip.start, 16), strip.size)
                out_ref[at, :] = (gh_ref[at, :] + scatter.total(h, strip)).astype(bf16)

            scatter.close(h)
            each_strip(half, 16, one)
        for h in (0, 1):
            scatter.finish(h)
        wait()

    return call(
        kernel,
        [
            shape((tok, width), bf16),
            shape((d_down.shape[0] // ways, ways * own_ff), bf16),
        ],
        [pltpu.SemaphoreType.DMA((ways,))] * 2 + RowScatter.scratch(ways // 2, tok, width),
        [grad_qkv, m_qkv, grad_hidden, d_down],
        ident,
        65,
        (3,),
        (1,),
    )


def half_turn(values, sign):
    half_dim = HEAD_DIM // 2
    lane = lax.broadcasted_iota(jnp.int32, values.shape, 1)
    swapped = pltpu.roll(values, half_dim, 1)
    return jnp.where(lane < half_dim, -sign * swapped, sign * swapped)


def attend(parts, block):
    row = parts[0].shape[0]
    width = parts[0].shape[1] // 3
    heads = width // HEAD_DIM
    scale = HEAD_DIM ** (-0.5)

    def kernel(
        qkv_ref, factor_ref, cos_ref, sin_ref, gain_ref, qpos_ref, kpos_ref, kmax_ref,
        q_ref, k_ref, v_ref, at_ref, low_ref, ws_ref
    ):
        def turn(i, carry):
            rows = rows_at(i, block)
            cosine, sine = cos_ref[rows, :], sin_ref[rows, :]
            for which, out_ref in ((0, q_ref), (1, k_ref)):
                factor = factor_ref[rows, pl.ds(which, 1)]
                for head in range(heads):
                    lanes = pl.ds(head * HEAD_DIM, HEAD_DIM)
                    raw = qkv_ref[rows, pl.ds(which * width + head * HEAD_DIM, HEAD_DIM)]
                    normed = raw * factor * gain_ref[which : which + 1, lanes]
                    out_ref[rows, lanes] = (
                        normed * cosine + half_turn(normed, 1.0) * sine
                    ).astype(bf16)
            v_ref[rows, :] = qkv_ref[rows, pl.ds(2 * width, width)].astype(bf16)
            return carry

        lax.fori_loop(0, row // block, turn, 0)

        def one(i, carry):
            rows = rows_at(i, block)
            qpos = qpos_ref[rows, :]
            mask = (kpos_ref[...] <= qpos) & (qpos <= kmax_ref[...])
            for head in range(heads):
                lanes = pl.ds(head * HEAD_DIM, HEAD_DIM)
                scores = dot_nt(q_ref[rows, lanes], k_ref[:, lanes]) * (scale * LOG2_E)
                expo = jnp.where(mask, jnp.exp2(scores), 0.0)
                total = jnp.sum(expo, axis=-1, keepdims=True)
                result = dot_nn(expo.astype(bf16), v_ref[:, lanes]) / total
                ws_ref[rows, pl.ds(head, 1)] = total
                at_ref[rows, lanes] = result
                low_ref[rows, lanes] = result.astype(bf16)
            return carry

        lax.fori_loop(0, row // block, one, 0)

    return pl.pallas_call(
        kernel,
        out_shape=[shape((row, width), bf16)] * 3
        + [shape((row, width), f32), shape((row, width), bf16), shape((row, heads), f32)],
        in_specs=[pl.BlockSpec(memory_space=pltpu.VMEM)] * len(parts),
        out_specs=[pl.BlockSpec(memory_space=pltpu.VMEM)] * 6,
        cost_estimate=pl.CostEstimate(
            flops=4 * row * row * width, transcendentals=row * row * heads, bytes_accessed=60 * 10**6
        ),
        compiler_params=pltpu.CompilerParams(vmem_limit_bytes=60 * 2**20),
    )(*parts)


def attend_back(parts, summed, block, ways, ident):
    row, width = parts[0].shape
    heads = width // HEAD_DIM
    scale = HEAD_DIM ** (-0.5)

    def kernel(
        q_ref, k_ref, v_ref, ga_ref, at_ref, ws_ref, cos_ref, sin_ref, qkv_ref, factor_ref,
        gain_ref, qpos_ref, kpos_ref, kmax_ref, sum_ref,
        cq_ref, ck_ref, dv_ref, terms_ref, gg_ref, home_ref, dk_acc, dv_acc, send, recv
    ):
        me = lax.axis_index("seq")
        greet_line(me, ways)
        start, wait = home_copies(me, ways, sum_ref, [home_ref], [summed.shape[1]], send, recv)
        start()
        gg_ref[...] = jnp.zeros_like(gg_ref)
        dk_acc[...] = jnp.zeros_like(dk_acc)
        dv_acc[...] = jnp.zeros_like(dv_acc)

        def turn_back(grad, rows, which, out_ref, head):
            lanes = pl.ds(head * HEAD_DIM, HEAD_DIM)
            cosine, sine = cos_ref[rows, :], sin_ref[rows, :]
            normed = grad * cosine + half_turn(grad * sine, -1.0)
            raw = qkv_ref[rows, pl.ds(which * width + head * HEAD_DIM, HEAD_DIM)]
            unit = raw * factor_ref[rows, pl.ds(which, 1)]
            gg_ref[which : which + 1, lanes] += jnp.sum(normed * unit, axis=0, keepdims=True)
            lifted = normed * gain_ref[which : which + 1, lanes]
            out_ref[rows, lanes] = lifted
            term = jnp.sum(lifted * unit, axis=-1, keepdims=True)
            column = pl.ds(which, 1)
            if head == 0:
                terms_ref[rows, column] = term
            else:
                terms_ref[rows, column] += term

        def one(i, carry):
            rows = rows_at(i, block)
            qpos = qpos_ref[rows, :]
            mask = (kpos_ref[...] <= qpos) & (qpos <= kmax_ref[...])
            for head in range(heads):
                lanes = pl.ds(head * HEAD_DIM, HEAD_DIM)
                grad = ga_ref[rows, lanes]
                inverse = 1.0 / ws_ref[rows, pl.ds(head, 1)]
                drop = jnp.sum(grad * at_ref[rows, lanes], axis=-1, keepdims=True) * inverse
                grad_num = (grad * inverse).astype(bf16)
                query, keys = q_ref[rows, lanes], k_ref[:, lanes]
                scores = dot_nt(query, keys) * (scale * LOG2_E)
                expo = jnp.where(mask, jnp.exp2(scores), 0.0)
                grad_expo = dot_nt(grad_num, v_ref[:, lanes])
                grad_scores = (expo * (grad_expo - drop)).astype(bf16)
                turn_back(dot_nn(grad_scores, keys) * scale, rows, 0, cq_ref, head)
                dk_acc[:, lanes] += dot_tn(grad_scores, query)
                dv_acc[:, lanes] += dot_tn(expo.astype(bf16), grad_num)
            return carry

        lax.fori_loop(0, row // block, one, 0)

        def last(i, carry):
            rows = rows_at(i, block)
            for head in range(heads):
                lanes = pl.ds(head * HEAD_DIM, HEAD_DIM)
                turn_back(dk_acc[rows, lanes] * scale, rows, 1, ck_ref, head)
                dv_ref[rows, lanes] = dv_acc[rows, lanes].astype(bf16)
            return carry

        lax.fori_loop(0, row // block, last, 0)
        wait()

    return call(
        kernel,
        [
            shape((row, width), f32),
            shape((row, width), f32),
            shape((row, width), bf16),
            shape((row, 2), f32),
            shape((2, width), f32),
            shape((summed.shape[0] // ways, ways * summed.shape[1]), bf16),
        ],
        [pltpu.VMEM((row, width), f32)] * 2 + [pltpu.SemaphoreType.DMA((ways,))] * 2,
        list(parts) + [summed],
        ident,
        25,
        (len(parts),),
        (5,),
    )


def attn_grads(x_row, grad_qkv, grad_branch, attn_low, gain_columns, summed, ways, ident):
    row, width = x_row.shape
    first, second = grad_qkv.shape[1], attn_low.shape[1]
    cols = first + second + gain_columns.shape[1]

    def kernel(
        x_far, dq_ref, gb_far, low_ref, gain_ref, sum_ref, out_far, home_ref,
        x_ref, gb_ref, out_ref, in_sem, out_sem, send, recv
    ):
        me = lax.axis_index("seq")
        fetch = [
            pltpu.make_async_copy(x_far, x_ref, in_sem.at[0]),
            pltpu.make_async_copy(gb_far, gb_ref, in_sem.at[1]),
        ]
        for copy in fetch:
            copy.start()
        greet_line(me, ways)
        start, wait = home_copies(me, ways, sum_ref, [home_ref], [summed.shape[1]], send, recv)
        start()
        for copy in fetch:
            copy.wait()
        tile = 256

        def keep(i):
            rows = rows_at(i, tile)
            return pltpu.make_async_copy(out_ref.at[rows], out_far.at[rows], out_sem.at[i])

        def one(i, carry):
            rows = rows_at(i, tile)
            out_ref[rows, pl.ds(0, first)] = dot_tn(x_ref[:, rows], dq_ref[...]).astype(bf16)
            out_ref[rows, pl.ds(first, second)] = dot_tn(gb_ref[:, rows], low_ref[...]).astype(bf16)
            out_ref[rows, pl.ds(first + second, gain_columns.shape[1])] = gain_ref[rows, :]
            keep(i).start()
            return carry

        lax.fori_loop(0, width // tile, one, 0)

        def kept(i, carry):
            keep(i).wait()
            return carry

        lax.fori_loop(0, width // tile, kept, 0)
        wait()

    return call(
        kernel,
        [
            shape((width, cols), bf16),
            shape((summed.shape[0] // ways, ways * summed.shape[1]), bf16),
        ],
        [
            pltpu.VMEM((row, width), bf16),
            pltpu.VMEM((row, width), bf16),
            pltpu.VMEM((width, cols), bf16),
            pltpu.SemaphoreType.DMA((2,)),
            pltpu.SemaphoreType.DMA((width // 256,)),
            pltpu.SemaphoreType.DMA((ways,)),
            pltpu.SemaphoreType.DMA((ways,)),
        ],
        [x_row, grad_qkv, grad_branch, attn_low, gain_columns, summed],
        ident,
        25,
        (0, 2, 5),
        (0, 1),
    )


def exchange(sources, ways, ident, cost):
    rows = sources[0].shape[0]
    widths = [a.shape[1] // ways for a in sources]
    begins = [sum(widths[:i]) for i in range(len(widths))]
    count = len(sources)

    def kernel(*refs):
        ins, out_ref, send, recv, local = refs[:count], *refs[count:]
        me = lax.axis_index("seq")
        barrier = pltpu.get_barrier_semaphore()

        def greet(off, carry):
            pl.semaphore_signal(
                barrier, inc=1, device_id={"seq": (me + off) % ways}, device_id_type=MESH
            )
            return carry

        def move(off, i):
            dest = (me + off) % ways
            return remote(
                ins[i].at[:, rows_at(dest, widths[i])],
                out_ref.at[rows_at(me, rows), pl.ds(begins[i], widths[i])],
                send.at[off * count + i],
                recv.at[off * count + i],
                dest,
            )

        def keep(i):
            return pltpu.make_async_copy(
                ins[i].at[:, rows_at(me, widths[i])],
                out_ref.at[rows_at(me, rows), pl.ds(begins[i], widths[i])],
                local.at[i],
            )

        def each(what):
            def one(off, carry):
                for i in range(count):
                    what(move(off, i))
                return carry

            lax.fori_loop(1, ways, one, 0)

        for i in range(count):
            keep(i).start()
        lax.fori_loop(1, ways, greet, 0)
        pl.semaphore_wait(barrier, ways - 1)
        each(lambda copy: copy.start())
        for i in range(count):
            keep(i).wait()
        each(lambda copy: copy.wait())

    return pl.pallas_call(
        kernel,
        out_shape=shape((ways * rows, sum(widths)), bf16),
        in_specs=[pl.BlockSpec(memory_space=pl.ANY)] * count,
        out_specs=pl.BlockSpec(memory_space=pl.ANY),
        scratch_shapes=[
            pltpu.SemaphoreType.DMA((ways * count,)),
            pltpu.SemaphoreType.DMA((ways * count,)),
            pltpu.SemaphoreType.DMA((count,)),
        ],
        cost_estimate=pl.CostEstimate(
            flops=cost * 10**9, transcendentals=0, bytes_accessed=cost * 3 * 10**6
        ),
        compiler_params=pltpu.CompilerParams(collective_id=ident, has_side_effects=True),
    )(*sources)


def finish_grads(grads, kept, gains, ways):
    rows, count = gains.shape[0], len(grads)
    parts = list(grads) + list(kept) + [gains]

    def kernel(*refs):
        ins, outs = refs[: len(parts)], refs[len(parts) :]
        for i in range(len(parts) - 1):
            outs[i][...] = ins[i][...].astype(outs[i].dtype)
        total = ins[-1][:, pl.ds(0, HEAD_DIM)].astype(f32)
        for off in range(1, ways):
            total = total + ins[-1][:, pl.ds(off * HEAD_DIM, HEAD_DIM)].astype(f32)
        outs[-1][...] = total.T[:8, :]

    return pl.pallas_call(
        kernel,
        out_shape=[shape(part.shape, f32 if i < count else part.dtype) for i, part in enumerate(parts[:-1])]
        + [shape((8, rows), f32)],
        in_specs=[pl.BlockSpec(memory_space=pltpu.VMEM)] * len(parts),
        out_specs=[pl.BlockSpec(memory_space=pltpu.VMEM)] * len(parts),
        cost_estimate=pl.CostEstimate(flops=10**6, transcendentals=0, bytes_accessed=10**7),
        compiler_params=pltpu.CompilerParams(vmem_limit_bytes=60 * 2**20),
    )(*parts)


def line_sum(terms, ways, ident):
    def kernel(terms_ref, out_ref, slots, send, recv):
        me = lax.axis_index("seq")
        barrier = pltpu.get_barrier_semaphore()
        for off in range(1, ways):
            pl.semaphore_signal(
                barrier, inc=1, device_id={"seq": (me + off) % ways}, device_id_type=MESH
            )
        pl.semaphore_wait(barrier, ways - 1)
        for off in range(1, ways):
            remote(
                terms_ref, slots.at[off], send.at[off], recv.at[off], (me + off) % ways
            ).start()
        total = terms_ref[...]
        for off in range(1, ways):
            remote(terms_ref, slots.at[off], send.at[off], recv.at[off], (me + off) % ways).wait_recv()
            total = total + slots[off]
        out_ref[...] = total
        for off in range(1, ways):
            remote(terms_ref, slots.at[off], send.at[off], recv.at[off], (me + off) % ways).wait_send()

    return call(
        kernel,
        [shape(terms.shape, f32)],
        [
            pltpu.VMEM((ways,) + terms.shape, f32),
            pltpu.SemaphoreType.DMA((ways,)),
            pltpu.SemaphoreType.DMA((ways,)),
        ],
        [terms],
        ident,
        8,
    )[0]


def body(
    tokens,
    w_query,
    w_key,
    w_value,
    w_out,
    w_gate,
    w_up,
    w_down,
    gain_query,
    gain_key,
    gain_attn,
    gain_mlp,
    cotangent,
    key_mask,
    lengths,
    tract_order,
):
    ways, groups = lax.axis_size("seq"), lax.axis_size("dp")
    me = lax.axis_index("seq")
    token_rows = tokens[0]
    tok_count, feat_width = token_rows.shape
    ff_width = w_gate.shape[1]
    own_feat = feat_width // ways
    own_heads = own_feat // HEAD_DIM
    own_ff = ff_width // ways
    row_len = tok_count * ways
    score_scale = HEAD_DIM ** (-0.5)
    half_len = tok_count // 2
    order_pair = tract_order[0]
    slot_index = jnp.arange(tok_count, dtype=jnp.int32)
    local_pos = (
        jnp.where(slot_index < half_len, order_pair[0], order_pair[1]) * half_len
        + slot_index % half_len
    )
    key_ok = ((key_mask[0] == 1) & (local_pos < lengths[0])).astype(jnp.int32)

    gain_local = jnp.stack([gain_query, gain_key, gain_attn, gain_mlp], axis=1)
    gain_pad = jnp.pad(gain_local, ((0, 0), (0, HEAD_DIM - 4)))
    gain_all = jnp.tile(gain_pad, (1, ways))
    p_qkv = exchange([w_query, w_key, w_value, gain_all], ways, 8, 20)
    m_qkv = across(p_qkv)
    p_qkv, w_gate, w_up, w_out_t = lax.optimization_barrier(
        (p_qkv, w_gate, w_up, jnp.transpose(w_out))
    )
    p_mid = exchange([w_gate, w_up, w_out_t], ways, 10, 50)
    m_mid = across(p_mid)
    gains = dot_nt(jnp.eye(8, HEAD_DIM, dtype=bf16), m_qkv[:, 3 * own_feat :])
    gain_q = lax.dynamic_slice_in_dim(gains[0], me * own_feat, own_feat, 0)
    gain_k = lax.dynamic_slice_in_dim(gains[1], me * own_feat, own_feat, 0)

    code_pad = -tok_count % HEAD_DIM
    local_code = jnp.pad(local_pos * 2 + key_ok, (0, code_pad))[None]
    down_blocks = jnp.transpose(w_down).reshape(w_down.shape[1], ways, own_ff)
    down_blocks = jnp.transpose(down_blocks, (1, 0, 2))
    local_code, p_mid, down_blocks = lax.optimization_barrier((local_code, p_mid, down_blocks))
    x_row, codes, qkv = gather_project(token_rows, local_code, m_qkv, ways, 1)
    key_code = codes[:, 0, :tok_count].reshape(ways, 2, half_len)
    key_code = jnp.transpose(key_code, (1, 0, 2)).reshape(row_len)
    pos = key_code // 2
    q_raw, k_raw, v_raw = (qkv[:, i * own_feat : (i + 1) * own_feat] for i in range(3))
    squares = line_sum(
        jnp.stack([jnp.sum(q_raw * q_raw, axis=-1), jnp.sum(k_raw * k_raw, axis=-1)]), ways, 2
    )
    squares, down_blocks = lax.optimization_barrier((squares, down_blocks))
    p_down = lax.all_to_all(down_blocks, "seq", split_axis=0, concat_axis=0, tiled=True)
    p_down = p_down.reshape(-1, own_ff)
    factors = jnp.transpose(lax.rsqrt(squares / feat_width + norm_eps))
    cosine, sine = rope_tables(pos, HEAD_DIM)
    key_most = jnp.where(key_code % 2 == 1, jnp.int32(2**30), pos)
    places = [pos[:, None], pos[None], key_most[None]]
    gain_qk = jnp.stack([gain_q, gain_k])
    query_low, key_low, value_low, attn, attn_low, weight_sum = attend(
        [qkv, factors, cosine, sine, gain_qk] + places, min(row_len, 160)
    )

    branch, layer_out, grad_gain_mlp, hidden_low, mixed_low, grad_mlp, grad_gu, first_half, turned = (
        attn_out_and_ff(
            attn_low, m_mid, p_down, token_rows, cotangent[0], gains, groups, ways, 3
        )
    )
    d_gate = dot_tn(hidden_low, grad_gu[:, :own_ff]).astype(bf16)
    grad_gu, d_gate = lax.optimization_barrier((grad_gu, d_gate))
    d_up = dot_tn(hidden_low, grad_gu[:, own_ff:]).astype(bf16)
    grad_gu, d_up = lax.optimization_barrier((grad_gu, d_up))
    d_gate, d_up = dp_sum(d_gate), dp_sum(d_up)
    grad_hidden, grad_gain_attn, grad_branch, grad_attn, d_down = ff_to_attn_back(
        grad_gu, first_half, turned, m_mid, branch, cotangent[0], gains[2:3], grad_mlp, mixed_low, ways, 5
    )
    d_down = dp_sum(d_down)
    c_q, c_k, grad_v, terms, gain_part, dw_gate = attend_back(
        [query_low, key_low, value_low, grad_attn, attn, weight_sum]
        + [cosine, sine, qkv, factors, gain_qk]
        + places,
        d_gate,
        min(row_len, 160),
        ways,
        13,
    )
    terms = jnp.transpose(terms)
    means = line_sum(terms, ways, 6) / feat_width
    q_factor, k_factor = factors[:, :1], factors[:, 1:]
    grad_q_raw = q_factor * (c_q - q_raw * q_factor * means[0][:, None])
    grad_k_raw = k_factor * (c_k - k_raw * k_factor * means[1][:, None])
    grad_qkv = jnp.concatenate(
        [grad_q_raw.astype(bf16), grad_k_raw.astype(bf16), grad_v], axis=1
    )

    own_slot = jnp.zeros((2, feat_width), f32)
    own_slot = lax.dynamic_update_slice(own_slot, gain_part, (0, me * own_feat))
    gain_terms = jnp.concatenate(
        [
            own_slot,
            jnp.sum(grad_gain_attn, axis=0, keepdims=True),
            jnp.sum(grad_gain_mlp, axis=0, keepdims=True),
        ]
    )
    gain_columns = jnp.pad(jnp.transpose(gain_terms), ((0, 0), (0, HEAD_DIM - 4)))
    d_attn, dw_up = attn_grads(
        x_row, grad_qkv, grad_branch, attn_low, gain_columns.astype(bf16), d_up, ways, 14
    )
    dw_gu = [dw_gate.astype(f32), dw_up.astype(f32)]
    grad_qkv, d_attn, dw_gu = lax.optimization_barrier((grad_qkv, d_attn, dw_gu))
    grad_tokens, dw_down = project_back(grad_qkv, m_qkv, grad_hidden, d_down, ways, 7)
    grad_tokens, d_attn = lax.optimization_barrier((grad_tokens, dp_sum(d_attn)))
    dw_gu = [dw_gate.astype(f32), dw_up.astype(f32)]
    dw_qkv = bring_home(d_attn, [own_feat] * 4 + [HEAD_DIM], ways, 12)
    d_query, d_key, d_value, d_out, d_down, layer_out, grad_tokens, gain_grads = finish_grads(
        list(dw_qkv[:4]) + [dw_down], [layer_out, grad_tokens], dw_qkv[4], ways
    )
    return (
        layer_out[None],
        grad_tokens[None],
        d_query,
        d_key,
        d_value,
        jnp.transpose(d_out),
        dw_gu[0],
        dw_gu[1],
        jnp.transpose(d_down),
        gain_grads[0],
        gain_grads[1],
        gain_grads[2],
        gain_grads[3],
    )


def solution(mesh):
    both = ("dp", "seq")
    in_specs = (
        P("dp", "seq", None),
        P(both, None),
        P(both, None),
        P(both, None),
        P(None, both),
        P(both, None),
        P(both, None),
        P(None, both),
        P(both),
        P(both),
        P(both),
        P(both),
        P("dp", "seq", None),
        P("dp", "seq"),
        P("dp"),
        P("dp", "seq"),
    )
    out_specs = (
        P("dp", "seq", None),
        P("dp", "seq", None),
        P(both, None),
        P(both, None),
        P(both, None),
        P(None, both),
        P(both, None),
        P(both, None),
        P(None, both),
        P(both),
        P(both),
        P(both),
        P(both),
    )
    return jax.shard_map(body, mesh=mesh, in_specs=in_specs, out_specs=out_specs, check_vma=False)
```
